256 devices in a mesh: dp: 32 (over z, y), section: 2 (over core), tensor: 4 (over x).
Axes of the slice: x: 4, y: 4, z: 8, core: 2. Of those that a mesh axis runs over, the one named last changes fastest.
Arguments:
- tokens: bfloat16 [8192, 2048], P('dp'), may hold values from -6 to 6
- base_rows: int32 [128], replicated, may hold values from 1 to 6, as said below
- baseline_owner: int32 [128], replicated, may hold values from 0 to 31, as said below
- cotangent: bfloat16 [2, 16384, 2048], P('section', 'dp'), may hold values from -6 to 6
- pre_gain: float32 [2, 2048], P('section'), may hold values from 0.25 to 1.75
- input_proj: bfloat16 [2, 2048, 2048], P('section', None, 'tensor'), may hold values from -0.125 to 0.125
- gate_proj: bfloat16 [2, 2048, 2048], P('section', None, 'tensor'), may hold values from -0.125 to 0.125
- state_proj: bfloat16 [2, 2048, 256], P('section'), may hold values from -0.125 to 0.125
- step_proj: bfloat16 [2, 2048, 32], P('section', None, 'tensor'), may hold values from -0.125 to 0.125
- step_bias: float32 [2, 32], P('section', 'tensor'), may hold values from -6 to -1.5
- decay_log: float32 [2, 32], P('section', 'tensor'), may hold values from 0 to 2.5
- skip_gain: float32 [2, 32], P('section', 'tensor'), may hold values from 0.5 to 1.5
- norm_gain: float32 [2, 2048], P('section', 'tensor'), may hold values from 0.25 to 1.75
- out_proj: bfloat16 [2, 2048, 2048], P('section', 'tensor'), may hold values from -0.125 to 0.125
Outputs:
- activations: bfloat16 [2, 16384, 2048], P('section', 'dp')
- out_grad: bfloat16 [2, 2048, 2048], P('section', 'tensor', 'dp')
The draws below stay inside these ranges and needn't reach their ends.
Inputs may be any that keep to these rules, and one draw needn't show every extreme that they name: `base_rows`: over all baselines they sum to 256; some baseline has exactly 6. `baseline_owner`: every owner holds exactly 4 baselines; the base_rows of one owner's baselines sum to at most 16, and for some owner to exactly 16.
All inputs are finite; a program needn't handle non-finite values.
Results may differ from the reference program's by a relative error of at most 0.025.
Values may be sent and summed in bfloat16 or wider, within the bound.
A program may use at most 128 MiB of HBM per device.

```python
import jax
import jax.numpy as jnp
from jax import lax

D = 2048
HEADS = 32
HEADDIM = 64
NSTATE = 128
BLOCK = 64
TOK_DEV = 256
TOKENS = 8192
SPAN = 2
PACK = 4
ROWS_OWN = 512
STREAM = 16384
INNER = 2048
OWNERS = 32
N_DP = 32


def pack_layout(key):
    groups = OWNERS // 4
    unit = PACK * SPAN
    half = unit // 2
    longest = 3 * SPAN
    key_load, key_order, key_move, key_perm = jax.random.split(key, 4)
    extra = jax.random.randint(key_load, (groups, 2), 0, unit // 4 + 1, dtype=jnp.int32)
    sorted_loads = jnp.stack([jnp.full((groups,), 2 * unit, jnp.int32), half + extra[:, 0], half + extra[:, 1], unit - extra[:, 0] - extra[:, 1]], axis=1)
    order = jax.vmap(lambda sub: jax.random.permutation(sub, 4))(jax.random.split(key_order, groups))
    loads = jnp.take_along_axis(sorted_loads, order, axis=1).reshape(OWNERS)
    busiest = (order == 0).reshape(OWNERS)
    even_part = loads // PACK
    remainder = loads % PACK
    parts = even_part[:, None] + (jnp.arange(PACK, dtype=jnp.int32)[None, :] < remainder[:, None]).astype(jnp.int32)
    first = parts[:, 0::2]
    second = parts[:, 1::2]
    upper = jnp.minimum(second - 1, longest - first)
    lower = -jnp.minimum(first - 1, longest - second)
    moved_rows = jax.random.randint(key_move, first.shape, lower, upper + 1, dtype=jnp.int32)
    forced = busiest[:, None] & (jnp.arange(PACK // 2, dtype=jnp.int32)[None, :] == 0)
    moved_rows = jnp.where(forced, upper, moved_rows)
    first = first + moved_rows
    second = second - moved_rows
    parts = jnp.stack([first, second], axis=2).reshape(OWNERS * PACK).astype(jnp.int32)
    shuffle = jax.random.permutation(key_perm, OWNERS * PACK)
    rows_each = jnp.zeros((OWNERS * PACK,), jnp.int32).at[shuffle].set(parts)
    owner_each = jnp.zeros((OWNERS * PACK,), jnp.int32).at[shuffle].set((jnp.arange(OWNERS * PACK, dtype=jnp.int32) // PACK).astype(jnp.int32))
    return (rows_each, owner_each)


def draw_base_rows(key, part):
    return pack_layout(jax.random.fold_in(key, 11))[0]


def draw_baseline_owner(key, part):
    return pack_layout(jax.random.fold_in(key, 11))[1]


def strengthened(values, rng, source, target, shards_of, factor):
    owner, partner = [(jnp.arange(values.shape[axis_at]) // (values.shape[axis_at] // shards_of)).reshape([-1 if axis == axis_at else 1 for axis in range(values.ndim)]) for axis_at in (source, target)]
    chosen = jax.random.permutation(rng, shards_of)[partner]
    strong = (owner == chosen) | (owner == (partner + shards_of // 2) % shards_of)
    return jnp.where(strong, factor * values, values)


def shard_levels(key, dims, shards, low, largest):
    def one(axis_at, blocks):
        heights = jax.random.uniform(jax.random.fold_in(jax.random.fold_in(key, 6), axis_at), (blocks,), jnp.float32, low / len(shards), largest / len(shards))
        return jnp.repeat(jnp.exp(heights), dims[axis_at] // blocks).reshape((-1,) + (1,) * (len(dims) - axis_at - 1))

    gain = one(*shards[0])
    for cut in shards[1:]:
        gain = gain * one(*cut)
    return gain


def centred(rng, dims, scale, most, cuts=(), held_as=jnp.bfloat16):
    level = shard_levels(rng, dims, cuts, -0.22, 0.18) if cuts else 1.0
    drawn = jax.random.normal(rng, dims, jnp.float32) * scale * level
    return jnp.minimum(jnp.maximum(drawn, -most), most).astype(held_as)


def heavy_noise(stream_key, dims, deviation, most, cuts, heavy, kind=jnp.bfloat16):
    drawn = deviation * jax.random.normal(stream_key, dims, jnp.float32)
    if cuts:
        drawn = drawn * shard_levels(stream_key, dims, cuts, -0.22, 0.18)
    return jnp.clip(strengthened(drawn, jax.random.fold_in(stream_key, 3), *heavy), -most, most).astype(kind)


def setup_inputs(seed: int = 0) -> dict:
    key_of = jax.random.split(jax.random.key(seed), 15)
    return {
        "tokens": centred(key_of[0], (TOKENS, D), 1.0, 6.0, ((0, 32),)),
        "base_rows": draw_base_rows(jax.random.fold_in(key_of[14], 71), 0),
        "baseline_owner": draw_baseline_owner(jax.random.fold_in(key_of[14], 71), 0),
        "cotangent": heavy_noise(key_of[3], (2, STREAM, D), 1.0, 6.0, ((0, 2), (1, 32)), (1, 2, 32, 2.75)),
        "pre_gain": jnp.clip(1.0 + 0.15 * jax.random.normal(key_of[4], (2, D), jnp.float32), 0.25, 1.75),
        "input_proj": centred(key_of[5], (2, D, INNER), D ** -0.5, 0.125, ((0, 2), (2, 4))),
        "gate_proj": centred(key_of[6], (2, D, INNER), D ** -0.5, 0.125, ((0, 2), (2, 4))),
        "state_proj": centred(key_of[7], (2, D, 2 * NSTATE), D ** -0.5, 0.125, ((0, 2),)),
        "step_proj": centred(key_of[8], (2, D, HEADS), D ** -0.5, 0.125, ((0, 2), (2, 4))),
        "step_bias": jnp.clip(-6.0 + 4.5 * jax.random.uniform(key_of[9], (2, HEADS), jnp.float32) ** shard_levels(key_of[9], (2, HEADS), ((0, 2), (1, 4)), -0.2, 0.2), -6.0, -1.5),
        "decay_log": jnp.clip(2.5 * jax.random.uniform(key_of[10], (2, HEADS), jnp.float32) ** shard_levels(key_of[10], (2, HEADS), ((0, 2), (1, 4)), -0.2, 0.2), 0.0, 2.5),
        "skip_gain": jnp.clip(0.5 + 1.0 * jax.random.uniform(key_of[11], (2, HEADS), jnp.float32) ** shard_levels(key_of[11], (2, HEADS), ((0, 2), (1, 4)), -0.2, 0.2), 0.5, 1.5),
        "norm_gain": jnp.clip(1.0 + 0.15 * jax.random.normal(key_of[12], (2, INNER), jnp.float32), 0.25, 1.75),
        "out_proj": centred(key_of[13], (2, INNER, D), INNER ** -0.5, 0.125, ((0, 2), (1, 4))),
    }


EPS = 1e-05
HIGH = lax.Precision.HIGHEST

def layout_tables(base_rows, baseline_owner):
    count = base_rows.shape[0]
    index = jnp.arange(count, dtype=jnp.int32)
    ends = jnp.cumsum(base_rows).astype(jnp.int32)
    starts = (ends - base_rows).astype(jnp.int32)
    earlier = (baseline_owner[:, None] == baseline_owner[None, :]) & (index[None, :] < index[:, None])
    owner_start = lax.optimization_barrier(jnp.sum(jnp.where(earlier, base_rows[None, :], 0), axis=1)).astype(jnp.int32)
    return (index, starts, ends, owner_start)

def block_scan(heads_in, b_rows, c_rows, step_size, decay_rate, segment, state, prev_segment, block):
    total_rows, head_count, head_dim = heads_in.shape
    blocks = total_rows // block

    def advance(carried_in, item):
        state_now, segment_before = carried_in
        x_blk, b_blk, c_blk, dt_blk, seg_blk = item
        running = jnp.cumsum(dt_blk * decay_rate[None, :], axis=0)
        positions = jnp.arange(block, dtype=jnp.int32)
        together = (seg_blk[:, None] == seg_blk[None, :]) & (positions[:, None] >= positions[None, :])
        spread = jnp.minimum(running[:, None, :] - running[None, :, :], 0.0)
        decay_mask = jnp.where(together[:, :, None], jnp.exp(spread), 0.0)
        scores = jnp.dot(c_blk, b_blk.T, preferred_element_type=jnp.float32)
        weights = (decay_mask * scores[:, :, None] * dt_blk[None, :, :]).astype(jnp.bfloat16)
        within = jnp.einsum('ijh,jhp->ihp', weights.astype(jnp.float32), x_blk.astype(jnp.float32), precision=HIGH)
        keep_in = (seg_blk == segment_before).astype(jnp.float32)
        state_low = lax.optimization_barrier(state_now.astype(jnp.bfloat16)).astype(jnp.float32)
        readout = jnp.einsum('in,hpn->ihp', c_blk.astype(jnp.float32), state_low, precision=HIGH)
        from_state = keep_in[:, None, None] * jnp.exp(running)[:, :, None] * readout
        last_segment = seg_blk[-1]
        tail_weight = jnp.where((seg_blk == last_segment)[:, None], jnp.exp(running[-1][None, :] - running), 0.0) * dt_blk
        scaled = (tail_weight[:, :, None] * x_blk.astype(jnp.float32)).astype(jnp.bfloat16)
        scaled = lax.optimization_barrier(scaled).astype(jnp.float32)
        fresh_term = jnp.einsum('jhp,jn->hpn', scaled, b_blk.astype(jnp.float32), precision=HIGH)
        keep_state = (last_segment == segment_before).astype(jnp.float32)
        state_next = keep_state * jnp.exp(running[-1])[:, None, None] * state_now + fresh_term
        return ((state_next, last_segment), within + from_state)
    scanned = (heads_in.reshape(blocks, block, head_count, head_dim), b_rows.reshape(blocks, block, -1), c_rows.reshape(blocks, block, -1), step_size.reshape(blocks, block, head_count), segment.reshape(blocks, block))
    (state, prev_segment), outputs = lax.scan(advance, (state, prev_segment), scanned)
    return (outputs.reshape(total_rows, head_count, head_dim), state, prev_segment)

def block_layer(rows_in, segment, params):
    pre_gain, input_proj, gate_proj, state_proj, step_proj, step_bias, decay_log, skip_gain, norm_gain, out_proj = params
    row_count = rows_in.shape[0]
    rows_f = rows_in.astype(jnp.float32)
    normed = (rows_f * lax.rsqrt(lax.optimization_barrier(jnp.mean(rows_f * rows_f, axis=-1, keepdims=True)) + EPS) * pre_gain).astype(jnp.bfloat16)
    scan_in = jax.nn.silu(jnp.dot(normed, input_proj, preferred_element_type=jnp.float32)).astype(jnp.bfloat16)
    gate_pre = jnp.dot(normed, gate_proj, preferred_element_type=jnp.float32)
    state_io = jax.nn.silu(jnp.dot(normed, state_proj, preferred_element_type=jnp.float32)).astype(jnp.bfloat16)
    step_size = jax.nn.softplus(jnp.dot(normed, step_proj, preferred_element_type=jnp.float32) + step_bias)
    decay_rate = -jnp.exp(decay_log)
    heads_in = scan_in.reshape(row_count, HEADS, HEADDIM)
    state_start = jnp.zeros((HEADS, HEADDIM, NSTATE), jnp.float32)
    scan_out, state_end, segment_end = block_scan(heads_in, state_io[:, :NSTATE], state_io[:, NSTATE:], step_size, decay_rate, segment, state_start, jnp.array(-1, jnp.int32), BLOCK)
    scan_out = scan_out + skip_gain[None, :, None] * heads_in.astype(jnp.float32)
    gated = scan_out.reshape(row_count, HEADS * HEADDIM) * jax.nn.silu(gate_pre)
    sq_sum = lax.optimization_barrier(jnp.sum(gated * gated, axis=-1, keepdims=True))
    y_norm = (gated * lax.rsqrt(sq_sum / (HEADS * HEADDIM) + EPS) * norm_gain).astype(jnp.bfloat16)
    result = (rows_f + jnp.dot(y_norm, out_proj, preferred_element_type=jnp.float32)).astype(jnp.bfloat16)
    return (result, y_norm)

def reference(tokens, base_rows, baseline_owner, cotangent, pre_gain, input_proj, gate_proj, state_proj, step_proj, step_bias, decay_log, skip_gain, norm_gain, out_proj):
    index, starts, ends, owner_start = layout_tables(base_rows, baseline_owner)
    local = jnp.arange(TOK_DEV, dtype=jnp.int32)
    inside = ((starts[None, :] <= local[:, None]) & (local[:, None] < ends[None, :])).astype(jnp.int32)
    row_id = lax.optimization_barrier(jnp.sum(inside * index[None, :], axis=1)).astype(jnp.int32)
    row_start = lax.optimization_barrier(jnp.sum(inside * starts[None, :], axis=1)).astype(jnp.int32)
    row_len = lax.optimization_barrier(jnp.sum(inside * base_rows[None, :], axis=1)).astype(jnp.int32)
    row_owner = lax.optimization_barrier(jnp.sum(inside * baseline_owner[None, :], axis=1)).astype(jnp.int32)
    row_ostart = lax.optimization_barrier(jnp.sum(inside * owner_start[None, :], axis=1)).astype(jnp.int32)
    reader = jnp.arange(N_DP, dtype=jnp.int32)[:, None]
    target = row_owner[None, :] * ROWS_OWN + OWNERS * row_ostart[None, :] + reader * row_len[None, :] + (local - row_start)[None, :]
    target = target.reshape(TOKENS).astype(jnp.int32)
    stream = jnp.zeros((STREAM, D), jnp.bfloat16).at[target].set(tokens).reshape(N_DP, ROWS_OWN, D)
    ids_all = jnp.tile(row_id, N_DP).astype(jnp.int32)
    slot_ids = jnp.full((STREAM,), -1, jnp.int32).at[target].set(ids_all).reshape(N_DP, ROWS_OWN)
    starts_flag = jnp.concatenate([jnp.ones((N_DP, 1), jnp.int32), (slot_ids[:, 1:] != slot_ids[:, :-1]).astype(jnp.int32)], axis=1)
    segment = jnp.cumsum(starts_flag, axis=1).astype(jnp.int32)
    everything = (pre_gain, input_proj, gate_proj, state_proj, step_proj, step_bias, decay_log, skip_gain, norm_gain, out_proj)
    enc_params = tuple((item[0] for item in everything))
    dec_params = tuple((item[1] for item in everything))
    cot_all = cotangent.reshape(2, N_DP, ROWS_OWN, D)

    def per_owner(totals, item):
        rows_in, seg_own, cot_enc, cot_dec = item
        latent, y_enc = block_layer(rows_in, seg_own, enc_params)
        rebuilt, y_dec = block_layer(latent, seg_own, dec_params)
        grad_enc = jnp.dot(y_enc.T, cot_enc, preferred_element_type=jnp.float32)
        grad_dec = jnp.dot(y_dec.T, cot_dec, preferred_element_type=jnp.float32)
        return ((totals[0] + grad_enc, totals[1] + grad_dec), (latent, rebuilt))
    zero_grad = jnp.zeros((HEADS * HEADDIM, D), jnp.float32)
    (grad_enc, grad_dec), (latents, rebuilts) = lax.scan(per_owner, (zero_grad, zero_grad), (stream, segment, cot_all[0], cot_all[1]))
    activations = jnp.stack([latents.reshape(STREAM, D), rebuilts.reshape(STREAM, D)])
    out_grad = jnp.stack([grad_enc, grad_dec]).astype(jnp.bfloat16)
    return (activations, out_grad)
```

```python
import functools

import jax
import jax.numpy as jnp
from jax import lax
from jax.experimental import pallas as pl
from jax.experimental.pallas import tpu as pltpu
from jax.sharding import PartitionSpec as P

MESH = pl.DeviceIdType.MESH
HEADDIM = 64
NSTATE = 128
ROWS = 128
RING = 4
EPS = 1e-05
F32 = jnp.float32
BF16 = jnp.bfloat16


def layout_tables(base_rows, baseline_owner):
    count = base_rows.shape[0]
    index = jnp.arange(count, dtype=jnp.int32)
    ends = jnp.cumsum(base_rows)
    starts = ends - base_rows
    earlier = (baseline_owner[:, None] == baseline_owner[None, :]) & (
        index[None, :] < index[:, None]
    )
    owner_start = jnp.sum(jnp.where(earlier, base_rows[None, :], 0), axis=1)
    return (index, starts, ends, owner_start)


def iota(shape, axis):
    return lax.broadcasted_iota(jnp.int32, shape, axis)


def silu(value):
    return value / (1.0 + jnp.exp(-value))


def softplus(value):
    return jnp.maximum(value, 0.0) + jnp.log1p(jnp.exp(-jnp.abs(value)))


def owner_starts(rows_c, rows_r, own_c, own_r):
    count = rows_r.shape[1]
    down, across = iota((count, count), 0), iota((count, count), 1)
    same = own_c == own_r
    row = jnp.sum(jnp.where(same & (down < across), rows_c, 0), axis=0, keepdims=True)
    col = jnp.sum(jnp.where(same & (across < down), rows_r, 0), axis=1, keepdims=True)
    return row, col


def block_kernel(
    chunks,
    heads,
    rows_c,
    rows_r,
    own_c,
    own_r,
    stream,
    pre_gain,
    w_in,
    w_gate,
    w_state,
    w_step,
    step_bias,
    decay_log,
    skip_gain,
    norm_gain,
    w_out,
    out_ref,
    y_ref,
    rs_ref,
    u_buf,
    o_buf,
    p_buf,
    a1,
    b1,
    a2,
    b2,
    normed,
    xs_buf,
    gate_buf,
    bc_buf,
    dt_buf,
    state,
    prev,
    seg_col,
    seg_row,
    sq_buf,
    skip_row,
    hand_sem,
    hand_send,
    out_sem,
    rs_send,
    rs_recv,
    ag_send,
    ag_recv,
    sq_send,
    sq_recv,
):
    me = lax.axis_index("tensor")
    sec = lax.axis_index("section")
    owner = lax.axis_index("dp")
    right, left, opposite = ((me + 1) % RING, (me + 3) % RING, (me + 2) % RING)
    width = o_buf.shape[1]
    readers = lax.axis_size("dp")
    inner = w_in.shape[1]
    pairs = heads // 2
    piece = ROWS // RING
    half = piece // 2
    count = rows_r.shape[1]

    barrier = pltpu.get_barrier_semaphore()
    for other in (right, left, opposite):
        pl.semaphore_signal(barrier, inc=1, device_id={"tensor": other}, device_id_type=MESH)
    pl.semaphore_signal(barrier, inc=1, device_id={"section": 1 - sec}, device_id_type=MESH)

    def rows_of(t):
        return pl.ds(pl.multiple_of(t * ROWS, ROWS), ROWS)

    def piece_of(who, which=None):
        if which is None:
            return pl.ds(pl.multiple_of(who * piece, piece), piece)
        return pl.ds(pl.multiple_of(who * piece + which * half, half), half)

    def out_piece(t, who, which=None):
        if which is None:
            return pl.ds(pl.multiple_of(t * ROWS + who * piece, piece), piece)
        return pl.ds(pl.multiple_of(t * ROWS + who * piece + which * half, half), half)

    def push(src, dst, send_sem, recv_sem, who):
        return pltpu.make_async_remote_copy(
            src_ref=src,
            dst_ref=dst,
            send_sem=send_sem,
            recv_sem=recv_sem,
            device_id={"tensor": who},
            device_id_type=MESH,
        )

    def feed(t):
        return pltpu.make_async_copy(stream.at[rows_of(t)], u_buf.at[rows_of(t)], hand_sem.at[t])

    def hand_over(t):
        return pltpu.make_async_remote_copy(
            src_ref=o_buf.at[rows_of(t)],
            dst_ref=u_buf.at[rows_of(t)],
            send_sem=hand_send.at[t],
            recv_sem=hand_sem.at[t],
            device_id={"section": 1 - sec},
            device_id_type=MESH,
        )

    def store_out(t):
        return pltpu.make_async_copy(o_buf.at[rows_of(t)], out_ref.at[rows_of(t)], out_sem.at[t])

    @pl.when(sec == 0)
    def _():
        for t in range(chunks):
            feed(t).start()

    start_row, start_col = owner_starts(rows_c[...], rows_r[...], own_c[...], own_r[...])
    slots = chunks * ROWS
    ids_c = (iota((count, 1), 0) + 1).astype(F32)
    ids_r = (iota((1, count), 1) + 1).astype(F32)
    slot_r = iota((count, slots), 1)
    held_c = (
        (own_c[...] == owner)
        & (slot_r >= readers * start_col)
        & (slot_r < readers * (start_col + rows_c[...]))
    )
    ids_row = jnp.sum(jnp.where(held_c, ids_c, 0.0), axis=0, keepdims=True)
    for t in range(chunks):
        seg_row[t] = jnp.broadcast_to(ids_row[:, t * ROWS : (t + 1) * ROWS], (8, ROWS))
    slot_c = iota((slots, count), 0)
    held_r = (
        (own_r[...] == owner)
        & (slot_c >= readers * start_row)
        & (slot_c < readers * (start_row + rows_r[...]))
    )
    ids_col = jnp.sum(jnp.where(held_r, ids_r, 0.0), axis=1, keepdims=True)
    seg_col[...] = jnp.broadcast_to(ids_col, (slots, ROWS))
    state[...] = jnp.zeros_like(state)
    prev[...] = jnp.full(prev.shape, -1.0, F32)
    lane = iota((ROWS, 128), 1)
    low = lane < HEADDIM

    def spread(value, pair):
        shape = (value.shape[0], 128)
        first = jnp.broadcast_to(value[:, 2 * pair : 2 * pair + 1], shape)
        second = jnp.broadcast_to(value[:, 2 * pair + 1 : 2 * pair + 2], shape)
        return jnp.where(iota(shape, 1) < HEADDIM, first, second)

    for pair in range(pairs):
        skip_row[:, pair * 128 : (pair + 1) * 128] = spread(
            jnp.broadcast_to(skip_gain[...], (8, 128)), pair
        )
    rate = -jnp.exp(decay_log[...])
    pl.semaphore_wait(barrier, 4)

    def stage_in(t):
        pltpu.make_async_copy(u_buf.at[rows_of(t)], u_buf.at[rows_of(t)], hand_sem.at[t]).wait()
        rows_f = u_buf[rows_of(t), :].astype(F32)
        scale = lax.rsqrt(jnp.mean(rows_f * rows_f, axis=-1, keepdims=True) + EPS)
        normed[...] = (rows_f * scale * pre_gain[...]).astype(BF16)
        xs_buf[...] = silu(jnp.dot(normed[...], w_in[...], preferred_element_type=F32)).astype(BF16)
        bc_buf[...] = silu(jnp.dot(normed[...], w_state[...], preferred_element_type=F32)).astype(
            BF16
        )
        dt_buf[...] = softplus(
            jnp.dot(normed[...], w_step[...], preferred_element_type=F32) + step_bias[...]
        )
        gate_buf[...] = silu(jnp.dot(normed[...], w_gate[...], preferred_element_type=F32))

    def stage_scan(t):
        segment_c = seg_col[rows_of(t), :]
        segment_r = jnp.broadcast_to(seg_row[t][0:1, :], (ROWS, ROWS))
        before = jnp.broadcast_to(prev[0:1, :], (ROWS, ROWS))
        last = segment_c[ROWS - 1 : ROWS, :]
        down, across = iota((ROWS, ROWS), 0), iota((ROWS, ROWS), 1)
        causal = down >= across
        hidden = jnp.where(causal & (segment_c == segment_r), 0.0, -1e30)
        dt = dt_buf[...]
        cum = jnp.dot(
            causal.astype(F32),
            dt * rate,
            preferred_element_type=F32,
            precision=lax.Precision.HIGHEST,
        )
        cum_t, dt_t = cum.T, dt.T
        grown = jnp.exp(cum)
        from_before = jnp.where(segment_c == before, grown, 0.0)
        last_cum = cum[ROWS - 1 : ROWS, :]
        tail = jnp.where(segment_c == last, jnp.exp(last_cum - cum), 0.0) * dt
        kept = jnp.where(last == prev[0:1, :], jnp.exp(last_cum), 0.0)
        b_rows, c_rows = bc_buf[:, :NSTATE], bc_buf[:, NSTATE:]
        scores = lax.dot_general(
            c_rows, b_rows, (((1,), (1,)), ((), ())), preferred_element_type=F32
        )
        readout = jnp.dot(c_rows, state[...].astype(BF16), preferred_element_type=F32)
        squares = jnp.zeros((ROWS, 128), F32)
        for pair in range(pairs):
            cols = slice(pair * 128, (pair + 1) * 128)
            x_pair = xs_buf[:, cols]
            x_f = x_pair.astype(F32)
            parts = []
            for head in (2 * pair, 2 * pair + 1):
                falling = jnp.minimum(cum[:, head : head + 1] - cum_t[head : head + 1, :], 0.0)
                weights = jnp.exp(falling + hidden) * scores * dt_t[head : head + 1, :]
                parts.append(jnp.dot(weights.astype(BF16), x_pair, preferred_element_type=F32))
            total = (
                jnp.where(low, parts[0], parts[1])
                + spread(from_before, pair) * readout[:, cols]
                + skip_row[0:1, cols] * x_f
            )
            gated = total * gate_buf[:, cols]
            squares = squares + gated * gated
            y_ref[rows_of(t), cols] = (gated * norm_gain[:, cols]).astype(BF16)
            scaled = (spread(tail, pair) * x_f).astype(BF16)
            fresh = lax.dot_general(
                b_rows, scaled, (((0,), (0,)), ((), ())), preferred_element_type=F32
            )
            state[:, cols] = spread(kept, pair) * state[:, cols] + fresh
        prev[...] = jnp.broadcast_to(last, prev.shape)
        sq_buf[0, t] = jnp.broadcast_to(jnp.sum(squares.T, axis=0, keepdims=True), (8, ROWS))

    def send_squares(t):
        return [
            push(
                sq_buf.at[0, t],
                sq_buf.at[k, t],
                sq_send.at[k - 1, t],
                sq_recv.at[k - 1, t],
                (me + k) % RING,
            )
            for k in range(1, RING)
        ]

    def reduce_copies(t):
        mine = p_buf.at[t]
        return (
            push(mine.at[piece_of(opposite, 0)], a1.at[t], rs_send.at[0, t], rs_recv.at[0, t], right),
            push(mine.at[piece_of(opposite, 1)], b1.at[t], rs_send.at[1, t], rs_recv.at[1, t], left),
            push(mine.at[piece_of(right, 1)], a2.at[t, 1], rs_send.at[2, t], rs_recv.at[2, t], right),
            push(mine.at[piece_of(left, 0)], b2.at[t, 0], rs_send.at[3, t], rs_recv.at[3, t], left),
            push(mine.at[piece_of(right, 0)], a2.at[t, 0], rs_send.at[4, t], rs_recv.at[4, t], right),
            push(mine.at[piece_of(left, 1)], b2.at[t, 1], rs_send.at[5, t], rs_recv.at[5, t], left),
        )

    def gather_copies(t):
        own, from_left, from_right = (
            o_buf.at[out_piece(t, me)],
            o_buf.at[out_piece(t, left, 0)],
            o_buf.at[out_piece(t, right, 1)],
        )
        return (
            push(own, own, ag_send.at[0, t], ag_recv.at[0, t], right),
            push(own, own, ag_send.at[1, t], ag_recv.at[1, t], left),
            push(from_left, from_left, ag_send.at[2, t], ag_recv.at[2, t], right),
            push(from_right, from_right, ag_send.at[3, t], ag_recv.at[3, t], left),
        )

    def stage_out(t):
        p_buf[t] = jnp.dot(y_ref[rows_of(t), :], w_out[...], preferred_element_type=F32).astype(
            BF16
        )
        for copy in reduce_copies(t)[:4]:
            copy.start()

    def reduce_second(t):
        copies = reduce_copies(t)
        copies[0].wait_recv()
        where = piece_of(right, 0)
        p_buf[t, where, :] = (p_buf[t, where, :].astype(F32) + a1[t].astype(F32)).astype(BF16)
        copies[4].start()
        copies[1].wait_recv()
        where = piece_of(left, 1)
        p_buf[t, where, :] = (p_buf[t, where, :].astype(F32) + b1[t].astype(F32)).astype(BF16)
        copies[5].start()

    def reduce_last(t):
        for copy in send_squares(t):
            copy.wait_recv()
        total = sq_buf[0, t] + sq_buf[1, t] + sq_buf[2, t] + sq_buf[3, t]
        scale = lax.rsqrt(total / (RING * inner) + EPS)
        rs_ref[rows_of(t), :] = jnp.broadcast_to(scale[0:1, :], (ROWS, ROWS)).T
        copies = reduce_copies(t)
        for copy in copies[2:]:
            copy.wait_recv()
        for which in (0, 1):
            where = out_piece(t, me, which)
            summed = (
                p_buf[t, piece_of(me, which), :].astype(F32)
                + a2[t, which].astype(F32)
                + b2[t, which].astype(F32)
            )
            o_buf[where, :] = (
                u_buf[where, :].astype(F32) + rs_ref[where, 0:1] * summed
            ).astype(BF16)
        for copy in gather_copies(t)[:2]:
            copy.start()

    def gather_second(t):
        copies = gather_copies(t)
        copies[0].wait_recv()
        copies[2].start()
        copies[1].wait_recv()
        copies[3].start()

    def gather_last(t):
        copies = gather_copies(t)
        copies[2].wait_recv()
        copies[3].wait_recv()

        @pl.when(sec == 0)
        def _():
            hand_over(t).start()

        store_out(t).start()

    def step(t, carry):
        @pl.when(t < chunks)
        def _():
            stage_in(t)

        @pl.when(t >= 2)
        def _():
            gather_last(t - 2)

        @pl.when((t >= 1) & (t <= chunks))
        def _():
            reduce_second(t - 1)

        @pl.when(t < chunks)
        def _():
            stage_scan(t)
            for copy in send_squares(t):
                copy.start()

        @pl.when((t >= 1) & (t <= chunks))
        def _():
            reduce_last(t - 1)

        @pl.when(t < chunks)
        def _():
            stage_out(t)

        @pl.when((t >= 1) & (t <= chunks))
        def _():
            gather_second(t - 1)

        return carry

    lax.fori_loop(0, chunks + 2, step, 0)

    def drain(t, carry):
        for copy in reduce_copies(t) + gather_copies(t) + tuple(send_squares(t)):
            copy.wait_send()

        @pl.when(sec == 0)
        def _():
            hand_over(t).wait_send()

        store_out(t).wait()
        return carry

    lax.fori_loop(0, chunks, drain, 0)


def run_blocks(tables, stream, params):
    (
        pre_gain,
        input_proj,
        gate_proj,
        state_proj,
        step_proj,
        step_bias,
        decay_log,
        skip_gain,
        norm_gain,
        out_proj,
    ) = params
    slots, width = stream.shape
    inner = input_proj.shape[1]
    heads = step_proj.shape[1]
    chunks = slots // ROWS
    pad = ((0, 0), (0, 128 - heads))
    vmem = pl.BlockSpec(memory_space=pltpu.VMEM)
    anywhere = pl.BlockSpec(memory_space=pl.ANY)
    piece = ROWS // RING
    half = piece // 2
    dma = pltpu.SemaphoreType.DMA
    return pl.pallas_call(
        functools.partial(block_kernel, chunks, heads),
        name="blocks",
        out_shape=(
            jax.ShapeDtypeStruct((slots, width), BF16),
            jax.ShapeDtypeStruct((slots, inner), BF16),
            jax.ShapeDtypeStruct((slots, 128), F32),
        ),
        in_specs=[vmem] * 4 + [anywhere] + [vmem] * 10,
        out_specs=(anywhere, vmem, vmem),
        scratch_shapes=[
            pltpu.VMEM((slots, width), BF16),
            pltpu.VMEM((slots, width), BF16),
            pltpu.VMEM((chunks, ROWS, width), BF16),
            pltpu.VMEM((chunks, half, width), BF16),
            pltpu.VMEM((chunks, half, width), BF16),
            pltpu.VMEM((chunks, 2, half, width), BF16),
            pltpu.VMEM((chunks, 2, half, width), BF16),
            pltpu.VMEM((ROWS, width), BF16),
            pltpu.VMEM((ROWS, inner), BF16),
            pltpu.VMEM((ROWS, inner), F32),
            pltpu.VMEM((ROWS, 2 * NSTATE), BF16),
            pltpu.VMEM((ROWS, 128), F32),
            pltpu.VMEM((NSTATE, inner), F32),
            pltpu.VMEM((8, 128), F32),
            pltpu.VMEM((slots, 128), F32),
            pltpu.VMEM((chunks, 8, 128), F32),
            pltpu.VMEM((RING, chunks, 8, 128), F32),
            pltpu.VMEM((8, inner), F32),
            dma((chunks,)),
            dma((chunks,)),
            dma((chunks,)),
            dma((6, chunks)),
            dma((6, chunks)),
            dma((4, chunks)),
            dma((4, chunks)),
            dma((3, chunks)),
            dma((3, chunks)),
        ],
        compiler_params=pltpu.CompilerParams(
            collective_id=1, has_side_effects=True, vmem_limit_bytes=60 * 1024 * 1024
        ),
    )(
        *tables,
        stream,
        pre_gain[None],
        input_proj,
        gate_proj,
        state_proj,
        jnp.pad(step_proj, pad),
        jnp.pad(step_bias[None], pad),
        jnp.pad(decay_log[None], pad),
        jnp.pad(skip_gain[None], pad),
        norm_gain[None],
        out_proj,
    )


def grad_kernel(
    y_ref,
    rs_ref,
    cot,
    out_ref,
    yn,
    g_buf,
    a1,
    b1,
    a2,
    b2,
    h_buf,
    z_buf,
    rs_send,
    rs_recv,
    z_send,
    z_recv,
):
    levels, share = g_buf.shape[0], g_buf.shape[2]
    index = lax.axis_index("dp")
    my_z, my_y = index // RING, index % RING
    right_y, left_y, opposite_y = ((my_y + 1) % RING, (my_y + 3) % RING, (my_y + 2) % RING)
    right, left = my_z * RING + right_y, my_z * RING + left_y
    block = RING * share
    some = levels // 2

    def level(k):
        return ((my_z + k) % levels) * RING + my_y

    barrier = pltpu.get_barrier_semaphore()
    others = [right, left] + [level(k) for k in range(1, levels)]
    for other in others:
        pl.semaphore_signal(barrier, inc=1, device_id={"dp": other}, device_id_type=MESH)

    yn[...] = (y_ref[...].astype(F32) * rs_ref[:, 0:1]).astype(BF16)

    def push(src, dst, send_sem, recv_sem, who):
        return pltpu.make_async_remote_copy(
            src_ref=src,
            dst_ref=dst,
            send_sem=send_sem,
            recv_sem=recv_sem,
            device_id={"dp": who},
            device_id_type=MESH,
        )

    low, high = pl.ds(0, some), pl.ds(some, some)
    copies = (
        push(g_buf.at[low, opposite_y], a1, rs_send.at[0], rs_recv.at[0], right),
        push(g_buf.at[high, opposite_y], b1, rs_send.at[1], rs_recv.at[1], left),
        push(g_buf.at[high, right_y], a2.at[high], rs_send.at[2], rs_recv.at[2], right),
        push(g_buf.at[low, left_y], b2.at[low], rs_send.at[3], rs_recv.at[3], left),
        push(g_buf.at[low, right_y], a2.at[low], rs_send.at[4], rs_recv.at[4], right),
        push(g_buf.at[high, left_y], b2.at[high], rs_send.at[5], rs_recv.at[5], left),
    )

    def term(k, carry):
        cols = pl.ds(pl.multiple_of(k * block, block), block)
        product = lax.dot_general(
            cot[:, cols], yn[...], (((0,), (0,)), ((), ())), preferred_element_type=F32
        )
        g_buf[k] = product.astype(BF16).reshape(RING, share, product.shape[1])
        return carry

    lax.fori_loop(0, some, term, 0)
    pl.semaphore_wait(barrier, len(others))
    copies[0].start()
    copies[3].start()
    lax.fori_loop(some, levels, term, 0)
    copies[1].start()
    copies[2].start()

    copies[0].wait_recv()

    def add_low(k, carry):
        g_buf[k, right_y] = (g_buf[k, right_y].astype(F32) + a1[k].astype(F32)).astype(BF16)
        return carry

    lax.fori_loop(0, some, add_low, 0)
    copies[4].start()
    copies[1].wait_recv()

    def add_high(k, carry):
        g_buf[some + k, left_y] = (g_buf[some + k, left_y].astype(F32) + b1[k].astype(F32)).astype(
            BF16
        )
        return carry

    lax.fori_loop(0, some, add_high, 0)
    copies[5].start()
    for copy in copies[2:]:
        copy.wait_recv()

    def exchange(k):
        return push(
            h_buf.at[(my_z + k) % levels], z_buf.at[k], z_send.at[k], z_recv.at[k], level(k)
        )

    def finish(k, carry):
        who = (my_z + k) % levels
        h_buf[who] = (
            g_buf[who, my_y].astype(F32) + a2[who].astype(F32) + b2[who].astype(F32)
        ).astype(BF16)
        exchange(k).start()
        return carry

    lax.fori_loop(1, levels, finish, 0)
    total = g_buf[my_z, my_y].astype(F32) + a2[my_z].astype(F32) + b2[my_z].astype(F32)

    def collect(k, value):
        exchange(k).wait_recv()
        return value + z_buf[k].astype(F32)

    total = lax.fori_loop(1, levels, collect, total)
    out_ref[...] = total.T.astype(BF16)
    for copy in copies:
        copy.wait_send()

    def drain(k, carry):
        exchange(k).wait_send()
        return carry

    lax.fori_loop(1, levels, drain, 0)


def reduce_grad(y, row_scale, cot, dp_count):
    slots, inner = y.shape
    width = cot.shape[1]
    share = width // dp_count
    levels = dp_count // RING
    some = levels // 2
    vmem = pl.BlockSpec(memory_space=pltpu.VMEM)
    dma = pltpu.SemaphoreType.DMA
    return pl.pallas_call(
        grad_kernel,
        name="grads",
        out_shape=jax.ShapeDtypeStruct((inner, share), BF16),
        in_specs=[vmem] * 3,
        out_specs=vmem,
        scratch_shapes=[
            pltpu.VMEM((slots, inner), BF16),
            pltpu.VMEM((levels, RING, share, inner), BF16),
            pltpu.VMEM((some, share, inner), BF16),
            pltpu.VMEM((some, share, inner), BF16),
            pltpu.VMEM((levels, share, inner), BF16),
            pltpu.VMEM((levels, share, inner), BF16),
            pltpu.VMEM((levels, share, inner), BF16),
            pltpu.VMEM((levels, share, inner), BF16),
            dma((6,)),
            dma((6,)),
            dma((levels,)),
            dma((levels,)),
        ],
        compiler_params=pltpu.CompilerParams(
            collective_id=2, has_side_effects=True, vmem_limit_bytes=60 * 1024 * 1024
        ),
    )(y, row_scale, cot)


def corner_turn(tokens, base_rows, baseline_owner):
    dp_count = lax.axis_size("dp")
    tok_rows, feat_width = tokens.shape
    slot_cap = 2 * tok_rows // dp_count
    own_slots = slot_cap * dp_count
    index, starts, ends, owner_start = layout_tables(base_rows, baseline_owner)
    local = jnp.arange(tok_rows, dtype=jnp.int32)
    inside = ((starts[None, :] <= local[:, None]) & (local[:, None] < ends[None, :])).astype(
        jnp.int32
    )
    row_start = jnp.sum(inside * starts[None, :], axis=1)
    row_owner = jnp.sum(inside * baseline_owner[None, :], axis=1)
    row_ostart = jnp.sum(inside * owner_start[None, :], axis=1)
    send_slot = row_owner * slot_cap + row_ostart + local - row_start
    outgoing = (
        jnp.zeros((own_slots, feat_width), jnp.bfloat16)
        .at[send_slot]
        .set(tokens)
        .reshape(dp_count, slot_cap, feat_width)
    )
    owner_index = lax.axis_index("dp")
    place = jnp.arange(slot_cap, dtype=jnp.int32)
    held = (
        (baseline_owner[None, :] == owner_index)
        & (owner_start[None, :] <= place[:, None])
        & (place[:, None] < owner_start[None, :] + base_rows[None, :])
    ).astype(jnp.int32)
    got_start = jnp.sum(held * owner_start[None, :], axis=1)
    got_len = jnp.sum(held * base_rows[None, :], axis=1)
    got_any = jnp.sum(held, axis=1)
    sender = jnp.arange(dp_count, dtype=jnp.int32)[:, None]
    recv_slot = (
        dp_count * got_start[None, :]
        + sender * got_len[None, :]
        + place[None, :]
        - got_start[None, :]
    )
    recv_slot = jnp.where(got_any[None, :] > 0, recv_slot, own_slots).reshape(-1)
    arrived = lax.all_to_all(outgoing, "dp", split_axis=0, concat_axis=0, tiled=True)
    return (
        jnp.zeros((own_slots, feat_width), jnp.bfloat16)
        .at[recv_slot]
        .set(arrived.reshape(-1, feat_width), mode="drop")
    )


def per_device(
    tokens,
    base_rows,
    baseline_owner,
    cotangent,
    *params,
):
    tables = (
        base_rows[:, None],
        base_rows[None, :],
        baseline_owner[:, None],
        baseline_owner[None, :],
    )
    stream = corner_turn(tokens, base_rows, baseline_owner)
    result, y, row_scale = run_blocks(tables, stream, tuple(item[0] for item in params))
    grad = reduce_grad(y, row_scale, cotangent[0], lax.axis_size("dp"))
    return (result[None], grad[None])


def solution(mesh):
    return jax.shard_map(
        per_device,
        mesh=mesh,
        in_specs=(
            P("dp", None),
            P(),
            P(),
            P("section", "dp", None),
            P("section", None),
            P("section", None, "tensor"),
            P("section", None, "tensor"),
            P("section", None, None),
            P("section", None, "tensor"),
            P("section", "tensor"),
            P("section", "tensor"),
            P("section", "tensor"),
            P("section", "tensor"),
            P("section", "tensor", None),
        ),
        out_specs=(P("section", "dp", None), P("section", "tensor", "dp")),
        check_vma=False,
    )
```

```python
import functools

import jax
import jax.numpy as jnp
from jax import lax
from jax.experimental import pallas as pl
from jax.experimental.pallas import tpu as pltpu
from jax.sharding import PartitionSpec as P

MESH = pl.DeviceIdType.MESH
HEADDIM = 64
NSTATE = 128
ROWS = 128
RING = 4
EPS = 1e-05
F32 = jnp.float32
BF16 = jnp.bfloat16


def iota(shape, axis):
    return lax.broadcasted_iota(jnp.int32, shape, axis)


def silu(value):
    return value / (1.0 + jnp.exp(-value))


def softplus(value):
    return jnp.maximum(value, 0.0) + jnp.log1p(jnp.exp(-jnp.abs(value)))


def owner_starts(rows_c, rows_r, own_c, own_r):
    count = rows_r.shape[1]
    down, across = iota((count, count), 0), iota((count, count), 1)
    same = own_c == own_r
    row = jnp.sum(jnp.where(same & (down < across), rows_c, 0), axis=0, keepdims=True)
    col = jnp.sum(jnp.where(same & (across < down), rows_r, 0), axis=1, keepdims=True)
    return row, col


def block_kernel(
    chunks,
    heads,
    rows_c,
    rows_r,
    own_c,
    own_r,
    pre_gain,
    step_bias,
    decay_log,
    skip_gain,
    norm_gain,
    tokens,
    in_hbm,
    gate_hbm,
    state_hbm,
    step_hbm,
    out_hbm,
    out_ref,
    y_ref,
    rs_ref,
    w_in,
    w_gate,
    w_state,
    w_step,
    w_out,
    tok_buf,
    away,
    arrived,
    s_buf,
    u_buf,
    o_buf,
    p_buf,
    a1,
    b1,
    a2,
    b2,
    normed,
    xs_buf,
    gate_buf,
    bc_buf,
    dt_buf,
    state,
    prev,
    seg_col,
    seg_row,
    sq_buf,
    skip_row,
    load_sem,
    turn_send,
    turn_recv,
    feed_send,
    hand_sem,
    hand_send,
    out_sem,
    rs_send,
    rs_recv,
    ag_send,
    ag_recv,
    sq_send,
    sq_recv,
):
    me = lax.axis_index("tensor")
    sec = lax.axis_index("section")
    owner = lax.axis_index("dp")
    right, left, opposite = ((me + 1) % RING, (me + 3) % RING, (me + 2) % RING)
    readers = lax.axis_size("dp")
    inner = w_in.shape[1]
    pairs = heads // 2
    piece = ROWS // RING
    half = piece // 2
    count = rows_r.shape[1]
    slots = chunks * ROWS
    cap = slots // readers
    tok_rows, part = tok_buf.shape
    my_cols = pl.ds(pl.multiple_of((2 * me + sec) * part, part), part)

    loads = [
        pltpu.make_async_copy(src, dst, load_sem.at[k])
        for k, (src, dst) in enumerate(
            (
                (tokens.at[:, my_cols], tok_buf),
                (in_hbm, w_in),
                (state_hbm, w_state),
                (step_hbm, w_step),
                (gate_hbm, w_gate),
                (out_hbm, w_out),
            )
        )
    ]
    for load in loads:
        load.start()

    barrier = pltpu.get_barrier_semaphore()

    def greet(k, carry):
        pl.semaphore_signal(
            barrier, inc=1, device_id={"dp": (owner + k) % readers}, device_id_type=MESH
        )
        return carry

    lax.fori_loop(1, readers, greet, 0)
    for k in range(RING):
        other = (me + k) % RING
        if k:
            pl.semaphore_signal(barrier, inc=1, device_id={"tensor": other}, device_id_type=MESH)
        pl.semaphore_signal(
            barrier,
            inc=1,
            device_id={"section": 1 - sec, "tensor": other},
            device_id_type=MESH,
        )

    def rows_of(t):
        return pl.ds(pl.multiple_of(t * ROWS, ROWS), ROWS)

    def piece_of(who, which=None):
        if which is None:
            return pl.ds(pl.multiple_of(who * piece, piece), piece)
        return pl.ds(pl.multiple_of(who * piece + which * half, half), half)

    def out_piece(t, who, which=None):
        if which is None:
            return pl.ds(pl.multiple_of(t * ROWS + who * piece, piece), piece)
        return pl.ds(pl.multiple_of(t * ROWS + who * piece + which * half, half), half)

    def cap_of(who):
        return pl.ds(pl.multiple_of(who * cap, cap), cap)

    def push(src, dst, send_sem, recv_sem, **where):
        return pltpu.make_async_remote_copy(
            src_ref=src,
            dst_ref=dst,
            send_sem=send_sem,
            recv_sem=recv_sem,
            device_id=where,
            device_id_type=MESH,
        )

    def turn(k):
        other = (owner + k) % readers
        return push(
            away.at[cap_of(other)],
            arrived.at[cap_of(owner)],
            turn_send.at[k],
            turn_recv.at[k],
            dp=other,
        )

    def feed_own(t):
        return pltpu.make_async_copy(s_buf.at[t], u_buf.at[rows_of(t), my_cols], hand_sem.at[t])

    def feed(t, k):
        return push(
            s_buf.at[t],
            u_buf.at[rows_of(t), my_cols],
            feed_send.at[k, t],
            hand_sem.at[t],
            section=0,
            tensor=(me + k) % RING,
        )

    def hand_over(t, k):
        where = (
            lambda: out_piece(t, me),
            lambda: out_piece(t, left),
            lambda: out_piece(t, right),
            lambda: out_piece(t, opposite, 0),
            lambda: out_piece(t, opposite, 1),
        )[k]()
        return push(
            o_buf.at[where], u_buf.at[where], hand_send.at[k, t], hand_sem.at[t], section=1 - sec
        )

    def pass_on(t, *which):
        @pl.when(sec == 0)
        def _():
            for k in which:
                hand_over(t, k).start()

    def store_out(t):
        return pltpu.make_async_copy(o_buf.at[rows_of(t)], out_ref.at[rows_of(t)], out_sem.at[t])

    start_row, start_col = owner_starts(rows_c[...], rows_r[...], own_c[...], own_r[...])
    down, across = iota((count, count), 0), iota((count, count), 1)
    first_c = jnp.sum(jnp.where(across < down, rows_r[...], 0), axis=1, keepdims=True)
    token = iota((count, tok_rows), 1)
    inside = (token >= first_c) & (token < first_c + rows_c[...])
    target = jnp.sum(
        jnp.where(inside, own_c[...] * cap + start_col - first_c + token, 0), axis=0, keepdims=True
    )
    chosen = (iota((slots, tok_rows), 0) == target).astype(F32).astype(BF16)
    loads[0].wait()
    away[...] = jnp.dot(chosen, tok_buf[...], preferred_element_type=F32).astype(BF16)
    arrived[cap_of(owner), :] = away[cap_of(owner), :]
    pl.semaphore_wait(barrier, readers - 1 + RING - 1 + RING)

    def send_turn(k, carry):
        turn(k).start()
        return carry

    lax.fori_loop(1, readers, send_turn, 0)

    ids_c = (iota((count, 1), 0) + 1).astype(F32)
    ids_r = (iota((1, count), 1) + 1).astype(F32)
    slot_r = iota((count, slots), 1)
    held_c = (
        (own_c[...] == owner)
        & (slot_r >= readers * start_col)
        & (slot_r < readers * (start_col + rows_c[...]))
    )
    ids_row = jnp.sum(jnp.where(held_c, ids_c, 0.0), axis=0, keepdims=True)
    for t in range(chunks):
        seg_row[t] = jnp.broadcast_to(ids_row[:, t * ROWS : (t + 1) * ROWS], (8, ROWS))
    slot_c = iota((slots, count), 0)
    held_r = (
        (own_r[...] == owner)
        & (slot_c >= readers * start_row)
        & (slot_c < readers * (start_row + rows_r[...]))
    )
    ids_col = jnp.sum(jnp.where(held_r, ids_r, 0.0), axis=1, keepdims=True)
    seg_col[...] = jnp.broadcast_to(ids_col, (slots, ROWS))
    place, reader = slot_r % cap, slot_r // cap
    held = (own_c[...] == owner) & (place >= start_col) & (place < start_col + rows_c[...])
    goal = jnp.sum(
        jnp.where(held, (readers - 1) * start_col + reader * rows_c[...] + place + 1, 0),
        axis=0,
        keepdims=True,
    ) - 1
    state[...] = jnp.zeros_like(state)
    prev[...] = jnp.full(prev.shape, -1.0, F32)
    lane = iota((ROWS, 128), 1)
    low = lane < HEADDIM

    def spread(value, pair):
        shape = (value.shape[0], 128)
        first = jnp.broadcast_to(value[:, 2 * pair : 2 * pair + 1], shape)
        second = jnp.broadcast_to(value[:, 2 * pair + 1 : 2 * pair + 2], shape)
        return jnp.where(iota(shape, 1) < HEADDIM, first, second)

    for pair in range(pairs):
        skip_row[:, pair * 128 : (pair + 1) * 128] = spread(
            jnp.broadcast_to(skip_gain[...], (8, 128)), pair
        )
    rate = -jnp.exp(decay_log[...])

    def take_turn(k, carry):
        turn(k).wait_recv()
        return carry

    lax.fori_loop(1, readers, take_turn, 0)
    for t in range(chunks):
        placed = (iota((ROWS, slots), 0) + t * ROWS == goal).astype(F32).astype(BF16)
        s_buf[t] = jnp.dot(placed, arrived[...], preferred_element_type=F32).astype(BF16)
        for k in range(1, RING):
            feed(t, k).start()

        @pl.when(sec == 0)
        def _():
            feed_own(t).start()

        @pl.when(sec == 1)
        def _():
            feed(t, 0).start()

    for load in loads[1:]:
        load.wait()

    def stage_in(t):
        pltpu.make_async_copy(u_buf.at[rows_of(t)], u_buf.at[rows_of(t)], hand_sem.at[t]).wait()
        rows_f = u_buf[rows_of(t), :].astype(F32)
        scale = lax.rsqrt(jnp.mean(rows_f * rows_f, axis=-1, keepdims=True) + EPS)
        normed[...] = (rows_f * scale * pre_gain[...]).astype(BF16)
        xs_buf[...] = silu(jnp.dot(normed[...], w_in[...], preferred_element_type=F32)).astype(BF16)
        bc_buf[...] = silu(jnp.dot(normed[...], w_state[...], preferred_element_type=F32)).astype(
            BF16
        )
        dt_buf[...] = softplus(
            jnp.dot(normed[...], w_step[...], preferred_element_type=F32) + step_bias[...]
        )
        gate_buf[...] = silu(jnp.dot(normed[...], w_gate[...], preferred_element_type=F32))

    def stage_scan(t):
        segment_c = seg_col[rows_of(t), :]
        segment_r = jnp.broadcast_to(seg_row[t][0:1, :], (ROWS, ROWS))
        before = jnp.broadcast_to(prev[0:1, :], (ROWS, ROWS))
        last = segment_c[ROWS - 1 : ROWS, :]
        down, across = iota((ROWS, ROWS), 0), iota((ROWS, ROWS), 1)
        causal = down >= across
        hidden = jnp.where(causal & (segment_c == segment_r), 0.0, -1e30)
        dt = dt_buf[...]
        cum = jnp.dot(
            causal.astype(F32),
            dt * rate,
            preferred_element_type=F32,
            precision=lax.Precision.HIGHEST,
        )
        cum_t, dt_t = cum.T, dt.T
        grown = jnp.exp(cum)
        from_before = jnp.where(segment_c == before, grown, 0.0)
        last_cum = cum[ROWS - 1 : ROWS, :]
        tail = jnp.where(segment_c == last, jnp.exp(last_cum - cum), 0.0) * dt
        kept = jnp.where(last == prev[0:1, :], jnp.exp(last_cum), 0.0)
        b_rows, c_rows = bc_buf[:, :NSTATE], bc_buf[:, NSTATE:]
        scores = lax.dot_general(
            c_rows, b_rows, (((1,), (1,)), ((), ())), preferred_element_type=F32
        )
        readout = jnp.dot(c_rows, state[...].astype(BF16), preferred_element_type=F32)
        squares = jnp.zeros((ROWS, 128), F32)
        for pair in range(pairs):
            cols = slice(pair * 128, (pair + 1) * 128)
            x_pair = xs_buf[:, cols]
            x_f = x_pair.astype(F32)
            parts = []
            for head in (2 * pair, 2 * pair + 1):
                falling = jnp.minimum(cum[:, head : head + 1] - cum_t[head : head + 1, :], 0.0)
                weights = jnp.exp(falling + hidden) * scores * dt_t[head : head + 1, :]
                parts.append(jnp.dot(weights.astype(BF16), x_pair, preferred_element_type=F32))
            total = (
                jnp.where(low, parts[0], parts[1])
                + spread(from_before, pair) * readout[:, cols]
                + skip_row[0:1, cols] * x_f
            )
            gated = total * gate_buf[:, cols]
            squares = squares + gated * gated
            y_ref[rows_of(t), cols] = (gated * norm_gain[:, cols]).astype(BF16)
            scaled = (spread(tail, pair) * x_f).astype(BF16)
            fresh = lax.dot_general(
                b_rows, scaled, (((0,), (0,)), ((), ())), preferred_element_type=F32
            )
            state[:, cols] = spread(kept, pair) * state[:, cols] + fresh
        prev[...] = jnp.broadcast_to(last, prev.shape)
        sq_buf[0, t] = jnp.broadcast_to(jnp.sum(squares.T, axis=0, keepdims=True), (8, ROWS))

    def square_copy(t, k):
        return push(
            sq_buf.at[0, t],
            sq_buf.at[k, t],
            sq_send.at[k - 1, t],
            sq_recv.at[k - 1, t],
            tensor=(me + k) % RING,
        )

    def reduce_copy(t, k):
        who, which, dst, to = (
            (opposite, 0, lambda: a1.at[t], right),
            (opposite, 1, lambda: b1.at[t], left),
            (right, 1, lambda: a2.at[t, 1], right),
            (left, 0, lambda: b2.at[t, 0], left),
            (right, 0, lambda: a2.at[t, 0], right),
            (left, 1, lambda: b2.at[t, 1], left),
        )[k]
        return push(
            p_buf.at[t, piece_of(who, which)], dst(), rs_send.at[k, t], rs_recv.at[k, t], tensor=to
        )

    def gather_copy(t, k):
        where, to = (
            (lambda: out_piece(t, me), right),
            (lambda: out_piece(t, me), left),
            (lambda: out_piece(t, left, 0), right),
            (lambda: out_piece(t, right, 1), left),
        )[k]
        rows = o_buf.at[where()]
        return push(rows, rows, ag_send.at[k, t], ag_recv.at[k, t], tensor=to)

    def stage_out(t):
        p_buf[t] = jnp.dot(y_ref[rows_of(t), :], w_out[...], preferred_element_type=F32).astype(
            BF16
        )
        for k in range(4):
            reduce_copy(t, k).start()

    def reduce_second(t):
        for k, who, which, got in ((0, right, 0, a1), (1, left, 1, b1)):
            reduce_copy(t, k).wait_recv()
            where = piece_of(who, which)
            p_buf[t, where, :] = (p_buf[t, where, :].astype(F32) + got[t].astype(F32)).astype(BF16)
            reduce_copy(t, k + 4).start()

    def reduce_last(t):
        for k in range(1, RING):
            square_copy(t, k).wait_recv()
        total = sq_buf[0, t] + sq_buf[1, t] + sq_buf[2, t] + sq_buf[3, t]
        scale = lax.rsqrt(total / (RING * inner) + EPS)
        rs_ref[rows_of(t), :] = jnp.broadcast_to(scale[0:1, :], (ROWS, ROWS)).T
        for k in range(2, 6):
            reduce_copy(t, k).wait_recv()
        for which in (0, 1):
            where = out_piece(t, me, which)
            summed = (
                p_buf[t, piece_of(me, which), :].astype(F32)
                + a2[t, which].astype(F32)
                + b2[t, which].astype(F32)
            )
            o_buf[where, :] = (
                u_buf[where, :].astype(F32) + rs_ref[where, 0:1] * summed
            ).astype(BF16)
        gather_copy(t, 0).start()
        gather_copy(t, 1).start()
        pass_on(t, 0)

    def gather_second(t):
        for k in (0, 1):
            gather_copy(t, k).wait_recv()
            gather_copy(t, k + 2).start()
        pass_on(t, 1, 2)

    def gather_last(t):
        gather_copy(t, 2).wait_recv()
        gather_copy(t, 3).wait_recv()
        pass_on(t, 3, 4)
        store_out(t).start()

    def step(t, carry):
        @pl.when(t >= 4)
        def _():
            gather_last(t - 4)

        @pl.when((t >= 3) & (t < chunks + 3))
        def _():
            gather_second(t - 3)

        @pl.when((t >= 2) & (t < chunks + 2))
        def _():
            reduce_last(t - 2)

        @pl.when(t < chunks)
        def _():
            stage_in(t)

        @pl.when((t >= 1) & (t < chunks + 1))
        def _():
            reduce_second(t - 1)

        @pl.when(t < chunks)
        def _():
            stage_scan(t)
            for k in range(1, RING):
                square_copy(t, k).start()
            stage_out(t)

        return carry

    lax.fori_loop(0, chunks + 4, step, 0)

    def sent_turn(k, carry):
        turn(k).wait_send()
        return carry

    lax.fori_loop(1, readers, sent_turn, 0)

    def drain(t, carry):
        for k in range(6):
            reduce_copy(t, k).wait_send()
        for k in range(4):
            gather_copy(t, k).wait_send()
        for k in range(1, RING):
            square_copy(t, k).wait_send()
            feed(t, k).wait_send()

        @pl.when(sec == 0)
        def _():
            for k in range(5):
                hand_over(t, k).wait_send()

        @pl.when(sec == 1)
        def _():
            feed(t, 0).wait_send()

        store_out(t).wait()
        return carry

    lax.fori_loop(0, chunks, drain, 0)


def run_blocks(tables, tokens, params):
    (
        pre_gain,
        input_proj,
        gate_proj,
        state_proj,
        step_proj,
        step_bias,
        decay_log,
        skip_gain,
        norm_gain,
        out_proj,
    ) = params
    readers = lax.axis_size("dp")
    tok_rows, width = tokens.shape
    slots = 2 * tok_rows
    inner = input_proj.shape[1]
    heads = step_proj.shape[1]
    chunks = slots // ROWS
    part = width // (2 * RING)
    pad = ((0, 0), (0, 128 - heads))
    vmem = pl.BlockSpec(memory_space=pltpu.VMEM)
    anywhere = pl.BlockSpec(memory_space=pl.ANY)
    half = ROWS // RING // 2
    dma = pltpu.SemaphoreType.DMA
    return pl.pallas_call(
        functools.partial(block_kernel, chunks, heads),
        name="blocks",
        out_shape=(
            jax.ShapeDtypeStruct((slots, width), BF16),
            jax.ShapeDtypeStruct((slots, inner), BF16),
            jax.ShapeDtypeStruct((slots, 128), F32),
        ),
        in_specs=[vmem] * 9 + [anywhere] * 6,
        out_specs=(anywhere, vmem, vmem),
        scratch_shapes=[
            pltpu.VMEM((width, inner), BF16),
            pltpu.VMEM((width, inner), BF16),
            pltpu.VMEM((width, 2 * NSTATE), BF16),
            pltpu.VMEM((width, 128), BF16),
            pltpu.VMEM((inner, width), BF16),
            pltpu.VMEM((tok_rows, part), BF16),
            pltpu.VMEM((slots, part), BF16),
            pltpu.VMEM((slots, part), BF16),
            pltpu.VMEM((chunks, ROWS, part), BF16),
            pltpu.VMEM((slots, width), BF16),
            pltpu.VMEM((slots, width), BF16),
            pltpu.VMEM((chunks, ROWS, width), BF16),
            pltpu.VMEM((chunks, half, width), BF16),
            pltpu.VMEM((chunks, half, width), BF16),
            pltpu.VMEM((chunks, 2, half, width), BF16),
            pltpu.VMEM((chunks, 2, half, width), BF16),
            pltpu.VMEM((ROWS, width), BF16),
            pltpu.VMEM((ROWS, inner), BF16),
            pltpu.VMEM((ROWS, inner), F32),
            pltpu.VMEM((ROWS, 2 * NSTATE), BF16),
            pltpu.VMEM((ROWS, 128), F32),
            pltpu.VMEM((NSTATE, inner), F32),
            pltpu.VMEM((8, 128), F32),
            pltpu.VMEM((slots, 128), F32),
            pltpu.VMEM((chunks, 8, 128), F32),
            pltpu.VMEM((RING, chunks, 8, 128), F32),
            pltpu.VMEM((8, inner), F32),
            dma((6,)),
            dma((readers,)),
            dma((readers,)),
            dma((RING, chunks)),
            dma((chunks,)),
            dma((5, chunks)),
            dma((chunks,)),
            dma((6, chunks)),
            dma((6, chunks)),
            dma((4, chunks)),
            dma((4, chunks)),
            dma((3, chunks)),
            dma((3, chunks)),
        ],
        compiler_params=pltpu.CompilerParams(
            collective_id=1, has_side_effects=True, vmem_limit_bytes=60 * 1024 * 1024
        ),
    )(
        *tables,
        pre_gain[None],
        jnp.pad(step_bias[None], pad),
        jnp.pad(decay_log[None], pad),
        jnp.pad(skip_gain[None], pad),
        norm_gain[None],
        tokens,
        input_proj,
        gate_proj,
        state_proj,
        jnp.pad(step_proj, pad),
        out_proj,
    )


def grad_kernel(
    y_ref,
    rs_ref,
    cot,
    out_ref,
    yn,
    g_buf,
    a1,
    b1,
    a2,
    b2,
    h_buf,
    z_buf,
    rs_send,
    rs_recv,
    z_send,
    z_recv,
):
    levels, share = g_buf.shape[0], g_buf.shape[2]
    index = lax.axis_index("dp")
    my_z, my_y = index // RING, index % RING
    right_y, left_y, opposite_y = ((my_y + 1) % RING, (my_y + 3) % RING, (my_y + 2) % RING)
    right, left = my_z * RING + right_y, my_z * RING + left_y
    block = RING * share
    some = levels // 2

    def level(k):
        return ((my_z + k) % levels) * RING + my_y

    barrier = pltpu.get_barrier_semaphore()
    others = [right, left] + [level(k) for k in range(1, levels)]
    for other in others:
        pl.semaphore_signal(barrier, inc=1, device_id={"dp": other}, device_id_type=MESH)

    yn[...] = (y_ref[...].astype(F32) * rs_ref[:, 0:1]).astype(BF16)

    def push(src, dst, send_sem, recv_sem, who):
        return pltpu.make_async_remote_copy(
            src_ref=src,
            dst_ref=dst,
            send_sem=send_sem,
            recv_sem=recv_sem,
            device_id={"dp": who},
            device_id_type=MESH,
        )

    low, high = pl.ds(0, some), pl.ds(some, some)
    copies = (
        push(g_buf.at[low, opposite_y], a1, rs_send.at[0], rs_recv.at[0], right),
        push(g_buf.at[high, opposite_y], b1, rs_send.at[1], rs_recv.at[1], left),
        push(g_buf.at[high, right_y], a2.at[high], rs_send.at[2], rs_recv.at[2], right),
        push(g_buf.at[low, left_y], b2.at[low], rs_send.at[3], rs_recv.at[3], left),
        push(g_buf.at[low, right_y], a2.at[low], rs_send.at[4], rs_recv.at[4], right),
        push(g_buf.at[high, left_y], b2.at[high], rs_send.at[5], rs_recv.at[5], left),
    )

    def term(k, carry):
        cols = pl.ds(pl.multiple_of(k * block, block), block)
        product = lax.dot_general(
            cot[:, cols], yn[...], (((0,), (0,)), ((), ())), preferred_element_type=F32
        )
        g_buf[k] = product.astype(BF16).reshape(RING, share, product.shape[1])
        return carry

    lax.fori_loop(0, some, term, 0)
    pl.semaphore_wait(barrier, len(others))
    copies[0].start()
    copies[3].start()
    lax.fori_loop(some, levels, term, 0)
    copies[1].start()
    copies[2].start()

    copies[0].wait_recv()

    def add_low(k, carry):
        g_buf[k, right_y] = (g_buf[k, right_y].astype(F32) + a1[k].astype(F32)).astype(BF16)
        return carry

    lax.fori_loop(0, some, add_low, 0)
    copies[4].start()
    copies[1].wait_recv()

    def add_high(k, carry):
        g_buf[some + k, left_y] = (g_buf[some + k, left_y].astype(F32) + b1[k].astype(F32)).astype(
            BF16
        )
        return carry

    lax.fori_loop(0, some, add_high, 0)
    copies[5].start()
    for copy in copies[2:]:
        copy.wait_recv()

    def exchange(k):
        return push(
            h_buf.at[(my_z + k) % levels], z_buf.at[k], z_send.at[k], z_recv.at[k], level(k)
        )

    def finish(k, carry):
        who = (my_z + k) % levels
        h_buf[who] = (
            g_buf[who, my_y].astype(F32) + a2[who].astype(F32) + b2[who].astype(F32)
        ).astype(BF16)
        exchange(k).start()
        return carry

    lax.fori_loop(1, levels, finish, 0)
    total = g_buf[my_z, my_y].astype(F32) + a2[my_z].astype(F32) + b2[my_z].astype(F32)

    def collect(k, value):
        exchange(k).wait_recv()
        return value + z_buf[k].astype(F32)

    total = lax.fori_loop(1, levels, collect, total)
    out_ref[...] = total.T.astype(BF16)
    for copy in copies:
        copy.wait_send()

    def drain(k, carry):
        exchange(k).wait_send()
        return carry

    lax.fori_loop(1, levels, drain, 0)


def reduce_grad(y, row_scale, cot, dp_count):
    slots, inner = y.shape
    width = cot.shape[1]
    share = width // dp_count
    levels = dp_count // RING
    some = levels // 2
    vmem = pl.BlockSpec(memory_space=pltpu.VMEM)
    dma = pltpu.SemaphoreType.DMA
    return pl.pallas_call(
        grad_kernel,
        name="grads",
        out_shape=jax.ShapeDtypeStruct((inner, share), BF16),
        in_specs=[vmem] * 3,
        out_specs=vmem,
        scratch_shapes=[
            pltpu.VMEM((slots, inner), BF16),
            pltpu.VMEM((levels, RING, share, inner), BF16),
            pltpu.VMEM((some, share, inner), BF16),
            pltpu.VMEM((some, share, inner), BF16),
            pltpu.VMEM((levels, share, inner), BF16),
            pltpu.VMEM((levels, share, inner), BF16),
            pltpu.VMEM((levels, share, inner), BF16),
            pltpu.VMEM((levels, share, inner), BF16),
            dma((6,)),
            dma((6,)),
            dma((levels,)),
            dma((levels,)),
        ],
        compiler_params=pltpu.CompilerParams(
            collective_id=2, has_side_effects=True, vmem_limit_bytes=60 * 1024 * 1024
        ),
    )(y, row_scale, cot)


def per_device(
    tokens,
    base_rows,
    baseline_owner,
    cotangent,
    *params,
):
    tables = (
        base_rows[:, None],
        base_rows[None, :],
        baseline_owner[:, None],
        baseline_owner[None, :],
    )
    result, y, row_scale = run_blocks(tables, tokens, tuple(item[0] for item in params))
    grad = reduce_grad(y, row_scale, cotangent[0], lax.axis_size("dp"))
    return (result[None], grad[None])


def solution(mesh):
    return jax.shard_map(
        per_device,
        mesh=mesh,
        in_specs=(
            P("dp", None),
            P(),
            P(),
            P("section", "dp", None),
            P("section", None),
            P("section", None, "tensor"),
            P("section", None, "tensor"),
            P("section", None, None),
            P("section", None, "tensor"),
            P("section", "tensor"),
            P("section", "tensor"),
            P("section", "tensor"),
            P("section", "tensor"),
            P("section", "tensor", None),
        ),
        out_specs=(P("section", "dp", None), P("section", "tensor", "dp")),
        check_vma=False,
    )
```

```python
import functools

import jax
import jax.numpy as jnp
from jax import lax
from jax.experimental import pallas as pl
from jax.experimental.pallas import tpu as pltpu
from jax.sharding import PartitionSpec as P

MESH = pl.DeviceIdType.MESH
HEADDIM = 64
NSTATE = 128
ROWS = 128
RING = 4
EPS = 1e-05
F32 = jnp.float32
BF16 = jnp.bfloat16


def iota(shape, axis):
    return lax.broadcasted_iota(jnp.int32, shape, axis)


def silu(value):
    return value / (1.0 + jnp.exp(-value))


def softplus(value):
    return jnp.maximum(value, 0.0) + jnp.log1p(jnp.exp(-jnp.abs(value)))


def owner_starts(rows_c, rows_r, own_c, own_r):
    count = rows_r.shape[1]
    down, across = iota((count, count), 0), iota((count, count), 1)
    same = own_c == own_r
    row = jnp.sum(jnp.where(same & (down < across), rows_c, 0), axis=0, keepdims=True)
    col = jnp.sum(jnp.where(same & (across < down), rows_r, 0), axis=1, keepdims=True)
    return row, col


def block_kernel(
    chunks,
    heads,
    levels,
    rows_r,
    own_r,
    pre_gain,
    step_bias,
    decay_log,
    skip_gain,
    norm_gain,
    step_t,
    tokens,
    in_hbm,
    gate_hbm,
    state_hbm,
    out_hbm,
    cot_hbm,
    out_ref,
    grad_ref,
    w_in,
    w_gate,
    w_state,
    w_step,
    w_out,
    small,
    tok_buf,
    away,
    arrived,
    s_buf,
    r_buf,
    u_buf,
    o_buf,
    p_buf,
    a1,
    b1,
    a2,
    b2,
    normed,
    xs_buf,
    gate_buf,
    bc_buf,
    dt_buf,
    y_ref,
    yn_buf,
    rs_ref,
    state,
    prev,
    seg_col,
    seg_row,
    sq_buf,
    skip_row,
    cot,
    cot_t,
    g_acc,
    g_buf,
    ga1,
    gb1,
    ga2,
    gb2,
    h_buf,
    z_buf,
    load_sem,
    turn_send,
    turn_recv,
    feed_send,
    side_recv,
    relay_send,
    relay_recv,
    fill_send,
    hand_sem,
    hand_send,
    out_sem,
    rs_send,
    rs_recv,
    ag_send,
    ag_recv,
    sq_send,
    sq_recv,
    g_send,
    g_recv,
    z_send,
    z_recv,
):
    me = lax.axis_index("tensor")
    sec = lax.axis_index("section")
    owner = lax.axis_index("dp")
    right, left, opposite = ((me + 1) % RING, (me + 3) % RING, (me + 2) % RING)
    readers = lax.axis_size("dp")
    inner = w_in.shape[1]
    pairs = heads // 2
    piece = ROWS // RING
    half = piece // 2
    count = rows_r.shape[1]
    slots = chunks * ROWS
    cap = slots // readers
    tok_rows, part = tok_buf.shape
    my_cols = pl.ds(pl.multiple_of((2 * me + sec) * part, part), part)
    my_z, my_y = owner // RING, owner % RING
    right_y, left_y, opposite_y = ((my_y + 1) % RING, (my_y + 3) % RING, (my_y + 2) % RING)
    share = g_buf.shape[2]
    block = RING * share
    group = levels // 2
    some = group // 2

    loads = [
        pltpu.make_async_copy(src, dst, load_sem.at[k])
        for k, (src, dst) in enumerate(
            (
                (tokens.at[:, my_cols], tok_buf),
                (in_hbm, w_in),
                (state_hbm, w_state),
                (gate_hbm, w_gate),
                (out_hbm, w_out),
                (cot_hbm, cot),
            )
        )
    ]
    for load in loads:
        load.start()

    barrier = pltpu.get_barrier_semaphore()

    def greet(k, carry):
        pl.semaphore_signal(
            barrier, inc=1, device_id={"dp": (owner + k) % readers}, device_id_type=MESH
        )
        return carry

    lax.fori_loop(1, readers, greet, 0)
    for k in range(RING):
        other = (me + k) % RING
        if k:
            pl.semaphore_signal(barrier, inc=1, device_id={"tensor": other}, device_id_type=MESH)
        pl.semaphore_signal(
            barrier,
            inc=1,
            device_id={"section": 1 - sec, "tensor": other},
            device_id_type=MESH,
        )

    def rows_of(t):
        return pl.ds(pl.multiple_of(t * ROWS, ROWS), ROWS)

    def piece_of(who, which=None):
        if which is None:
            return pl.ds(pl.multiple_of(who * piece, piece), piece)
        return pl.ds(pl.multiple_of(who * piece + which * half, half), half)

    def out_piece(t, who, which=None):
        if which is None:
            return pl.ds(pl.multiple_of(t * ROWS + who * piece, piece), piece)
        return pl.ds(pl.multiple_of(t * ROWS + who * piece + which * half, half), half)

    def cap_of(who):
        return pl.ds(pl.multiple_of(who * cap, cap), cap)

    def push(src, dst, send_sem, recv_sem, **where):
        return pltpu.make_async_remote_copy(
            src_ref=src,
            dst_ref=dst,
            send_sem=send_sem,
            recv_sem=recv_sem,
            device_id=where,
            device_id_type=MESH,
        )

    def turn(k):
        other = (owner + k) % readers
        return push(
            away.at[cap_of(other)],
            arrived.at[cap_of(owner)],
            turn_send.at[k],
            turn_recv.at[k],
            dp=other,
        )

    def feed_own(t):
        return pltpu.make_async_copy(s_buf.at[t], u_buf.at[rows_of(t), my_cols], hand_sem.at[t])

    def feed_core(t):
        return push(
            s_buf.at[t],
            u_buf.at[rows_of(t), my_cols],
            feed_send.at[2, t],
            hand_sem.at[t],
            section=0,
        )

    def feed_side(t, k):
        return push(
            s_buf.at[t],
            r_buf.at[t, :, my_cols],
            feed_send.at[k, t],
            side_recv.at[k, t],
            section=1,
            tensor=(right, left)[k],
        )

    def held_of(t, k, kind):
        near, far = (left, right)[k], opposite
        half_rows = pl.ds(k * (ROWS // 2), ROWS // 2)
        who = far if kind == 2 else near
        cols = pl.ds(pl.multiple_of(who * 2 * part, 2 * part), 2 * part)
        if kind == 0:
            return r_buf.at[t, :, cols], u_buf.at[rows_of(t), cols]
        there = pl.ds(pl.multiple_of(t * ROWS + k * (ROWS // 2), ROWS // 2), ROWS // 2)
        return r_buf.at[t, half_rows, cols], u_buf.at[there, cols]

    def relay(t, k):
        src, _ = held_of(t, k, 1)
        return push(
            src, src, relay_send.at[k, t], relay_recv.at[k, t], tensor=(right, left)[k]
        )

    def fill(t, k, kind):
        src, dst = held_of(t, k, kind)
        return push(src, dst, fill_send.at[k + kind, t], hand_sem.at[t], section=0)

    def sides(t, carry):
        for k in (0, 1):
            here, _ = held_of(t, k, 0)
            pltpu.make_async_copy(here, here, side_recv.at[k, t]).wait()
            relay(t, k).start()
            fill(t, k, 0).start()
        return carry

    def relayed(t, carry):
        for k in (0, 1):
            relay(t, k).wait_recv()
            fill(t, k, 2).start()
        return carry

    def hand_over(t, k):
        where = (
            lambda: out_piece(t, me),
            lambda: out_piece(t, left),
            lambda: out_piece(t, right),
            lambda: out_piece(t, opposite, 0),
            lambda: out_piece(t, opposite, 1),
        )[k]()
        return push(
            o_buf.at[where], u_buf.at[where], hand_send.at[k, t], hand_sem.at[t], section=1 - sec
        )

    def pass_on(t, *which):
        @pl.when(sec == 0)
        def _():
            for k in which:
                hand_over(t, k).start()

    def store_out(t):
        return pltpu.make_async_copy(o_buf.at[rows_of(t)], out_ref.at[rows_of(t)], out_sem.at[t])

    def column(row):
        return jnp.broadcast_to(row.astype(F32), (count, count)).T[:, 0:1].astype(jnp.int32)

    rows_c, own_c = column(rows_r[...]), column(own_r[...])
    start_row, start_col = owner_starts(rows_c, rows_r[...], own_c, own_r[...])
    down, across = iota((count, count), 0), iota((count, count), 1)
    first_c = jnp.sum(jnp.where(across < down, rows_r[...], 0), axis=1, keepdims=True)
    token = iota((count, tok_rows), 1)
    inside = (token >= first_c) & (token < first_c + rows_c)
    target = jnp.sum(
        jnp.where(inside, own_c * cap + start_col - first_c + token, 0), axis=0, keepdims=True
    )
    chosen = (iota((slots, tok_rows), 0) == target).astype(F32).astype(BF16)
    loads[0].wait()
    away[...] = jnp.dot(chosen, tok_buf[...], preferred_element_type=F32).astype(BF16)
    arrived[cap_of(owner), :] = away[cap_of(owner), :]
    pl.semaphore_wait(barrier, readers - 1 + RING - 1 + RING)

    def send_turn(k, carry):
        turn(k).start()
        return carry

    lax.fori_loop(1, readers, send_turn, 0)

    ids_c = (iota((count, 1), 0) + 1).astype(F32)
    ids_r = (iota((1, count), 1) + 1).astype(F32)
    slot_r = iota((count, slots), 1)
    held_c = (
        (own_c == owner)
        & (slot_r >= readers * start_col)
        & (slot_r < readers * (start_col + rows_c))
    )
    ids_row = jnp.sum(jnp.where(held_c, ids_c, 0.0), axis=0, keepdims=True)
    for t in range(chunks):
        seg_row[t] = jnp.broadcast_to(ids_row[:, t * ROWS : (t + 1) * ROWS], (8, ROWS))
    slot_c = iota((slots, count), 0)
    held_r = (
        (own_r[...] == owner)
        & (slot_c >= readers * start_row)
        & (slot_c < readers * (start_row + rows_r[...]))
    )
    ids_col = jnp.sum(jnp.where(held_r, ids_r, 0.0), axis=1, keepdims=True)
    seg_col[...] = jnp.broadcast_to(ids_col, (slots, ROWS))
    place, reader = slot_r % cap, slot_r // cap
    held = (own_c == owner) & (place >= start_col) & (place < start_col + rows_c)
    goal = jnp.sum(
        jnp.where(held, (readers - 1) * start_col + reader * rows_c + place + 1, 0),
        axis=0,
        keepdims=True,
    ) - 1
    state[...] = jnp.zeros_like(state)
    prev[...] = jnp.full(prev.shape, -1.0, F32)
    lane = iota((ROWS, 128), 1)
    low = lane < HEADDIM

    def spread(value, pair):
        shape = (value.shape[0], 128)
        first = jnp.broadcast_to(value[:, 2 * pair : 2 * pair + 1], shape)
        second = jnp.broadcast_to(value[:, 2 * pair + 1 : 2 * pair + 2], shape)
        return jnp.where(iota(shape, 1) < HEADDIM, first, second)

    small[...] = jnp.zeros_like(small)
    for k, ref in enumerate((step_bias, decay_log, skip_gain)):
        small[k, 0:1, 0:heads] = ref[...]
    w_step[...] = jnp.concatenate(
        [step_t[...].astype(F32), jnp.zeros((128 - heads, step_t.shape[1]), F32)], axis=0
    ).astype(BF16)
    for pair in range(pairs):
        skip_row[:, pair * 128 : (pair + 1) * 128] = spread(
            jnp.broadcast_to(small[2, 0:1, :], (8, 128)), pair
        )
    rate = -jnp.exp(small[1, 0:1, :])

    loads[5].wait()

    def level_of(m):
        return (my_z + m + 2) % levels

    def turn_cot(m, carry):
        cols = pl.ds(pl.multiple_of(level_of(m) * block, block), block)
        cot_t[m] = cot[:, cols].T
        return carry

    lax.fori_loop(0, levels, turn_cot, 0)

    def take_turn(k, carry):
        turn(k).wait_recv()
        return carry

    lax.fori_loop(1, readers, take_turn, 0)
    for t in range(chunks):
        placed = (iota((ROWS, slots), 0) + t * ROWS == goal).astype(F32).astype(BF16)
        s_buf[t] = jnp.dot(placed, arrived[...], preferred_element_type=F32).astype(BF16)
        feed_side(t, 0).start()
        feed_side(t, 1).start()

        @pl.when(sec == 0)
        def _():
            feed_own(t).start()

        @pl.when(sec == 1)
        def _():
            feed_core(t).start()

    @pl.when(sec == 1)
    def _():
        def relay_step(t, carry):
            @pl.when(t < chunks)
            def _():
                sides(t, 0)

            @pl.when(t >= 1)
            def _():
                relayed(t - 1, 0)

            return carry

        lax.fori_loop(0, chunks + 1, relay_step, 0)

    for load in loads[1:5]:
        load.wait()

    def stage_in(t):
        pltpu.make_async_copy(u_buf.at[rows_of(t)], u_buf.at[rows_of(t)], hand_sem.at[t]).wait()
        rows_f = u_buf[rows_of(t), :].astype(F32)
        scale = lax.rsqrt(jnp.mean(rows_f * rows_f, axis=-1, keepdims=True) + EPS)
        normed[...] = (rows_f * scale * pre_gain[...]).astype(BF16)
        xs_buf[...] = silu(jnp.dot(normed[...], w_in[...], preferred_element_type=F32)).astype(BF16)
        bc_buf[...] = silu(jnp.dot(normed[...], w_state[...], preferred_element_type=F32)).astype(
            BF16
        )
        dt_buf[...] = softplus(
            lax.dot_general(
                normed[...], w_step[...], (((1,), (1,)), ((), ())), preferred_element_type=F32
            )
            + small[0, 0:1, :]
        )
        gate_buf[...] = silu(jnp.dot(normed[...], w_gate[...], preferred_element_type=F32))

    def stage_scan(t):
        segment_c = seg_col[rows_of(t), :]
        segment_r = jnp.broadcast_to(seg_row[t][0:1, :], (ROWS, ROWS))
        before = jnp.broadcast_to(prev[0:1, :], (ROWS, ROWS))
        last = segment_c[ROWS - 1 : ROWS, :]
        down, across = iota((ROWS, ROWS), 0), iota((ROWS, ROWS), 1)
        causal = down >= across
        hidden = jnp.where(causal & (segment_c == segment_r), 0.0, -1e30)
        dt = dt_buf[...]
        cum = jnp.dot(
            causal.astype(F32),
            dt * rate,
            preferred_element_type=F32,
            precision=lax.Precision.HIGHEST,
        )
        cum_t, dt_t = cum.T, dt.T
        grown = jnp.exp(cum)
        from_before = jnp.where(segment_c == before, grown, 0.0)
        last_cum = cum[ROWS - 1 : ROWS, :]
        tail = jnp.where(segment_c == last, jnp.exp(last_cum - cum), 0.0) * dt
        kept = jnp.where(last == prev[0:1, :], jnp.exp(last_cum), 0.0)
        b_rows, c_rows = bc_buf[:, :NSTATE], bc_buf[:, NSTATE:]
        scores = lax.dot_general(
            c_rows, b_rows, (((1,), (1,)), ((), ())), preferred_element_type=F32
        )
        readout = jnp.dot(c_rows, state[...].astype(BF16), preferred_element_type=F32)
        squares = jnp.zeros((ROWS, 128), F32)
        for pair in range(pairs):
            cols = slice(pair * 128, (pair + 1) * 128)
            x_pair = xs_buf[:, cols]
            x_f = x_pair.astype(F32)
            parts = []
            for head in (2 * pair, 2 * pair + 1):
                falling = jnp.minimum(cum[:, head : head + 1] - cum_t[head : head + 1, :], 0.0)
                weights = jnp.exp(falling + hidden) * scores * dt_t[head : head + 1, :]
                parts.append(jnp.dot(weights.astype(BF16), x_pair, preferred_element_type=F32))
            total = (
                jnp.where(low, parts[0], parts[1])
                + spread(from_before, pair) * readout[:, cols]
                + skip_row[0:1, cols] * x_f
            )
            gated = total * gate_buf[:, cols]
            squares = squares + gated * gated
            y_ref[rows_of(t), cols] = (gated * norm_gain[:, cols]).astype(BF16)
            scaled = (spread(tail, pair) * x_f).astype(BF16)
            fresh = lax.dot_general(
                b_rows, scaled, (((0,), (0,)), ((), ())), preferred_element_type=F32
            )
            state[:, cols] = spread(kept, pair) * state[:, cols] + fresh
        prev[...] = jnp.broadcast_to(last, prev.shape)
        sq_buf[0, t] = jnp.broadcast_to(jnp.sum(squares.T, axis=0, keepdims=True), (8, ROWS))

    def square_copy(t, k):
        return push(
            sq_buf.at[0, t],
            sq_buf.at[k, t],
            sq_send.at[k - 1, t],
            sq_recv.at[k - 1, t],
            tensor=(me + k) % RING,
        )

    def reduce_copy(t, k):
        who, which, dst, to = (
            (opposite, 0, lambda: a1.at[t], right),
            (opposite, 1, lambda: b1.at[t], left),
            (right, 1, lambda: a2.at[t, 1], right),
            (left, 0, lambda: b2.at[t, 0], left),
            (right, 0, lambda: a2.at[t, 0], right),
            (left, 1, lambda: b2.at[t, 1], left),
        )[k]
        return push(
            p_buf.at[t, piece_of(who, which)], dst(), rs_send.at[k, t], rs_recv.at[k, t], tensor=to
        )

    def gather_copy(t, k):
        where, to = (
            (lambda: out_piece(t, me), right),
            (lambda: out_piece(t, me), left),
            (lambda: out_piece(t, left, 0), right),
            (lambda: out_piece(t, right, 1), left),
        )[k]
        rows = o_buf.at[where()]
        return push(rows, rows, ag_send.at[k, t], ag_recv.at[k, t], tensor=to)

    def stage_out(t):
        p_buf[t] = jnp.dot(y_ref[rows_of(t), :], w_out[...], preferred_element_type=F32).astype(
            BF16
        )
        for k in range(4):
            reduce_copy(t, k).start()

    def reduce_second(t):
        for k, who, which, got in ((0, right, 0, a1), (1, left, 1, b1)):
            reduce_copy(t, k).wait_recv()
            where = piece_of(who, which)
            p_buf[t, where, :] = (p_buf[t, where, :].astype(F32) + got[t].astype(F32)).astype(BF16)
            reduce_copy(t, k + 4).start()

    def reduce_last(t):
        for k in range(1, RING):
            square_copy(t, k).wait_recv()
        total = sq_buf[0, t] + sq_buf[1, t] + sq_buf[2, t] + sq_buf[3, t]
        scale = lax.rsqrt(total / (RING * inner) + EPS)
        rs_ref[rows_of(t), :] = jnp.broadcast_to(scale[0:1, :], (ROWS, ROWS)).T
        yn_buf[rows_of(t), :] = (
            y_ref[rows_of(t), :].astype(F32) * rs_ref[rows_of(t), 0:1]
        ).astype(BF16)
        for k in range(2, 6):
            reduce_copy(t, k).wait_recv()
        for which in (0, 1):
            where = out_piece(t, me, which)
            summed = (
                p_buf[t, piece_of(me, which), :].astype(F32)
                + a2[t, which].astype(F32)
                + b2[t, which].astype(F32)
            )
            o_buf[where, :] = (
                u_buf[where, :].astype(F32) + rs_ref[where, 0:1] * summed
            ).astype(BF16)
        gather_copy(t, 0).start()
        gather_copy(t, 1).start()
        pass_on(t, 0)

    def gather_second(t):
        for k in (0, 1):
            gather_copy(t, k).wait_recv()
            gather_copy(t, k + 2).start()
        pass_on(t, 1, 2)

    def gather_last(t):
        gather_copy(t, 2).wait_recv()
        gather_copy(t, 3).wait_recv()
        pass_on(t, 3, 4)
        store_out(t).start()

    early = (chunks - 1) * ROWS

    def grad_early(m, carry):
        g_acc[m] = jnp.dot(cot_t[m, :, :early], yn_buf[:early, :], preferred_element_type=F32)
        return carry

    def grad_late(m, carry):
        term = g_acc[m] + jnp.dot(
            cot_t[m, :, early:], yn_buf[early:, :], preferred_element_type=F32
        )
        g_buf[m] = term.astype(BF16).reshape(RING, share, inner)
        return carry

    def grad_copy(g, k):
        base = g * group
        first, second = pl.ds(base, some), pl.ds(base + some, some)
        src, dst, to = (
            (lambda: g_buf.at[first, opposite_y], lambda: ga1.at[g], right_y),
            (lambda: g_buf.at[second, opposite_y], lambda: gb1.at[g], left_y),
            (lambda: g_buf.at[second, right_y], lambda: ga2.at[second], right_y),
            (lambda: g_buf.at[first, left_y], lambda: gb2.at[first], left_y),
            (lambda: g_buf.at[first, right_y], lambda: ga2.at[first], right_y),
            (lambda: g_buf.at[second, left_y], lambda: gb2.at[second], left_y),
        )[k]
        return push(src(), dst(), g_send.at[k, g], g_recv.at[k, g], dp=my_z * RING + to)

    def exchange(m):
        return push(
            h_buf.at[m],
            z_buf.at[m],
            z_send.at[m],
            z_recv.at[m],
            dp=level_of(m) * RING + my_y,
        )

    def grad_send(g):
        lax.fori_loop(g * group, (g + 1) * group, grad_late, 0)
        for k in range(4):
            grad_copy(g, k).start()

    def grad_second(g):
        for k, offset, who, got in ((0, 0, right_y, ga1), (1, some, left_y, gb1)):
            grad_copy(g, k).wait_recv()
            for j in range(some):
                m = g * group + offset + j
                g_buf[m, who] = (g_buf[m, who].astype(F32) + got[g, j].astype(F32)).astype(BF16)
            grad_copy(g, k + 4).start()

    def level_sum(m):
        return g_buf[m, my_y].astype(F32) + ga2[m].astype(F32) + gb2[m].astype(F32)

    def grad_finish(g):
        for k in range(2, 6):
            grad_copy(g, k).wait_recv()
        for m in range(g * group, (g + 1) * group):
            if m != levels - 2:
                h_buf[m] = level_sum(m).astype(BF16)
                exchange(m).start()

    def step(t, carry):
        @pl.when(t >= 4)
        def _():
            gather_last(t - 4)

        @pl.when((t >= 3) & (t < chunks + 3))
        def _():
            gather_second(t - 3)

        @pl.when((t >= 2) & (t < chunks + 2))
        def _():
            reduce_last(t - 2)

        @pl.when(t < chunks)
        def _():
            stage_in(t)

        @pl.when((t >= 1) & (t < chunks + 1))
        def _():
            reduce_second(t - 1)

        @pl.when(t < chunks)
        def _():
            stage_scan(t)
            for k in range(1, RING):
                square_copy(t, k).start()
            stage_out(t)

        @pl.when(t == chunks)
        def _():
            lax.fori_loop(0, levels, grad_early, 0)

        @pl.when(t == chunks + 1)
        def _():
            grad_send(0)
            grad_send(1)

        return carry

    lax.fori_loop(0, chunks + 4, step, 0)
    grad_second(0)
    grad_second(1)
    grad_finish(0)
    grad_finish(1)
    total = level_sum(levels - 2)
    for m in range(levels):
        if m != levels - 2:
            exchange(m).wait_recv()
            total = total + z_buf[m].astype(F32)
    grad_ref[...] = total.astype(BF16)
    for g in (0, 1):
        for k in range(6):
            grad_copy(g, k).wait_send()
    for m in range(levels):
        if m != levels - 2:
            exchange(m).wait_send()

    def sent_turn(k, carry):
        turn(k).wait_send()
        return carry

    lax.fori_loop(1, readers, sent_turn, 0)

    def drain(t, carry):
        for k in range(6):
            reduce_copy(t, k).wait_send()
        for k in range(4):
            gather_copy(t, k).wait_send()
        for k in range(1, RING):
            square_copy(t, k).wait_send()
        feed_side(t, 0).wait_send()
        feed_side(t, 1).wait_send()

        @pl.when(sec == 0)
        def _():
            for k in range(5):
                hand_over(t, k).wait_send()

        @pl.when(sec == 1)
        def _():
            feed_core(t).wait_send()
            for k in (0, 1):
                relay(t, k).wait_send()
                fill(t, k, 0).wait_send()
                fill(t, k, 2).wait_send()

        store_out(t).wait()
        return carry

    lax.fori_loop(0, chunks, drain, 0)


def run_blocks(tables, tokens, cot, params):
    (
        pre_gain,
        input_proj,
        gate_proj,
        state_proj,
        step_proj,
        step_bias,
        decay_log,
        skip_gain,
        norm_gain,
        out_proj,
    ) = params
    readers = lax.axis_size("dp")
    tok_rows, width = tokens.shape
    slots = 2 * tok_rows
    inner = input_proj.shape[1]
    heads = step_proj.shape[1]
    chunks = slots // ROWS
    part = width // (2 * RING)
    share = width // readers
    levels = readers // RING
    some = levels // 4
    vmem = pl.BlockSpec(memory_space=pltpu.VMEM)
    anywhere = pl.BlockSpec(memory_space=pl.ANY)
    half = ROWS // RING // 2
    dma = pltpu.SemaphoreType.DMA
    return pl.pallas_call(
        functools.partial(block_kernel, chunks, heads, levels),
        name="blocks",
        out_shape=(
            jax.ShapeDtypeStruct((slots, width), BF16),
            jax.ShapeDtypeStruct((share, inner), BF16),
        ),
        in_specs=[vmem] * 8 + [anywhere] * 6,
        out_specs=(anywhere, vmem),
        scratch_shapes=[
            pltpu.VMEM((width, inner), BF16),
            pltpu.VMEM((width, inner), BF16),
            pltpu.VMEM((width, 2 * NSTATE), BF16),
            pltpu.VMEM((128, width), BF16),
            pltpu.VMEM((inner, width), BF16),
            pltpu.VMEM((3, 8, 128), F32),
            pltpu.VMEM((tok_rows, part), BF16),
            pltpu.VMEM((slots, part), BF16),
            pltpu.VMEM((slots, part), BF16),
            pltpu.VMEM((chunks, ROWS, part), BF16),
            pltpu.VMEM((chunks, ROWS, width), BF16),
            pltpu.VMEM((slots, width), BF16),
            pltpu.VMEM((slots, width), BF16),
            pltpu.VMEM((chunks, ROWS, width), BF16),
            pltpu.VMEM((chunks, half, width), BF16),
            pltpu.VMEM((chunks, half, width), BF16),
            pltpu.VMEM((chunks, 2, half, width), BF16),
            pltpu.VMEM((chunks, 2, half, width), BF16),
            pltpu.VMEM((ROWS, width), BF16),
            pltpu.VMEM((ROWS, inner), BF16),
            pltpu.VMEM((ROWS, inner), F32),
            pltpu.VMEM((ROWS, 2 * NSTATE), BF16),
            pltpu.VMEM((ROWS, 128), F32),
            pltpu.VMEM((slots, inner), BF16),
            pltpu.VMEM((slots, inner), BF16),
            pltpu.VMEM((slots, 128), F32),
            pltpu.VMEM((NSTATE, inner), F32),
            pltpu.VMEM((8, 128), F32),
            pltpu.VMEM((slots, 128), F32),
            pltpu.VMEM((chunks, 8, 128), F32),
            pltpu.VMEM((RING, chunks, 8, 128), F32),
            pltpu.VMEM((8, inner), F32),
            pltpu.VMEM((slots, width), BF16),
            pltpu.VMEM((levels, RING * share, slots), BF16),
            pltpu.VMEM((levels, RING * share, inner), F32),
            pltpu.VMEM((levels, RING, share, inner), BF16),
            pltpu.VMEM((2, some, share, inner), BF16),
            pltpu.VMEM((2, some, share, inner), BF16),
            pltpu.VMEM((levels, share, inner), BF16),
            pltpu.VMEM((levels, share, inner), BF16),
            pltpu.VMEM((levels, share, inner), BF16),
            pltpu.VMEM((levels, share, inner), BF16),
            dma((6,)),
            dma((readers,)),
            dma((readers,)),
            dma((3, chunks)),
            dma((2, chunks)),
            dma((2, chunks)),
            dma((2, chunks)),
            dma((4, chunks)),
            dma((chunks,)),
            dma((5, chunks)),
            dma((chunks,)),
            dma((6, chunks)),
            dma((6, chunks)),
            dma((4, chunks)),
            dma((4, chunks)),
            dma((3, chunks)),
            dma((3, chunks)),
            dma((6, 2)),
            dma((6, 2)),
            dma((levels,)),
            dma((levels,)),
        ],
        compiler_params=pltpu.CompilerParams(
            collective_id=1, has_side_effects=True, vmem_limit_bytes=60 * 1024 * 1024
        ),
    )(
        *tables,
        pre_gain[None],
        step_bias[None],
        decay_log[None],
        skip_gain[None],
        norm_gain[None],
        step_proj.T,
        tokens,
        input_proj,
        gate_proj,
        state_proj,
        out_proj,
        cot,
    )


def per_device(
    tokens,
    base_rows,
    baseline_owner,
    cotangent,
    *params,
):
    tables = (base_rows[None, :], baseline_owner[None, :])
    result, grad = run_blocks(
        tables, tokens, cotangent[0], tuple(item[0] for item in params)
    )
    return (result[None], grad.T[None])


def solution(mesh):
    return jax.shard_map(
        per_device,
        mesh=mesh,
        in_specs=(
            P("dp", None),
            P(),
            P(),
            P("section", "dp", None),
            P("section", None),
            P("section", None, "tensor"),
            P("section", None, "tensor"),
            P("section", None, None),
            P("section", None, "tensor"),
            P("section", "tensor"),
            P("section", "tensor"),
            P("section", "tensor"),
            P("section", "tensor"),
            P("section", "tensor", None),
        ),
        out_specs=(P("section", "dp", None), P("section", "tensor", "dp")),
        check_vma=False,
    )
```

```python
import functools

import jax
import jax.numpy as jnp
from jax import lax
from jax.experimental import pallas as pl
from jax.experimental.pallas import tpu as pltpu
from jax.sharding import PartitionSpec as P

MESH = pl.DeviceIdType.MESH
HEADDIM = 64
NSTATE = 128
ROWS = 128
SUB = 128
RING = 4
EPS = 1e-05
F32 = jnp.float32
BF16 = jnp.bfloat16


def iota(shape, axis):
    return lax.broadcasted_iota(jnp.int32, shape, axis)


def silu(value):
    return value / (1.0 + jnp.exp(-value))


def softplus(value):
    return jnp.maximum(value, 0.0) + jnp.log1p(jnp.exp(-jnp.abs(value)))


def owner_starts(rows_c, rows_r, own_c, own_r):
    count = rows_r.shape[1]
    down, across = iota((count, count), 0), iota((count, count), 1)
    same = own_c == own_r
    row = jnp.sum(jnp.where(same & (down < across), rows_c, 0), axis=0, keepdims=True)
    col = jnp.sum(jnp.where(same & (across < down), rows_r, 0), axis=1, keepdims=True)
    return row, col


def block_kernel(
    chunks,
    heads,
    levels,
    rows_r,
    own_r,
    pre_gain,
    step_bias,
    decay_log,
    skip_gain,
    norm_gain,
    step_t,
    tokens,
    in_hbm,
    gate_hbm,
    state_hbm,
    out_hbm,
    cot_hbm,
    out_ref,
    grad_ref,
    w_in,
    w_gate,
    w_state,
    w_step,
    w_out,
    small,
    tok_buf,
    away,
    arrived,
    s_buf,
    r_buf,
    u_buf,
    o_buf,
    p_buf,
    a1,
    b1,
    a2,
    b2,
    normed,
    xs_buf,
    gate_buf,
    bc_buf,
    dt_buf,
    y_ref,
    yn_buf,
    rs_ref,
    state,
    prev,
    seg_col,
    seg_row,
    sq_buf,
    skip_row,
    cot,
    cot_t,
    g_acc,
    g_buf,
    ga1,
    gb1,
    ga2,
    gb2,
    h_buf,
    z_buf,
    load_sem,
    turn_send,
    turn_recv,
    feed_send,
    side_recv,
    relay_send,
    relay_recv,
    fill_send,
    hand_sem,
    hand_send,
    out_sem,
    rs_send,
    rs_recv,
    ag_send,
    ag_recv,
    sq_send,
    sq_recv,
    g_send,
    g_recv,
    z_send,
    z_recv,
):
    me = lax.axis_index("tensor")
    sec = lax.axis_index("section")
    owner = lax.axis_index("dp")
    right, left, opposite = ((me + 1) % RING, (me + 3) % RING, (me + 2) % RING)
    readers = lax.axis_size("dp")
    inner = w_in.shape[1]
    pairs = heads // 2
    piece = ROWS // RING
    half = piece // 2
    count = rows_r.shape[1]
    slots = chunks * ROWS
    subs = ROWS // SUB
    cap = slots // readers
    tok_rows, part = tok_buf.shape
    my_cols = pl.ds(pl.multiple_of((2 * me + sec) * part, part), part)
    my_z, my_y = owner // RING, owner % RING
    right_y, left_y, opposite_y = ((my_y + 1) % RING, (my_y + 3) % RING, (my_y + 2) % RING)
    share = g_buf.shape[2]
    block = RING * share
    group = levels // 2
    some = group // 2

    loads = [
        pltpu.make_async_copy(src, dst, load_sem.at[k])
        for k, (src, dst) in enumerate(
            (
                (tokens.at[:, my_cols], tok_buf),
                (in_hbm, w_in),
                (state_hbm, w_state),
                (gate_hbm, w_gate),
                (out_hbm, w_out),
                (cot_hbm, cot),
            )
        )
    ]
    for load in loads:
        load.start()

    barrier = pltpu.get_barrier_semaphore()

    def greet(k, carry):
        pl.semaphore_signal(
            barrier, inc=1, device_id={"dp": (owner + k) % readers}, device_id_type=MESH
        )
        return carry

    lax.fori_loop(1, readers, greet, 0)
    for k in range(RING):
        other = (me + k) % RING
        if k:
            pl.semaphore_signal(barrier, inc=1, device_id={"tensor": other}, device_id_type=MESH)
        pl.semaphore_signal(
            barrier,
            inc=1,
            device_id={"section": 1 - sec, "tensor": other},
            device_id_type=MESH,
        )

    def rows_of(t):
        return pl.ds(pl.multiple_of(t * ROWS, ROWS), ROWS)

    def piece_of(who, which=None):
        if which is None:
            return pl.ds(pl.multiple_of(who * piece, piece), piece)
        return pl.ds(pl.multiple_of(who * piece + which * half, half), half)

    def out_piece(t, who, which=None):
        if which is None:
            return pl.ds(pl.multiple_of(t * ROWS + who * piece, piece), piece)
        return pl.ds(pl.multiple_of(t * ROWS + who * piece + which * half, half), half)

    def cap_of(who):
        return pl.ds(pl.multiple_of(who * cap, cap), cap)

    def push(src, dst, send_sem, recv_sem, **where):
        return pltpu.make_async_remote_copy(
            src_ref=src,
            dst_ref=dst,
            send_sem=send_sem,
            recv_sem=recv_sem,
            device_id=where,
            device_id_type=MESH,
        )

    def turn(k):
        other = (owner + k) % readers
        return push(
            away.at[cap_of(other)],
            arrived.at[cap_of(owner)],
            turn_send.at[k],
            turn_recv.at[k],
            dp=other,
        )

    def feed_own(t):
        return pltpu.make_async_copy(s_buf.at[t], u_buf.at[rows_of(t), my_cols], hand_sem.at[t])

    def feed_core(t):
        return push(
            s_buf.at[t],
            u_buf.at[rows_of(t), my_cols],
            feed_send.at[2, t],
            hand_sem.at[t],
            section=0,
        )

    def feed_side(t, k):
        return push(
            s_buf.at[t],
            r_buf.at[t, :, my_cols],
            feed_send.at[k, t],
            side_recv.at[k, t],
            section=1,
            tensor=(right, left)[k],
        )

    def held_of(t, k, kind):
        near, far = (left, right)[k], opposite
        half_rows = pl.ds(k * (ROWS // 2), ROWS // 2)
        who = far if kind == 2 else near
        cols = pl.ds(pl.multiple_of(who * 2 * part, 2 * part), 2 * part)
        if kind == 0:
            return r_buf.at[t, :, cols], u_buf.at[rows_of(t), cols]
        there = pl.ds(pl.multiple_of(t * ROWS + k * (ROWS // 2), ROWS // 2), ROWS // 2)
        return r_buf.at[t, half_rows, cols], u_buf.at[there, cols]

    def relay(t, k):
        src, _ = held_of(t, k, 1)
        return push(
            src, src, relay_send.at[k, t], relay_recv.at[k, t], tensor=(right, left)[k]
        )

    def fill(t, k, kind):
        src, dst = held_of(t, k, kind)
        return push(src, dst, fill_send.at[k + kind, t], hand_sem.at[t], section=0)

    def sides(t, carry):
        for k in (0, 1):
            here, _ = held_of(t, k, 0)
            pltpu.make_async_copy(here, here, side_recv.at[k, t]).wait()
            relay(t, k).start()
            fill(t, k, 0).start()
        return carry

    def relayed(t, carry):
        for k in (0, 1):
            relay(t, k).wait_recv()
            fill(t, k, 2).start()
        return carry

    def hand_over(t, k):
        where = (
            lambda: out_piece(t, me),
            lambda: out_piece(t, left),
            lambda: out_piece(t, right),
            lambda: out_piece(t, opposite, 0),
            lambda: out_piece(t, opposite, 1),
        )[k]()
        return push(
            o_buf.at[where], u_buf.at[where], hand_send.at[k, t], hand_sem.at[t], section=1 - sec
        )

    def pass_on(t, *which):
        @pl.when(sec == 0)
        def _():
            for k in which:
                hand_over(t, k).start()

    def store_out(t):
        return pltpu.make_async_copy(o_buf.at[rows_of(t)], out_ref.at[rows_of(t)], out_sem.at[t])

    def column(row):
        return jnp.broadcast_to(row.astype(F32), (count, count)).T[:, 0:1].astype(jnp.int32)

    rows_c, own_c = column(rows_r[...]), column(own_r[...])
    start_row, start_col = owner_starts(rows_c, rows_r[...], own_c, own_r[...])
    down, across = iota((count, count), 0), iota((count, count), 1)
    first_c = jnp.sum(jnp.where(across < down, rows_r[...], 0), axis=1, keepdims=True)
    token = iota((count, tok_rows), 1)
    inside = (token >= first_c) & (token < first_c + rows_c)
    target = jnp.sum(
        jnp.where(inside, own_c * cap + start_col - first_c + token, 0), axis=0, keepdims=True
    )
    chosen = (iota((slots, tok_rows), 0) == target).astype(F32).astype(BF16)
    loads[0].wait()
    away[...] = jnp.dot(chosen, tok_buf[...], preferred_element_type=F32).astype(BF16)
    arrived[cap_of(owner), :] = away[cap_of(owner), :]
    pl.semaphore_wait(barrier, readers - 1 + RING - 1 + RING)

    def send_turn(k, carry):
        turn(k).start()
        return carry

    lax.fori_loop(1, readers, send_turn, 0)

    ids_c = (iota((count, 1), 0) + 1).astype(F32)
    ids_r = (iota((1, count), 1) + 1).astype(F32)
    slot_r = iota((count, slots), 1)
    held_c = (
        (own_c == owner)
        & (slot_r >= readers * start_col)
        & (slot_r < readers * (start_col + rows_c))
    )
    ids_row = jnp.sum(jnp.where(held_c, ids_c, 0.0), axis=0, keepdims=True)
    for k in range(slots // SUB):
        seg_row[k] = jnp.broadcast_to(ids_row[:, k * SUB : (k + 1) * SUB], (8, SUB))
    slot_c = iota((slots, count), 0)
    held_r = (
        (own_r[...] == owner)
        & (slot_c >= readers * start_row)
        & (slot_c < readers * (start_row + rows_r[...]))
    )
    ids_col = jnp.sum(jnp.where(held_r, ids_r, 0.0), axis=1, keepdims=True)
    seg_col[...] = jnp.broadcast_to(ids_col, (slots, SUB))
    place, reader = slot_r % cap, slot_r // cap
    held = (own_c == owner) & (place >= start_col) & (place < start_col + rows_c)
    goal = jnp.sum(
        jnp.where(held, (readers - 1) * start_col + reader * rows_c + place + 1, 0),
        axis=0,
        keepdims=True,
    ) - 1
    state[...] = jnp.zeros_like(state)
    prev[...] = jnp.full(prev.shape, -1.0, F32)
    lane = iota((SUB, 128), 1)
    low = lane < HEADDIM

    def spread(value, pair):
        shape = (value.shape[0], 128)
        first = jnp.broadcast_to(value[:, 2 * pair : 2 * pair + 1], shape)
        second = jnp.broadcast_to(value[:, 2 * pair + 1 : 2 * pair + 2], shape)
        return jnp.where(iota(shape, 1) < HEADDIM, first, second)

    small[...] = jnp.zeros_like(small)
    for k, ref in enumerate((step_bias, decay_log, skip_gain)):
        small[k, 0:1, 0:heads] = ref[...]
    w_step[...] = jnp.concatenate(
        [step_t[...].astype(F32), jnp.zeros((128 - heads, step_t.shape[1]), F32)], axis=0
    ).astype(BF16)
    for pair in range(pairs):
        skip_row[:, pair * 128 : (pair + 1) * 128] = spread(
            jnp.broadcast_to(small[2, 0:1, :], (8, 128)), pair
        )
    rate = -jnp.exp(small[1, 0:1, :])

    loads[5].wait()

    def level_of(m):
        return (my_z + m + 2) % levels

    def turn_cot(m, carry):
        cols = pl.ds(pl.multiple_of(level_of(m) * block, block), block)
        cot_t[m] = cot[:, cols].T
        return carry

    lax.fori_loop(0, levels, turn_cot, 0)

    def take_turn(k, carry):
        turn(k).wait_recv()
        return carry

    lax.fori_loop(1, readers, take_turn, 0)
    for t in range(chunks):
        placed = (iota((ROWS, slots), 0) + t * ROWS == goal).astype(F32).astype(BF16)
        s_buf[t] = jnp.dot(placed, arrived[...], preferred_element_type=F32).astype(BF16)
        feed_side(t, 0).start()
        feed_side(t, 1).start()

        @pl.when(sec == 0)
        def _():
            feed_own(t).start()

        @pl.when(sec == 1)
        def _():
            feed_core(t).start()

    @pl.when(sec == 1)
    def _():
        def relay_step(t, carry):
            @pl.when(t < chunks)
            def _():
                sides(t, 0)

            @pl.when(t >= 1)
            def _():
                relayed(t - 1, 0)

            return carry

        lax.fori_loop(0, chunks + 1, relay_step, 0)

    for load in loads[1:5]:
        load.wait()

    def stage_in(t):
        pltpu.make_async_copy(u_buf.at[rows_of(t)], u_buf.at[rows_of(t)], hand_sem.at[t]).wait()
        rows_f = u_buf[rows_of(t), :].astype(F32)
        scale = lax.rsqrt(jnp.mean(rows_f * rows_f, axis=-1, keepdims=True) + EPS)
        normed[...] = (rows_f * scale * pre_gain[...]).astype(BF16)
        xs_buf[...] = silu(jnp.dot(normed[...], w_in[...], preferred_element_type=F32)).astype(BF16)
        bc_buf[...] = silu(jnp.dot(normed[...], w_state[...], preferred_element_type=F32)).astype(
            BF16
        )
        dt_buf[...] = softplus(
            lax.dot_general(
                normed[...], w_step[...], (((1,), (1,)), ((), ())), preferred_element_type=F32
            )
            + small[0, 0:1, :]
        )
        gate_buf[...] = silu(jnp.dot(normed[...], w_gate[...], preferred_element_type=F32))

    def stage_scan(t, sub):
        here = slice(sub * SUB, (sub + 1) * SUB)
        rows = pl.ds(pl.multiple_of(t * ROWS + sub * SUB, SUB), SUB)
        segment_c = seg_col[rows, :]
        segment_r = jnp.broadcast_to(seg_row[t * subs + sub][0:1, :], (SUB, SUB))
        before = jnp.broadcast_to(prev[0:1, :], (SUB, SUB))
        last = segment_c[SUB - 1 : SUB, :]
        down, across = iota((SUB, SUB), 0), iota((SUB, SUB), 1)
        causal = down >= across
        hidden = jnp.where(causal & (segment_c == segment_r), 0.0, -1e30)
        dt = dt_buf[here, :]
        cum = jnp.dot(
            causal.astype(F32),
            dt * rate,
            preferred_element_type=F32,
            precision=lax.Precision.HIGHEST,
        )
        cum_t, dt_t = cum.T, dt.T
        grown = jnp.exp(cum)
        from_before = jnp.where(segment_c == before, grown, 0.0)
        last_cum = cum[SUB - 1 : SUB, :]
        tail = jnp.where(segment_c == last, jnp.exp(last_cum - cum), 0.0) * dt
        kept = jnp.where(last == prev[0:1, :], jnp.exp(last_cum), 0.0)
        b_rows, c_rows = bc_buf[here, :NSTATE], bc_buf[here, NSTATE:]
        scores = lax.dot_general(
            c_rows, b_rows, (((1,), (1,)), ((), ())), preferred_element_type=F32
        )
        readout = jnp.dot(c_rows, state[...].astype(BF16), preferred_element_type=F32)
        squares = jnp.zeros((SUB, 128), F32)
        for pair in range(pairs):
            cols = slice(pair * 128, (pair + 1) * 128)
            x_pair = xs_buf[here, cols]
            x_f = x_pair.astype(F32)
            parts = []
            for head in (2 * pair, 2 * pair + 1):
                falling = jnp.minimum(cum[:, head : head + 1] - cum_t[head : head + 1, :], 0.0)
                weights = jnp.exp(falling + hidden) * scores * dt_t[head : head + 1, :]
                parts.append(jnp.dot(weights.astype(BF16), x_pair, preferred_element_type=F32))
            total = (
                jnp.where(low, parts[0], parts[1])
                + spread(from_before, pair) * readout[:, cols]
                + skip_row[0:1, cols] * x_f
            )
            gated = total * gate_buf[here, cols]
            squares = squares + gated * gated
            y_ref[rows, cols] = (gated * norm_gain[:, cols]).astype(BF16)
            scaled = (spread(tail, pair) * x_f).astype(BF16)
            fresh = lax.dot_general(
                b_rows, scaled, (((0,), (0,)), ((), ())), preferred_element_type=F32
            )
            state[:, cols] = spread(kept, pair) * state[:, cols] + fresh
        prev[...] = jnp.broadcast_to(last, prev.shape)
        sq_buf[0, t, sub] = jnp.broadcast_to(jnp.sum(squares.T, axis=0, keepdims=True), (8, SUB))

    def square_copy(t, k):
        return push(
            sq_buf.at[0, t],
            sq_buf.at[k, t],
            sq_send.at[k - 1, t],
            sq_recv.at[k - 1, t],
            tensor=(me + k) % RING,
        )

    def reduce_copy(t, k):
        who, which, dst, to = (
            (opposite, 0, lambda: a1.at[t], right),
            (opposite, 1, lambda: b1.at[t], left),
            (right, 1, lambda: a2.at[t, 1], right),
            (left, 0, lambda: b2.at[t, 0], left),
            (right, 0, lambda: a2.at[t, 0], right),
            (left, 1, lambda: b2.at[t, 1], left),
        )[k]
        return push(
            p_buf.at[t, piece_of(who, which)], dst(), rs_send.at[k, t], rs_recv.at[k, t], tensor=to
        )

    def gather_copy(t, k):
        who, which, to = (
            (me, 0, right),
            (me, 1, left),
            (me, 1, right),
            (me, 0, left),
            (left, 0, right),
            (right, 1, left),
        )[k]
        rows = o_buf.at[out_piece(t, who, which)]
        return push(rows, rows, ag_send.at[k, t], ag_recv.at[k, t], tensor=to)

    def stage_out(t):
        p_buf[t] = jnp.dot(y_ref[rows_of(t), :], w_out[...], preferred_element_type=F32).astype(
            BF16
        )
        for k in range(4):
            reduce_copy(t, k).start()

    def reduce_second(t):
        for k, who, which, got in ((0, right, 0, a1), (1, left, 1, b1)):
            reduce_copy(t, k).wait_recv()
            where = piece_of(who, which)
            p_buf[t, where, :] = (p_buf[t, where, :].astype(F32) + got[t].astype(F32)).astype(BF16)
            reduce_copy(t, k + 4).start()

    def reduce_last(t):
        for k in range(1, RING):
            square_copy(t, k).wait_recv()
        total = sq_buf[0, t] + sq_buf[1, t] + sq_buf[2, t] + sq_buf[3, t]
        scale = lax.rsqrt(total / (RING * inner) + EPS)
        for sub in range(subs):
            rows = pl.ds(pl.multiple_of(t * ROWS + sub * SUB, SUB), SUB)
            rs_ref[rows, :] = jnp.broadcast_to(scale[sub, 0:1, :], (SUB, SUB)).T
        yn_buf[rows_of(t), :] = (
            y_ref[rows_of(t), :].astype(F32) * rs_ref[rows_of(t), 0:1]
        ).astype(BF16)
        for k in range(2, 6):
            reduce_copy(t, k).wait_recv()
        for which in (0, 1):
            where = out_piece(t, me, which)
            summed = (
                p_buf[t, piece_of(me, which), :].astype(F32)
                + a2[t, which].astype(F32)
                + b2[t, which].astype(F32)
            )
            o_buf[where, :] = (
                u_buf[where, :].astype(F32) + rs_ref[where, 0:1] * summed
            ).astype(BF16)
        for k in range(4):
            gather_copy(t, k).start()
        pass_on(t, 0)

    def gather_second(t):
        for k in (0, 1):
            gather_copy(t, k).wait_recv()
            gather_copy(t, k + 4).start()
        for k in (2, 3):
            gather_copy(t, k).wait_recv()
        pass_on(t, 1, 2)

    def gather_last(t):
        gather_copy(t, 4).wait_recv()
        gather_copy(t, 5).wait_recv()
        pass_on(t, 3, 4)
        store_out(t).start()

    early = (chunks - 1) * ROWS

    def grad_early(m, carry):
        g_acc[m] = jnp.dot(cot_t[m, :, :early], yn_buf[:early, :], preferred_element_type=F32)
        return carry

    def grad_late(m, carry):
        term = g_acc[m] + jnp.dot(
            cot_t[m, :, early:], yn_buf[early:, :], preferred_element_type=F32
        )
        g_buf[m] = term.astype(BF16).reshape(RING, share, inner)
        return carry

    def grad_copy(g, k):
        base = g * group
        first, second = pl.ds(base, some), pl.ds(base + some, some)
        src, dst, to = (
            (lambda: g_buf.at[first, opposite_y], lambda: ga1.at[g], right_y),
            (lambda: g_buf.at[second, opposite_y], lambda: gb1.at[g], left_y),
            (lambda: g_buf.at[second, right_y], lambda: ga2.at[second], right_y),
            (lambda: g_buf.at[first, left_y], lambda: gb2.at[first], left_y),
            (lambda: g_buf.at[first, right_y], lambda: ga2.at[first], right_y),
            (lambda: g_buf.at[second, left_y], lambda: gb2.at[second], left_y),
        )[k]
        return push(src(), dst(), g_send.at[k, g], g_recv.at[k, g], dp=my_z * RING + to)

    def exchange(m):
        return push(
            h_buf.at[m],
            z_buf.at[m],
            z_send.at[m],
            z_recv.at[m],
            dp=level_of(m) * RING + my_y,
        )

    def grad_send(g):
        lax.fori_loop(g * group, (g + 1) * group, grad_late, 0)
        for k in range(4):
            grad_copy(g, k).start()

    def grad_second(g):
        for k, offset, who, got in ((0, 0, right_y, ga1), (1, some, left_y, gb1)):
            grad_copy(g, k).wait_recv()
            for j in range(some):
                m = g * group + offset + j
                g_buf[m, who] = (g_buf[m, who].astype(F32) + got[g, j].astype(F32)).astype(BF16)
            grad_copy(g, k + 4).start()

    def level_sum(m):
        return g_buf[m, my_y].astype(F32) + ga2[m].astype(F32) + gb2[m].astype(F32)

    def grad_finish(g):
        for k in range(2, 6):
            grad_copy(g, k).wait_recv()
        for m in range(g * group, (g + 1) * group):
            if m != levels - 2:
                h_buf[m] = level_sum(m).astype(BF16)
                exchange(m).start()

    def step(t, carry):
        @pl.when(t < chunks)
        def _():
            stage_in(t)
            for sub in range(subs):
                stage_scan(t, sub)
            for k in range(1, RING):
                square_copy(t, k).start()
            stage_out(t)

        @pl.when((t >= 1) & (t < chunks + 1))
        def _():
            reduce_second(t - 1)

        @pl.when((t >= 2) & (t < chunks + 2))
        def _():
            reduce_last(t - 2)

        @pl.when(t == chunks + 4 * (1 - sec))
        def _():
            lax.fori_loop(0, levels, grad_early, 0)

        @pl.when(t == chunks + 1 + 3 * (1 - sec))
        def _():
            grad_send(0)
            grad_send(1)

        @pl.when((t >= 3) & (t < chunks + 3))
        def _():
            gather_second(t - 3)

        @pl.when((t >= 4) & (t < chunks + 4))
        def _():
            gather_last(t - 4)

        return carry

    lax.fori_loop(0, chunks + 4 + (1 - sec), step, 0)
    grad_second(0)
    grad_second(1)
    grad_finish(0)
    grad_finish(1)
    total = level_sum(levels - 2)
    for m in range(levels):
        if m != levels - 2:
            exchange(m).wait_recv()
            total = total + z_buf[m].astype(F32)
    grad_ref[...] = total.astype(BF16)
    for g in (0, 1):
        for k in range(6):
            grad_copy(g, k).wait_send()
    for m in range(levels):
        if m != levels - 2:
            exchange(m).wait_send()

    def sent_turn(k, carry):
        turn(k).wait_send()
        return carry

    lax.fori_loop(1, readers, sent_turn, 0)

    def drain(t, carry):
        for k in range(6):
            reduce_copy(t, k).wait_send()
        for k in range(6):
            gather_copy(t, k).wait_send()
        for k in range(1, RING):
            square_copy(t, k).wait_send()
        feed_side(t, 0).wait_send()
        feed_side(t, 1).wait_send()

        @pl.when(sec == 0)
        def _():
            for k in range(5):
                hand_over(t, k).wait_send()

        @pl.when(sec == 1)
        def _():
            feed_core(t).wait_send()
            for k in (0, 1):
                relay(t, k).wait_send()
                fill(t, k, 0).wait_send()
                fill(t, k, 2).wait_send()

        store_out(t).wait()
        return carry

    lax.fori_loop(0, chunks, drain, 0)


def run_blocks(tables, tokens, cot, params):
    (
        pre_gain,
        input_proj,
        gate_proj,
        state_proj,
        step_proj,
        step_bias,
        decay_log,
        skip_gain,
        norm_gain,
        out_proj,
    ) = params
    readers = lax.axis_size("dp")
    tok_rows, width = tokens.shape
    slots = 2 * tok_rows
    inner = input_proj.shape[1]
    heads = step_proj.shape[1]
    chunks = slots // ROWS
    part = width // (2 * RING)
    share = width // readers
    levels = readers // RING
    some = levels // 4
    vmem = pl.BlockSpec(memory_space=pltpu.VMEM)
    anywhere = pl.BlockSpec(memory_space=pl.ANY)
    half = ROWS // RING // 2
    dma = pltpu.SemaphoreType.DMA
    return pl.pallas_call(
        functools.partial(block_kernel, chunks, heads, levels),
        name="blocks",
        out_shape=(
            pltpu.VMEM((slots, width), BF16),
            pltpu.VMEM((share, inner), BF16),
        ),
        in_specs=[vmem] * 8 + [anywhere] * 6,
        out_specs=(vmem, vmem),
        scratch_shapes=[
            pltpu.VMEM((width, inner), BF16),
            pltpu.VMEM((width, inner), BF16),
            pltpu.VMEM((width, 2 * NSTATE), BF16),
            pltpu.VMEM((128, width), BF16),
            pltpu.VMEM((inner, width), BF16),
            pltpu.VMEM((3, 8, 128), F32),
            pltpu.VMEM((tok_rows, part), BF16),
            pltpu.VMEM((slots, part), BF16),
            pltpu.VMEM((slots, part), BF16),
            pltpu.VMEM((chunks, ROWS, part), BF16),
            pltpu.VMEM((chunks, ROWS, width), BF16),
            pltpu.VMEM((slots, width), BF16),
            pltpu.VMEM((slots, width), BF16),
            pltpu.VMEM((chunks, ROWS, width), BF16),
            pltpu.VMEM((chunks, half, width), BF16),
            pltpu.VMEM((chunks, half, width), BF16),
            pltpu.VMEM((chunks, 2, half, width), BF16),
            pltpu.VMEM((chunks, 2, half, width), BF16),
            pltpu.VMEM((ROWS, width), BF16),
            pltpu.VMEM((ROWS, inner), BF16),
            pltpu.VMEM((ROWS, inner), F32),
            pltpu.VMEM((ROWS, 2 * NSTATE), BF16),
            pltpu.VMEM((ROWS, 128), F32),
            pltpu.VMEM((slots, inner), BF16),
            pltpu.VMEM((slots, inner), BF16),
            pltpu.VMEM((slots, 128), F32),
            pltpu.VMEM((NSTATE, inner), F32),
            pltpu.VMEM((8, 128), F32),
            pltpu.VMEM((slots, 128), F32),
            pltpu.VMEM((slots // SUB, 8, 128), F32),
            pltpu.VMEM((RING, chunks, ROWS // SUB, 8, 128), F32),
            pltpu.VMEM((8, inner), F32),
            pltpu.VMEM((slots, width), BF16),
            pltpu.VMEM((levels, RING * share, slots), BF16),
            pltpu.VMEM((levels, RING * share, inner), F32),
            pltpu.VMEM((levels, RING, share, inner), BF16),
            pltpu.VMEM((2, some, share, inner), BF16),
            pltpu.VMEM((2, some, share, inner), BF16),
            pltpu.VMEM((levels, share, inner), BF16),
            pltpu.VMEM((levels, share, inner), BF16),
            pltpu.VMEM((levels, share, inner), BF16),
            pltpu.VMEM((levels, share, inner), BF16),
            dma((6,)),
            dma((readers,)),
            dma((readers,)),
            dma((3, chunks)),
            dma((2, chunks)),
            dma((2, chunks)),
            dma((2, chunks)),
            dma((4, chunks)),
            dma((chunks,)),
            dma((5, chunks)),
            dma((chunks,)),
            dma((6, chunks)),
            dma((6, chunks)),
            dma((6, chunks)),
            dma((6, chunks)),
            dma((3, chunks)),
            dma((3, chunks)),
            dma((6, 2)),
            dma((6, 2)),
            dma((levels,)),
            dma((levels,)),
        ],
        compiler_params=pltpu.CompilerParams(
            collective_id=1, has_side_effects=True, vmem_limit_bytes=60 * 1024 * 1024
        ),
    )(
        *tables,
        pre_gain[None],
        step_bias[None],
        decay_log[None],
        skip_gain[None],
        norm_gain[None],
        step_proj.T,
        tokens,
        input_proj,
        gate_proj,
        state_proj,
        out_proj,
        cot,
    )


def per_device(
    tokens,
    base_rows,
    baseline_owner,
    cotangent,
    *params,
):
    tables = (base_rows[None, :], baseline_owner[None, :])
    result, grad = run_blocks(
        tables, tokens, cotangent[0], tuple(item[0] for item in params)
    )
    return (result[None], grad.T[None])


def solution(mesh):
    return jax.shard_map(
        per_device,
        mesh=mesh,
        in_specs=(
            P("dp", None),
            P(),
            P(),
            P("section", "dp", None),
            P("section", None),
            P("section", None, "tensor"),
            P("section", None, "tensor"),
            P("section", None, None),
            P("section", None, "tensor"),
            P("section", "tensor"),
            P("section", "tensor"),
            P("section", "tensor"),
            P("section", "tensor"),
            P("section", "tensor", None),
        ),
        out_specs=(P("section", "dp", None), P("section", "tensor", "dp")),
        check_vma=False,
    )
```

```python
import functools

import jax
import jax.numpy as jnp
from jax import lax
from jax.experimental import pallas as pl
from jax.experimental.pallas import tpu as pltpu
from jax.sharding import PartitionSpec as P

MESH = pl.DeviceIdType.MESH
HEADDIM = 64
NSTATE = 128
ROWS = 128
SUB = 128
RING = 4
EPS = 1e-05
F32 = jnp.float32
BF16 = jnp.bfloat16


def iota(shape, axis):
    return lax.broadcasted_iota(jnp.int32, shape, axis)


def silu(value):
    return value / (1.0 + jnp.exp(-value))


def softplus(value):
    return jnp.maximum(value, 0.0) + jnp.log1p(jnp.exp(-jnp.abs(value)))


def owner_starts(rows_c, rows_r, own_c, own_r):
    count = rows_r.shape[1]
    down, across = iota((count, count), 0), iota((count, count), 1)
    same = own_c == own_r
    row = jnp.sum(jnp.where(same & (down < across), rows_c, 0), axis=0, keepdims=True)
    col = jnp.sum(jnp.where(same & (across < down), rows_r, 0), axis=1, keepdims=True)
    return row, col


def block_kernel(
    chunks,
    heads,
    levels,
    rows_r,
    own_r,
    pre_gain,
    step_bias,
    decay_log,
    skip_gain,
    norm_gain,
    step_t,
    tokens,
    in_hbm,
    gate_hbm,
    state_hbm,
    out_hbm,
    cot_hbm,
    out_ref,
    grad_ref,
    w_in,
    w_gate,
    w_state,
    w_step,
    w_out,
    small,
    tok_buf,
    away,
    arrived,
    s_buf,
    u_buf,
    o_buf,
    p_buf,
    a1,
    b1,
    a2,
    b2,
    normed,
    xs_buf,
    gate_buf,
    bc_buf,
    dt_buf,
    y_ref,
    yn_buf,
    rs_ref,
    state,
    prev,
    seg_col,
    seg_row,
    sq_buf,
    skip_row,
    cot,
    cot_t,
    g_acc,
    g_buf,
    ga1,
    gb1,
    ga2,
    gb2,
    h_buf,
    z_buf,
    load_sem,
    turn_send,
    turn_recv,
    feed_send,
    hand_sem,
    hand_send,
    out_sem,
    rs_send,
    rs_recv,
    ag_send,
    ag_recv,
    sq_send,
    sq_recv,
    g_send,
    g_recv,
    z_send,
    z_recv,
):
    me = lax.axis_index("tensor")
    sec = lax.axis_index("section")
    owner = lax.axis_index("dp")
    right, left, opposite = ((me + 1) % RING, (me + 3) % RING, (me + 2) % RING)
    readers = lax.axis_size("dp")
    inner = w_in.shape[1]
    pairs = heads // 2
    piece = ROWS // RING
    half = piece // 2
    count = rows_r.shape[1]
    slots = chunks * ROWS
    subs = ROWS // SUB
    cap = slots // readers
    tok_rows, part = tok_buf.shape
    my_cols = pl.ds(pl.multiple_of((2 * me + sec) * part, part), part)
    my_z, my_y = owner // RING, owner % RING
    right_y, left_y, opposite_y = ((my_y + 1) % RING, (my_y + 3) % RING, (my_y + 2) % RING)
    share = g_buf.shape[2]
    block = RING * share
    group = levels // 2
    some = group // 2

    loads = [
        pltpu.make_async_copy(src, dst, load_sem.at[k])
        for k, (src, dst) in enumerate(
            (
                (tokens.at[:, my_cols], tok_buf),
                (in_hbm, w_in),
                (state_hbm, w_state),
                (gate_hbm, w_gate),
                (out_hbm, w_out),
                (cot_hbm, cot),
            )
        )
    ]
    for load in loads:
        load.start()

    barrier = pltpu.get_barrier_semaphore()

    def greet(k, carry):
        pl.semaphore_signal(
            barrier, inc=1, device_id={"dp": (owner + k) % readers}, device_id_type=MESH
        )
        return carry

    lax.fori_loop(1, readers, greet, 0)
    for k in range(RING):
        other = (me + k) % RING
        if k:
            pl.semaphore_signal(barrier, inc=1, device_id={"tensor": other}, device_id_type=MESH)
        pl.semaphore_signal(
            barrier,
            inc=1,
            device_id={"section": 1 - sec, "tensor": other},
            device_id_type=MESH,
        )

    def rows_of(t):
        return pl.ds(pl.multiple_of(t * ROWS, ROWS), ROWS)

    def piece_of(who, which=None):
        if which is None:
            return pl.ds(pl.multiple_of(who * piece, piece), piece)
        return pl.ds(pl.multiple_of(who * piece + which * half, half), half)

    def out_piece(t, who, which=None):
        if which is None:
            return pl.ds(pl.multiple_of(t * ROWS + who * piece, piece), piece)
        return pl.ds(pl.multiple_of(t * ROWS + who * piece + which * half, half), half)

    def cap_of(who):
        return pl.ds(pl.multiple_of(who * cap, cap), cap)

    def push(src, dst, send_sem, recv_sem, **where):
        return pltpu.make_async_remote_copy(
            src_ref=src,
            dst_ref=dst,
            send_sem=send_sem,
            recv_sem=recv_sem,
            device_id=where,
            device_id_type=MESH,
        )

    def turn(k):
        other = (owner + k) % readers
        return push(
            away.at[cap_of(other)],
            arrived.at[cap_of(owner)],
            turn_send.at[k],
            turn_recv.at[k],
            dp=other,
        )

    def feed_own(t):
        return pltpu.make_async_copy(s_buf.at[t], u_buf.at[rows_of(t), my_cols], hand_sem.at[t])

    def feed(t, k):
        return push(
            s_buf.at[t],
            u_buf.at[rows_of(t), my_cols],
            feed_send.at[k, t],
            hand_sem.at[t],
            section=0,
            tensor=(me + k) % RING,
        )

    def hand_over(t, k):
        where = (
            lambda: out_piece(t, me),
            lambda: out_piece(t, left),
            lambda: out_piece(t, right),
            lambda: out_piece(t, opposite, 0),
            lambda: out_piece(t, opposite, 1),
        )[k]()
        return push(
            o_buf.at[where], u_buf.at[where], hand_send.at[k, t], hand_sem.at[t], section=1 - sec
        )

    def pass_on(t, *which):
        @pl.when(sec == 0)
        def _():
            for k in which:
                hand_over(t, k).start()

    def store_out(t):
        return pltpu.make_async_copy(o_buf.at[rows_of(t)], out_ref.at[rows_of(t)], out_sem.at[t])

    def column(row):
        return jnp.broadcast_to(row.astype(F32), (count, count)).T[:, 0:1].astype(jnp.int32)

    rows_c, own_c = column(rows_r[...]), column(own_r[...])
    start_row, start_col = owner_starts(rows_c, rows_r[...], own_c, own_r[...])
    down, across = iota((count, count), 0), iota((count, count), 1)
    first_c = jnp.sum(jnp.where(across < down, rows_r[...], 0), axis=1, keepdims=True)
    token = iota((count, tok_rows), 1)
    inside = (token >= first_c) & (token < first_c + rows_c)
    target = jnp.sum(
        jnp.where(inside, own_c * cap + start_col - first_c + token, 0), axis=0, keepdims=True
    )
    chosen = (iota((slots, tok_rows), 0) == target).astype(F32).astype(BF16)
    loads[0].wait()
    away[...] = jnp.dot(chosen, tok_buf[...], preferred_element_type=F32).astype(BF16)
    arrived[cap_of(owner), :] = away[cap_of(owner), :]
    pl.semaphore_wait(barrier, readers - 1 + RING - 1 + RING)

    def send_turn(k, carry):
        turn(k).start()
        return carry

    lax.fori_loop(1, readers, send_turn, 0)

    ids_c = (iota((count, 1), 0) + 1).astype(F32)
    ids_r = (iota((1, count), 1) + 1).astype(F32)
    slot_r = iota((count, slots), 1)
    held_c = (
        (own_c == owner)
        & (slot_r >= readers * start_col)
        & (slot_r < readers * (start_col + rows_c))
    )
    ids_row = jnp.sum(jnp.where(held_c, ids_c, 0.0), axis=0, keepdims=True)
    for k in range(slots // SUB):
        seg_row[k] = jnp.broadcast_to(ids_row[:, k * SUB : (k + 1) * SUB], (8, SUB))
    slot_c = iota((slots, count), 0)
    held_r = (
        (own_r[...] == owner)
        & (slot_c >= readers * start_row)
        & (slot_c < readers * (start_row + rows_r[...]))
    )
    ids_col = jnp.sum(jnp.where(held_r, ids_r, 0.0), axis=1, keepdims=True)
    seg_col[...] = jnp.broadcast_to(ids_col, (slots, SUB))
    place, reader = slot_r % cap, slot_r // cap
    held = (own_c == owner) & (place >= start_col) & (place < start_col + rows_c)
    goal = jnp.sum(
        jnp.where(held, (readers - 1) * start_col + reader * rows_c + place + 1, 0),
        axis=0,
        keepdims=True,
    ) - 1
    state[...] = jnp.zeros_like(state)
    prev[...] = jnp.full(prev.shape, -1.0, F32)
    lane = iota((SUB, 128), 1)
    low = lane < HEADDIM

    def spread(value, pair):
        shape = (value.shape[0], 128)
        first = jnp.broadcast_to(value[:, 2 * pair : 2 * pair + 1], shape)
        second = jnp.broadcast_to(value[:, 2 * pair + 1 : 2 * pair + 2], shape)
        return jnp.where(iota(shape, 1) < HEADDIM, first, second)

    small[...] = jnp.zeros_like(small)
    for k, ref in enumerate((step_bias, decay_log, skip_gain)):
        small[k, 0:1, 0:heads] = ref[...]
    w_step[...] = jnp.concatenate(
        [step_t[...].astype(F32), jnp.zeros((128 - heads, step_t.shape[1]), F32)], axis=0
    ).astype(BF16)
    for pair in range(pairs):
        skip_row[:, pair * 128 : (pair + 1) * 128] = spread(
            jnp.broadcast_to(small[2, 0:1, :], (8, 128)), pair
        )
    rate = -jnp.exp(small[1, 0:1, :])

    loads[5].wait()

    def level_of(m):
        return (my_z + m + 2) % levels

    def turn_cot(m, carry):
        cols = pl.ds(pl.multiple_of(level_of(m) * block, block), block)
        cot_t[m] = cot[:, cols].T
        return carry

    lax.fori_loop(0, levels, turn_cot, 0)

    def take_turn(k, carry):
        turn(k).wait_recv()
        return carry

    lax.fori_loop(1, readers, take_turn, 0)
    for t in range(chunks):
        placed = (iota((ROWS, slots), 0) + t * ROWS == goal).astype(F32).astype(BF16)
        s_buf[t] = jnp.dot(placed, arrived[...], preferred_element_type=F32).astype(BF16)
        for k in (2, 1, 3):
            feed(t, k).start()

        @pl.when(sec == 0)
        def _():
            feed_own(t).start()

        @pl.when(sec == 1)
        def _():
            feed(t, 0).start()

    for load in loads[1:5]:
        load.wait()

    def stage_in(t):
        pltpu.make_async_copy(u_buf.at[rows_of(t)], u_buf.at[rows_of(t)], hand_sem.at[t]).wait()
        rows_f = u_buf[rows_of(t), :].astype(F32)
        scale = lax.rsqrt(jnp.mean(rows_f * rows_f, axis=-1, keepdims=True) + EPS)
        normed[...] = (rows_f * scale * pre_gain[...]).astype(BF16)
        xs_buf[...] = silu(jnp.dot(normed[...], w_in[...], preferred_element_type=F32)).astype(BF16)
        bc_buf[...] = silu(jnp.dot(normed[...], w_state[...], preferred_element_type=F32)).astype(
            BF16
        )
        dt_buf[...] = softplus(
            lax.dot_general(
                normed[...], w_step[...], (((1,), (1,)), ((), ())), preferred_element_type=F32
            )
            + small[0, 0:1, :]
        )
        gate_buf[...] = silu(jnp.dot(normed[...], w_gate[...], preferred_element_type=F32))

    def stage_scan(t, sub):
        here = slice(sub * SUB, (sub + 1) * SUB)
        rows = pl.ds(pl.multiple_of(t * ROWS + sub * SUB, SUB), SUB)
        segment_c = seg_col[rows, :]
        segment_r = jnp.broadcast_to(seg_row[t * subs + sub][0:1, :], (SUB, SUB))
        before = jnp.broadcast_to(prev[0:1, :], (SUB, SUB))
        last = segment_c[SUB - 1 : SUB, :]
        down, across = iota((SUB, SUB), 0), iota((SUB, SUB), 1)
        causal = down >= across
        hidden = jnp.where(causal & (segment_c == segment_r), 0.0, -1e30)
        dt = dt_buf[here, :]
        cum = jnp.dot(
            causal.astype(F32),
            dt * rate,
            preferred_element_type=F32,
            precision=lax.Precision.HIGHEST,
        )
        cum_t, dt_t = cum.T, dt.T
        grown = jnp.exp(cum)
        from_before = jnp.where(segment_c == before, grown, 0.0)
        last_cum = cum[SUB - 1 : SUB, :]
        tail = jnp.where(segment_c == last, jnp.exp(last_cum - cum), 0.0) * dt
        kept = jnp.where(last == prev[0:1, :], jnp.exp(last_cum), 0.0)
        b_rows, c_rows = bc_buf[here, :NSTATE], bc_buf[here, NSTATE:]
        scores = lax.dot_general(
            c_rows, b_rows, (((1,), (1,)), ((), ())), preferred_element_type=F32
        )
        readout = jnp.dot(c_rows, state[...].astype(BF16), preferred_element_type=F32)
        squares = jnp.zeros((SUB, 128), F32)
        for pair in range(pairs):
            cols = slice(pair * 128, (pair + 1) * 128)
            x_pair = xs_buf[here, cols]
            x_f = x_pair.astype(F32)
            parts = []
            for head in (2 * pair, 2 * pair + 1):
                falling = jnp.minimum(cum[:, head : head + 1] - cum_t[head : head + 1, :], 0.0)
                weights = jnp.exp(falling + hidden) * scores * dt_t[head : head + 1, :]
                parts.append(jnp.dot(weights.astype(BF16), x_pair, preferred_element_type=F32))
            total = (
                jnp.where(low, parts[0], parts[1])
                + spread(from_before, pair) * readout[:, cols]
                + skip_row[0:1, cols] * x_f
            )
            gated = total * gate_buf[here, cols]
            squares = squares + gated * gated
            y_ref[rows, cols] = (gated * norm_gain[:, cols]).astype(BF16)
            scaled = (spread(tail, pair) * x_f).astype(BF16)
            fresh = lax.dot_general(
                b_rows, scaled, (((0,), (0,)), ((), ())), preferred_element_type=F32
            )
            state[:, cols] = spread(kept, pair) * state[:, cols] + fresh
        prev[...] = jnp.broadcast_to(last, prev.shape)
        sq_buf[0, t, sub] = jnp.broadcast_to(jnp.sum(squares.T, axis=0, keepdims=True), (8, SUB))

    def square_copy(t, k):
        return push(
            sq_buf.at[0, t],
            sq_buf.at[k, t],
            sq_send.at[k - 1, t],
            sq_recv.at[k - 1, t],
            tensor=(me + k) % RING,
        )

    def reduce_copy(t, k):
        who, which, dst, to = (
            (opposite, 0, lambda: a1.at[t], right),
            (opposite, 1, lambda: b1.at[t], left),
            (right, 1, lambda: a2.at[t, 1], right),
            (left, 0, lambda: b2.at[t, 0], left),
            (right, 0, lambda: a2.at[t, 0], right),
            (left, 1, lambda: b2.at[t, 1], left),
        )[k]
        return push(
            p_buf.at[t, piece_of(who, which)], dst(), rs_send.at[k, t], rs_recv.at[k, t], tensor=to
        )

    def gather_copy(t, k):
        who, which, to = (
            (me, 0, right),
            (me, 1, left),
            (me, 1, right),
            (me, 0, left),
            (left, 0, right),
            (right, 1, left),
        )[k]
        rows = o_buf.at[out_piece(t, who, which)]
        return push(rows, rows, ag_send.at[k, t], ag_recv.at[k, t], tensor=to)

    def stage_out(t):
        p_buf[t] = jnp.dot(y_ref[rows_of(t), :], w_out[...], preferred_element_type=F32).astype(
            BF16
        )
        for k in range(4):
            reduce_copy(t, k).start()

    def reduce_second(t):
        for k, who, which, got in ((0, right, 0, a1), (1, left, 1, b1)):
            reduce_copy(t, k).wait_recv()
            where = piece_of(who, which)
            p_buf[t, where, :] = (p_buf[t, where, :].astype(F32) + got[t].astype(F32)).astype(BF16)
            reduce_copy(t, k + 4).start()

    def reduce_last(t):
        for k in range(1, RING):
            square_copy(t, k).wait_recv()
        total = sq_buf[0, t] + sq_buf[1, t] + sq_buf[2, t] + sq_buf[3, t]
        scale = lax.rsqrt(total / (RING * inner) + EPS)
        for sub in range(subs):
            rows = pl.ds(pl.multiple_of(t * ROWS + sub * SUB, SUB), SUB)
            rs_ref[rows, :] = jnp.broadcast_to(scale[sub, 0:1, :], (SUB, SUB)).T
        yn_buf[rows_of(t), :] = (
            y_ref[rows_of(t), :].astype(F32) * rs_ref[rows_of(t), 0:1]
        ).astype(BF16)
        for k in range(2, 6):
            reduce_copy(t, k).wait_recv()
        for which in (0, 1):
            where = out_piece(t, me, which)
            summed = (
                p_buf[t, piece_of(me, which), :].astype(F32)
                + a2[t, which].astype(F32)
                + b2[t, which].astype(F32)
            )
            o_buf[where, :] = (
                u_buf[where, :].astype(F32) + rs_ref[where, 0:1] * summed
            ).astype(BF16)
        for k in range(4):
            gather_copy(t, k).start()
        pass_on(t, 0)

    def gather_second(t):
        for k in (0, 1):
            gather_copy(t, k).wait_recv()
            gather_copy(t, k + 4).start()
        for k in (2, 3):
            gather_copy(t, k).wait_recv()
        pass_on(t, 1, 2)

    def gather_last(t):
        gather_copy(t, 4).wait_recv()
        gather_copy(t, 5).wait_recv()
        pass_on(t, 3, 4)
        store_out(t).start()

    early = (chunks - 1) * ROWS

    def grad_early(m, carry):
        g_acc[m] = jnp.dot(cot_t[m, :, :early], yn_buf[:early, :], preferred_element_type=F32)
        return carry

    def grad_late(m, carry):
        term = g_acc[m] + jnp.dot(
            cot_t[m, :, early:], yn_buf[early:, :], preferred_element_type=F32
        )
        g_buf[m] = term.astype(BF16).reshape(RING, share, inner)
        return carry

    def grad_copy(g, k):
        base = g * group
        first, second = pl.ds(base, some), pl.ds(base + some, some)
        src, dst, to = (
            (lambda: g_buf.at[first, opposite_y], lambda: ga1.at[g], right_y),
            (lambda: g_buf.at[second, opposite_y], lambda: gb1.at[g], left_y),
            (lambda: g_buf.at[second, right_y], lambda: ga2.at[second], right_y),
            (lambda: g_buf.at[first, left_y], lambda: gb2.at[first], left_y),
            (lambda: g_buf.at[first, right_y], lambda: ga2.at[first], right_y),
            (lambda: g_buf.at[second, left_y], lambda: gb2.at[second], left_y),
        )[k]
        return push(src(), dst(), g_send.at[k, g], g_recv.at[k, g], dp=my_z * RING + to)

    def exchange(m):
        return push(
            h_buf.at[m],
            z_buf.at[m],
            z_send.at[m],
            z_recv.at[m],
            dp=level_of(m) * RING + my_y,
        )

    def grad_send(g):
        lax.fori_loop(g * group, (g + 1) * group, grad_late, 0)
        for k in range(4):
            grad_copy(g, k).start()

    def grad_second(g):
        for k, offset, who, got in ((0, 0, right_y, ga1), (1, some, left_y, gb1)):
            grad_copy(g, k).wait_recv()
            for j in range(some):
                m = g * group + offset + j
                g_buf[m, who] = (g_buf[m, who].astype(F32) + got[g, j].astype(F32)).astype(BF16)
            grad_copy(g, k + 4).start()

    def level_sum(m):
        return g_buf[m, my_y].astype(F32) + ga2[m].astype(F32) + gb2[m].astype(F32)

    def grad_finish(g):
        for k in range(2, 6):
            grad_copy(g, k).wait_recv()
        for m in range(g * group, (g + 1) * group):
            if m != levels - 2:
                h_buf[m] = level_sum(m).astype(BF16)
                exchange(m).start()

    def step(t, carry):
        @pl.when(t < chunks)
        def _():
            stage_in(t)
            for sub in range(subs):
                stage_scan(t, sub)
            for k in range(1, RING):
                square_copy(t, k).start()
            stage_out(t)

        @pl.when((t >= 1) & (t < chunks + 1))
        def _():
            reduce_second(t - 1)

        @pl.when((t >= 2) & (t < chunks + 2))
        def _():
            reduce_last(t - 2)

        @pl.when(t == chunks + 4 * (1 - sec))
        def _():
            lax.fori_loop(0, levels, grad_early, 0)

        @pl.when(t == chunks + 1 + 3 * (1 - sec))
        def _():
            grad_send(0)
            grad_send(1)

        @pl.when((t >= 3) & (t < chunks + 3))
        def _():
            gather_second(t - 3)

        @pl.when((t >= 4) & (t < chunks + 4))
        def _():
            gather_last(t - 4)

        return carry

    lax.fori_loop(0, chunks + 4 + (1 - sec), step, 0)
    grad_second(0)
    grad_second(1)
    grad_finish(0)
    grad_finish(1)
    total = level_sum(levels - 2)
    for m in range(levels):
        if m != levels - 2:
            exchange(m).wait_recv()
            total = total + z_buf[m].astype(F32)
    grad_ref[...] = total.astype(BF16)
    for g in (0, 1):
        for k in range(6):
            grad_copy(g, k).wait_send()
    for m in range(levels):
        if m != levels - 2:
            exchange(m).wait_send()

    def sent_turn(k, carry):
        turn(k).wait_send()
        return carry

    lax.fori_loop(1, readers, sent_turn, 0)

    def drain(t, carry):
        for k in range(6):
            reduce_copy(t, k).wait_send()
        for k in range(6):
            gather_copy(t, k).wait_send()
        for k in range(1, RING):
            square_copy(t, k).wait_send()
            feed(t, k).wait_send()

        @pl.when(sec == 0)
        def _():
            for k in range(5):
                hand_over(t, k).wait_send()

        @pl.when(sec == 1)
        def _():
            feed(t, 0).wait_send()

        store_out(t).wait()
        return carry

    lax.fori_loop(0, chunks, drain, 0)


def run_blocks(tables, tokens, cot, params):
    (
        pre_gain,
        input_proj,
        gate_proj,
        state_proj,
        step_proj,
        step_bias,
        decay_log,
        skip_gain,
        norm_gain,
        out_proj,
    ) = params
    readers = lax.axis_size("dp")
    tok_rows, width = tokens.shape
    slots = 2 * tok_rows
    inner = input_proj.shape[1]
    heads = step_proj.shape[1]
    chunks = slots // ROWS
    part = width // (2 * RING)
    share = width // readers
    levels = readers // RING
    some = levels // 4
    vmem = pl.BlockSpec(memory_space=pltpu.VMEM)
    anywhere = pl.BlockSpec(memory_space=pl.ANY)
    half = ROWS // RING // 2
    dma = pltpu.SemaphoreType.DMA
    return pl.pallas_call(
        functools.partial(block_kernel, chunks, heads, levels),
        name="blocks",
        out_shape=(
            pltpu.VMEM((slots, width), BF16),
            pltpu.VMEM((share, inner), BF16),
        ),
        in_specs=[vmem] * 8 + [anywhere] * 6,
        out_specs=(vmem, vmem),
        scratch_shapes=[
            pltpu.VMEM((width, inner), BF16),
            pltpu.VMEM((width, inner), BF16),
            pltpu.VMEM((width, 2 * NSTATE), BF16),
            pltpu.VMEM((128, width), BF16),
            pltpu.VMEM((inner, width), BF16),
            pltpu.VMEM((3, 8, 128), F32),
            pltpu.VMEM((tok_rows, part), BF16),
            pltpu.VMEM((slots, part), BF16),
            pltpu.VMEM((slots, part), BF16),
            pltpu.VMEM((chunks, ROWS, part), BF16),
            pltpu.VMEM((slots, width), BF16),
            pltpu.VMEM((slots, width), BF16),
            pltpu.VMEM((chunks, ROWS, width), BF16),
            pltpu.VMEM((chunks, half, width), BF16),
            pltpu.VMEM((chunks, half, width), BF16),
            pltpu.VMEM((chunks, 2, half, width), BF16),
            pltpu.VMEM((chunks, 2, half, width), BF16),
            pltpu.VMEM((ROWS, width), BF16),
            pltpu.VMEM((ROWS, inner), BF16),
            pltpu.VMEM((ROWS, inner), F32),
            pltpu.VMEM((ROWS, 2 * NSTATE), BF16),
            pltpu.VMEM((ROWS, 128), F32),
            pltpu.VMEM((slots, inner), BF16),
            pltpu.VMEM((slots, inner), BF16),
            pltpu.VMEM((slots, 128), F32),
            pltpu.VMEM((NSTATE, inner), F32),
            pltpu.VMEM((8, 128), F32),
            pltpu.VMEM((slots, 128), F32),
            pltpu.VMEM((slots // SUB, 8, 128), F32),
            pltpu.VMEM((RING, chunks, ROWS // SUB, 8, 128), F32),
            pltpu.VMEM((8, inner), F32),
            pltpu.VMEM((slots, width), BF16),
            pltpu.VMEM((levels, RING * share, slots), BF16),
            pltpu.VMEM((levels, RING * share, inner), F32),
            pltpu.VMEM((levels, RING, share, inner), BF16),
            pltpu.VMEM((2, some, share, inner), BF16),
            pltpu.VMEM((2, some, share, inner), BF16),
            pltpu.VMEM((levels, share, inner), BF16),
            pltpu.VMEM((levels, share, inner), BF16),
            pltpu.VMEM((levels, share, inner), BF16),
            pltpu.VMEM((levels, share, inner), BF16),
            dma((6,)),
            dma((readers,)),
            dma((readers,)),
            dma((RING, chunks)),
            dma((chunks,)),
            dma((5, chunks)),
            dma((chunks,)),
            dma((6, chunks)),
            dma((6, chunks)),
            dma((6, chunks)),
            dma((6, chunks)),
            dma((3, chunks)),
            dma((3, chunks)),
            dma((6, 2)),
            dma((6, 2)),
            dma((levels,)),
            dma((levels,)),
        ],
        compiler_params=pltpu.CompilerParams(
            collective_id=1, has_side_effects=True, vmem_limit_bytes=60 * 1024 * 1024
        ),
    )(
        *tables,
        pre_gain[None],
        step_bias[None],
        decay_log[None],
        skip_gain[None],
        norm_gain[None],
        step_proj.T,
        tokens,
        input_proj,
        gate_proj,
        state_proj,
        out_proj,
        cot,
    )


def per_device(
    tokens,
    base_rows,
    baseline_owner,
    cotangent,
    *params,
):
    tables = (base_rows[None, :], baseline_owner[None, :])
    result, grad = run_blocks(
        tables, tokens, cotangent[0], tuple(item[0] for item in params)
    )
    return (result[None], grad.T[None])


def solution(mesh):
    return jax.shard_map(
        per_device,
        mesh=mesh,
        in_specs=(
            P("dp", None),
            P(),
            P(),
            P("section", "dp", None),
            P("section", None),
            P("section", None, "tensor"),
            P("section", None, "tensor"),
            P("section", None, None),
            P("section", None, "tensor"),
            P("section", "tensor"),
            P("section", "tensor"),
            P("section", "tensor"),
            P("section", "tensor"),
            P("section", "tensor", None),
        ),
        out_specs=(P("section", "dp", None), P("section", "tensor", "dp")),
        check_vma=False,
    )
```

```python
import functools

import jax
import jax.numpy as jnp
from jax import lax
from jax.experimental import pallas as pl
from jax.experimental.pallas import tpu as pltpu
from jax.sharding import PartitionSpec as P

MESH = pl.DeviceIdType.MESH
HEADDIM = 64
NSTATE = 128
ROWS = 128
SUB = 128
RING = 4
EPS = 1e-05
F32 = jnp.float32
BF16 = jnp.bfloat16


def iota(shape, axis):
    return lax.broadcasted_iota(jnp.int32, shape, axis)


def silu(value):
    return value / (1.0 + jnp.exp(-value))


def softplus(value):
    return jnp.maximum(value, 0.0) + jnp.log1p(jnp.exp(-jnp.abs(value)))


def owner_starts(rows_c, rows_r, own_c, own_r):
    count = rows_r.shape[1]
    down, across = iota((count, count), 0), iota((count, count), 1)
    same = own_c == own_r
    row = jnp.sum(jnp.where(same & (down < across), rows_c, 0), axis=0, keepdims=True)
    col = jnp.sum(jnp.where(same & (across < down), rows_r, 0), axis=1, keepdims=True)
    return row, col


def block_kernel(
    chunks,
    heads,
    levels,
    rows_r,
    own_r,
    pre_gain,
    step_bias,
    decay_log,
    skip_gain,
    norm_gain,
    step_t,
    tokens,
    in_hbm,
    gate_hbm,
    state_hbm,
    out_hbm,
    cot_hbm,
    out_ref,
    grad_ref,
    w_in,
    w_gate,
    w_state,
    w_step,
    w_out,
    small,
    tok_buf,
    away,
    arrived,
    s_buf,
    u_buf,
    o_buf,
    p_buf,
    a1,
    b1,
    a2,
    b2,
    normed,
    xs_buf,
    gate_buf,
    bc_buf,
    dt_buf,
    y_ref,
    yn_buf,
    rs_ref,
    state,
    prev,
    seg_col,
    seg_row,
    sq_buf,
    skip_row,
    cot,
    cot_t,
    g_acc,
    g_buf,
    ga1,
    gb1,
    ga2,
    gb2,
    h_buf,
    z_buf,
    load_sem,
    turn_send,
    turn_recv,
    feed_send,
    hand_sem,
    hand_send,
    out_sem,
    rs_send,
    rs_recv,
    ag_send,
    ag_recv,
    sq_send,
    sq_recv,
    g_send,
    g_recv,
    z_send,
    z_recv,
):
    me = lax.axis_index("tensor")
    sec = lax.axis_index("section")
    owner = lax.axis_index("dp")
    right, left, opposite = ((me + 1) % RING, (me + 3) % RING, (me + 2) % RING)
    readers = lax.axis_size("dp")
    inner = w_in.shape[1]
    pairs = heads // 2
    piece = ROWS // RING
    half = piece // 2
    count = rows_r.shape[1]
    slots = chunks * ROWS
    subs = ROWS // SUB
    cap = slots // readers
    tok_rows, part = tok_buf.shape
    my_cols = pl.ds(pl.multiple_of((2 * me + sec) * part, part), part)
    my_z, my_y = owner // RING, owner % RING
    right_y, left_y, opposite_y = ((my_y + 1) % RING, (my_y + 3) % RING, (my_y + 2) % RING)
    share = g_buf.shape[2]
    block = RING * share
    group = levels // 2
    some = group // 2

    loads = [
        pltpu.make_async_copy(src, dst, load_sem.at[k])
        for k, (src, dst) in enumerate(
            (
                (tokens.at[:, my_cols], tok_buf),
                (in_hbm, w_in),
                (state_hbm, w_state),
                (gate_hbm, w_gate),
                (out_hbm, w_out),
                (cot_hbm, cot),
            )
        )
    ]
    loads[0].start()

    barrier = pltpu.get_barrier_semaphore()

    def greet(k, carry):
        pl.semaphore_signal(
            barrier, inc=1, device_id={"dp": (owner + k) % readers}, device_id_type=MESH
        )
        return carry

    lax.fori_loop(1, readers, greet, 0)
    for k in range(RING):
        other = (me + k) % RING
        if k:
            pl.semaphore_signal(barrier, inc=1, device_id={"tensor": other}, device_id_type=MESH)
        pl.semaphore_signal(
            barrier,
            inc=1,
            device_id={"section": 1 - sec, "tensor": other},
            device_id_type=MESH,
        )

    def rows_of(t):
        return pl.ds(pl.multiple_of(t * ROWS, ROWS), ROWS)

    def piece_of(who, which=None):
        if which is None:
            return pl.ds(pl.multiple_of(who * piece, piece), piece)
        return pl.ds(pl.multiple_of(who * piece + which * half, half), half)

    def out_piece(t, who, which=None):
        if which is None:
            return pl.ds(pl.multiple_of(t * ROWS + who * piece, piece), piece)
        return pl.ds(pl.multiple_of(t * ROWS + who * piece + which * half, half), half)

    def cap_of(who):
        return pl.ds(pl.multiple_of(who * cap, cap), cap)

    def push(src, dst, send_sem, recv_sem, **where):
        return pltpu.make_async_remote_copy(
            src_ref=src,
            dst_ref=dst,
            send_sem=send_sem,
            recv_sem=recv_sem,
            device_id=where,
            device_id_type=MESH,
        )

    def turn(k):
        other = (owner + k) % readers
        return push(
            away.at[cap_of(other)],
            arrived.at[cap_of(owner)],
            turn_send.at[k],
            turn_recv.at[k],
            dp=other,
        )

    def feed_own(t):
        return pltpu.make_async_copy(s_buf.at[t], u_buf.at[rows_of(t), my_cols], hand_sem.at[t])

    def feed(t, k):
        return push(
            s_buf.at[t],
            u_buf.at[rows_of(t), my_cols],
            feed_send.at[k, t],
            hand_sem.at[t],
            section=0,
            tensor=(me + k) % RING,
        )

    def hand_over(t, k):
        where = (
            lambda: out_piece(t, me),
            lambda: out_piece(t, left),
            lambda: out_piece(t, right),
            lambda: out_piece(t, opposite, 0),
            lambda: out_piece(t, opposite, 1),
        )[k]()
        return push(
            o_buf.at[where], u_buf.at[where], hand_send.at[k, t], hand_sem.at[t], section=1 - sec
        )

    def pass_on(t, *which):
        @pl.when(sec == 0)
        def _():
            for k in which:
                hand_over(t, k).start()

    def store_out(t):
        return pltpu.make_async_copy(o_buf.at[rows_of(t)], out_ref.at[rows_of(t)], out_sem.at[t])

    def column(row):
        return jnp.broadcast_to(row.astype(F32), (count, count)).T[:, 0:1].astype(jnp.int32)

    rows_c, own_c = column(rows_r[...]), column(own_r[...])
    start_row, start_col = owner_starts(rows_c, rows_r[...], own_c, own_r[...])
    down, across = iota((count, count), 0), iota((count, count), 1)
    first_c = jnp.sum(jnp.where(across < down, rows_r[...], 0), axis=1, keepdims=True)
    token = iota((count, tok_rows), 1)
    inside = (token >= first_c) & (token < first_c + rows_c)
    target = jnp.sum(
        jnp.where(inside, own_c * cap + start_col - first_c + token, 0), axis=0, keepdims=True
    )
    chosen = (iota((slots, tok_rows), 0) == target).astype(F32).astype(BF16)
    loads[0].wait()
    for load in loads[1:]:
        load.start()
    away[...] = jnp.dot(chosen, tok_buf[...], preferred_element_type=F32).astype(BF16)
    arrived[cap_of(owner), :] = away[cap_of(owner), :]
    pl.semaphore_wait(barrier, readers - 1 + RING - 1 + RING)

    def send_turn(k, carry):
        far = (k + readers // 2) % readers

        @pl.when(far != 0)
        def _():
            turn(far).start()

        return carry

    lax.fori_loop(0, readers, send_turn, 0)

    ids_c = (iota((count, 1), 0) + 1).astype(F32)
    ids_r = (iota((1, count), 1) + 1).astype(F32)
    slot_r = iota((count, slots), 1)
    held_c = (
        (own_c == owner)
        & (slot_r >= readers * start_col)
        & (slot_r < readers * (start_col + rows_c))
    )
    ids_row = jnp.sum(jnp.where(held_c, ids_c, 0.0), axis=0, keepdims=True)
    for k in range(slots // SUB):
        seg_row[k] = jnp.broadcast_to(ids_row[:, k * SUB : (k + 1) * SUB], (8, SUB))
    slot_c = iota((slots, count), 0)
    held_r = (
        (own_r[...] == owner)
        & (slot_c >= readers * start_row)
        & (slot_c < readers * (start_row + rows_r[...]))
    )
    ids_col = jnp.sum(jnp.where(held_r, ids_r, 0.0), axis=1, keepdims=True)
    seg_col[...] = jnp.broadcast_to(ids_col, (slots, SUB))
    place, reader = slot_r % cap, slot_r // cap
    held = (own_c == owner) & (place >= start_col) & (place < start_col + rows_c)
    goal = jnp.sum(
        jnp.where(held, (readers - 1) * start_col + reader * rows_c + place + 1, 0),
        axis=0,
        keepdims=True,
    ) - 1
    state[...] = jnp.zeros_like(state)
    prev[...] = jnp.full(prev.shape, -1.0, F32)
    lane = iota((SUB, 128), 1)
    low = lane < HEADDIM

    def spread(value, pair):
        shape = (value.shape[0], 128)
        first = jnp.broadcast_to(value[:, 2 * pair : 2 * pair + 1], shape)
        second = jnp.broadcast_to(value[:, 2 * pair + 1 : 2 * pair + 2], shape)
        return jnp.where(iota(shape, 1) < HEADDIM, first, second)

    small[...] = jnp.zeros_like(small)
    for k, ref in enumerate((step_bias, decay_log, skip_gain)):
        small[k, 0:1, 0:heads] = ref[...]
    w_step[...] = jnp.concatenate(
        [step_t[...].astype(F32), jnp.zeros((128 - heads, step_t.shape[1]), F32)], axis=0
    ).astype(BF16)
    for pair in range(pairs):
        skip_row[:, pair * 128 : (pair + 1) * 128] = spread(
            jnp.broadcast_to(small[2, 0:1, :], (8, 128)), pair
        )
    rate = -jnp.exp(small[1, 0:1, :])

    loads[5].wait()

    def level_of(m):
        return (my_z + m + 2) % levels

    def turn_cot(m, carry):
        cols = pl.ds(pl.multiple_of(level_of(m) * block, block), block)
        cot_t[m] = cot[:, cols].T
        return carry

    lax.fori_loop(0, levels, turn_cot, 0)

    def take_turn(k, carry):
        turn(k).wait_recv()
        return carry

    lax.fori_loop(1, readers, take_turn, 0)
    for t in range(chunks):
        placed = (iota((ROWS, slots), 0) + t * ROWS == goal).astype(F32).astype(BF16)
        s_buf[t] = jnp.dot(placed, arrived[...], preferred_element_type=F32).astype(BF16)
        for k in (2, 1, 3):
            feed(t, k).start()

        @pl.when(sec == 0)
        def _():
            feed_own(t).start()

        @pl.when(sec == 1)
        def _():
            feed(t, 0).start()

    for load in loads[1:5]:
        load.wait()

    def stage_in(t):
        pltpu.make_async_copy(u_buf.at[rows_of(t)], u_buf.at[rows_of(t)], hand_sem.at[t]).wait()
        rows_f = u_buf[rows_of(t), :].astype(F32)
        scale = lax.rsqrt(jnp.mean(rows_f * rows_f, axis=-1, keepdims=True) + EPS)
        normed[...] = (rows_f * scale * pre_gain[...]).astype(BF16)
        xs_buf[...] = silu(jnp.dot(normed[...], w_in[...], preferred_element_type=F32)).astype(BF16)
        bc_buf[...] = silu(jnp.dot(normed[...], w_state[...], preferred_element_type=F32)).astype(
            BF16
        )
        dt_buf[...] = softplus(
            lax.dot_general(
                normed[...], w_step[...], (((1,), (1,)), ((), ())), preferred_element_type=F32
            )
            + small[0, 0:1, :]
        )
        gate_buf[...] = silu(jnp.dot(normed[...], w_gate[...], preferred_element_type=F32))

    def stage_scan(t, sub):
        here = slice(sub * SUB, (sub + 1) * SUB)
        rows = pl.ds(pl.multiple_of(t * ROWS + sub * SUB, SUB), SUB)
        segment_c = seg_col[rows, :]
        segment_r = jnp.broadcast_to(seg_row[t * subs + sub][0:1, :], (SUB, SUB))
        before = jnp.broadcast_to(prev[0:1, :], (SUB, SUB))
        last = segment_c[SUB - 1 : SUB, :]
        down, across = iota((SUB, SUB), 0), iota((SUB, SUB), 1)
        causal = down >= across
        hidden = jnp.where(causal & (segment_c == segment_r), 0.0, -1e30)
        dt = dt_buf[here, :]
        cum = jnp.dot(
            causal.astype(F32),
            dt * rate,
            preferred_element_type=F32,
            precision=lax.Precision.HIGHEST,
        )
        cum_t, dt_t = cum.T, dt.T
        grown = jnp.exp(cum)
        from_before = jnp.where(segment_c == before, grown, 0.0)
        last_cum = cum[SUB - 1 : SUB, :]
        tail = jnp.where(segment_c == last, jnp.exp(last_cum - cum), 0.0) * dt
        kept = jnp.where(last == prev[0:1, :], jnp.exp(last_cum), 0.0)
        b_rows, c_rows = bc_buf[here, :NSTATE], bc_buf[here, NSTATE:]
        scores = lax.dot_general(
            c_rows, b_rows, (((1,), (1,)), ((), ())), preferred_element_type=F32
        )
        readout = jnp.dot(c_rows, state[...].astype(BF16), preferred_element_type=F32)
        squares = jnp.zeros((SUB, 128), F32)
        for pair in range(pairs):
            cols = slice(pair * 128, (pair + 1) * 128)
            x_pair = xs_buf[here, cols]
            x_f = x_pair.astype(F32)
            parts = []
            for head in (2 * pair, 2 * pair + 1):
                falling = jnp.minimum(cum[:, head : head + 1] - cum_t[head : head + 1, :], 0.0)
                weights = jnp.exp(falling + hidden) * scores * dt_t[head : head + 1, :]
                parts.append(jnp.dot(weights.astype(BF16), x_pair, preferred_element_type=F32))
            total = (
                jnp.where(low, parts[0], parts[1])
                + spread(from_before, pair) * readout[:, cols]
                + skip_row[0:1, cols] * x_f
            )
            gated = total * gate_buf[here, cols]
            squares = squares + gated * gated
            y_ref[rows, cols] = (gated * norm_gain[:, cols]).astype(BF16)
            scaled = (spread(tail, pair) * x_f).astype(BF16)
            fresh = lax.dot_general(
                b_rows, scaled, (((0,), (0,)), ((), ())), preferred_element_type=F32
            )
            state[:, cols] = spread(kept, pair) * state[:, cols] + fresh
        prev[...] = jnp.broadcast_to(last, prev.shape)
        sq_buf[0, t, sub] = jnp.broadcast_to(jnp.sum(squares.T, axis=0, keepdims=True), (8, SUB))

    def square_copy(t, k):
        return push(
            sq_buf.at[0, t],
            sq_buf.at[k, t],
            sq_send.at[k - 1, t],
            sq_recv.at[k - 1, t],
            tensor=(me + k) % RING,
        )

    def reduce_copy(t, k):
        who, which, dst, to = (
            (opposite, 0, lambda: a1.at[t], right),
            (opposite, 1, lambda: b1.at[t], left),
            (right, 1, lambda: a2.at[t, 1], right),
            (left, 0, lambda: b2.at[t, 0], left),
            (right, 0, lambda: a2.at[t, 0], right),
            (left, 1, lambda: b2.at[t, 1], left),
        )[k]
        return push(
            p_buf.at[t, piece_of(who, which)], dst(), rs_send.at[k, t], rs_recv.at[k, t], tensor=to
        )

    def gather_copy(t, k):
        who, which, to = (
            (me, 0, right),
            (me, 1, left),
            (me, 1, right),
            (me, 0, left),
            (left, 0, right),
            (right, 1, left),
        )[k]
        rows = o_buf.at[out_piece(t, who, which)]
        return push(rows, rows, ag_send.at[k, t], ag_recv.at[k, t], tensor=to)

    def stage_out(t):
        p_buf[t] = jnp.dot(y_ref[rows_of(t), :], w_out[...], preferred_element_type=F32).astype(
            BF16
        )
        for k in range(4):
            reduce_copy(t, k).start()

    def reduce_second(t):
        for k, who, which, got in ((0, right, 0, a1), (1, left, 1, b1)):
            reduce_copy(t, k).wait_recv()
            where = piece_of(who, which)
            p_buf[t, where, :] = (p_buf[t, where, :].astype(F32) + got[t].astype(F32)).astype(BF16)
            reduce_copy(t, k + 4).start()

    def reduce_last(t):
        for k in range(1, RING):
            square_copy(t, k).wait_recv()
        total = sq_buf[0, t] + sq_buf[1, t] + sq_buf[2, t] + sq_buf[3, t]
        scale = lax.rsqrt(total / (RING * inner) + EPS)
        for sub in range(subs):
            rows = pl.ds(pl.multiple_of(t * ROWS + sub * SUB, SUB), SUB)
            rs_ref[rows, :] = jnp.broadcast_to(scale[sub, 0:1, :], (SUB, SUB)).T
        yn_buf[rows_of(t), :] = (
            y_ref[rows_of(t), :].astype(F32) * rs_ref[rows_of(t), 0:1]
        ).astype(BF16)
        for k in range(2, 6):
            reduce_copy(t, k).wait_recv()
        for which in (0, 1):
            where = out_piece(t, me, which)
            summed = (
                p_buf[t, piece_of(me, which), :].astype(F32)
                + a2[t, which].astype(F32)
                + b2[t, which].astype(F32)
            )
            o_buf[where, :] = (
                u_buf[where, :].astype(F32) + rs_ref[where, 0:1] * summed
            ).astype(BF16)
        for k in range(4):
            gather_copy(t, k).start()
        pass_on(t, 0)

    def gather_second(t):
        for k in (0, 1):
            gather_copy(t, k).wait_recv()
            gather_copy(t, k + 4).start()
        for k in (2, 3):
            gather_copy(t, k).wait_recv()
        pass_on(t, 1, 2)

    def gather_last(t):
        gather_copy(t, 4).wait_recv()
        gather_copy(t, 5).wait_recv()
        pass_on(t, 3, 4)
        store_out(t).start()

    early = (chunks - 1) * ROWS

    def grad_early(m, carry):
        g_acc[m] = jnp.dot(cot_t[m, :, :early], yn_buf[:early, :], preferred_element_type=F32)
        return carry

    def grad_late(m, carry):
        term = g_acc[m] + jnp.dot(
            cot_t[m, :, early:], yn_buf[early:, :], preferred_element_type=F32
        )
        g_buf[m] = term.astype(BF16).reshape(RING, share, inner)
        return carry

    def grad_copy(g, k):
        base = g * group
        first, second = pl.ds(base, some), pl.ds(base + some, some)
        src, dst, to = (
            (lambda: g_buf.at[first, opposite_y], lambda: ga1.at[g], right_y),
            (lambda: g_buf.at[second, opposite_y], lambda: gb1.at[g], left_y),
            (lambda: g_buf.at[second, right_y], lambda: ga2.at[second], right_y),
            (lambda: g_buf.at[first, left_y], lambda: gb2.at[first], left_y),
            (lambda: g_buf.at[first, right_y], lambda: ga2.at[first], right_y),
            (lambda: g_buf.at[second, left_y], lambda: gb2.at[second], left_y),
        )[k]
        return push(src(), dst(), g_send.at[k, g], g_recv.at[k, g], dp=my_z * RING + to)

    def exchange(m):
        return push(
            h_buf.at[m],
            z_buf.at[m],
            z_send.at[m],
            z_recv.at[m],
            dp=level_of(m) * RING + my_y,
        )

    def grad_send(g):
        lax.fori_loop(g * group, (g + 1) * group, grad_late, 0)
        for k in range(4):
            grad_copy(g, k).start()

    def grad_second(g):
        for k, offset, who, got in ((0, 0, right_y, ga1), (1, some, left_y, gb1)):
            grad_copy(g, k).wait_recv()
            for j in range(some):
                m = g * group + offset + j
                g_buf[m, who] = (g_buf[m, who].astype(F32) + got[g, j].astype(F32)).astype(BF16)
            grad_copy(g, k + 4).start()

    def level_sum(m):
        return g_buf[m, my_y].astype(F32) + ga2[m].astype(F32) + gb2[m].astype(F32)

    def grad_finish(g):
        for k in range(2, 6):
            grad_copy(g, k).wait_recv()
        for m in range(g * group, (g + 1) * group):
            if m != levels - 2:
                h_buf[m] = level_sum(m).astype(BF16)
                exchange(m).start()

    def step(t, carry):
        @pl.when(t < chunks)
        def _():
            stage_in(t)
            for sub in range(subs):
                stage_scan(t, sub)
            for k in range(1, RING):
                square_copy(t, k).start()
            stage_out(t)

        @pl.when((t >= 1) & (t < chunks + 1))
        def _():
            reduce_second(t - 1)

        @pl.when((t >= 2) & (t < chunks + 2))
        def _():
            reduce_last(t - 2)

        @pl.when(t == chunks + 4 * (1 - sec))
        def _():
            lax.fori_loop(0, levels, grad_early, 0)

        @pl.when(t == chunks + 1 + 3 * (1 - sec))
        def _():
            grad_send(0)
            grad_send(1)

        @pl.when((t >= 3) & (t < chunks + 3))
        def _():
            gather_second(t - 3)

        @pl.when((t >= 4) & (t < chunks + 4))
        def _():
            gather_last(t - 4)

        return carry

    lax.fori_loop(0, chunks + 4 + (1 - sec), step, 0)
    grad_second(0)
    grad_second(1)
    grad_finish(0)
    grad_finish(1)
    total = level_sum(levels - 2)
    for m in range(levels):
        if m != levels - 2:
            exchange(m).wait_recv()
            total = total + z_buf[m].astype(F32)
    grad_ref[...] = total.astype(BF16)
    for g in (0, 1):
        for k in range(6):
            grad_copy(g, k).wait_send()
    for m in range(levels):
        if m != levels - 2:
            exchange(m).wait_send()

    def sent_turn(k, carry):
        turn(k).wait_send()
        return carry

    lax.fori_loop(1, readers, sent_turn, 0)

    def drain(t, carry):
        for k in range(6):
            reduce_copy(t, k).wait_send()
        for k in range(6):
            gather_copy(t, k).wait_send()
        for k in range(1, RING):
            square_copy(t, k).wait_send()
            feed(t, k).wait_send()

        @pl.when(sec == 0)
        def _():
            for k in range(5):
                hand_over(t, k).wait_send()

        @pl.when(sec == 1)
        def _():
            feed(t, 0).wait_send()

        store_out(t).wait()
        return carry

    lax.fori_loop(0, chunks, drain, 0)


def run_blocks(tables, tokens, cot, params):
    (
        pre_gain,
        input_proj,
        gate_proj,
        state_proj,
        step_proj,
        step_bias,
        decay_log,
        skip_gain,
        norm_gain,
        out_proj,
    ) = params
    readers = lax.axis_size("dp")
    tok_rows, width = tokens.shape
    slots = 2 * tok_rows
    inner = input_proj.shape[1]
    heads = step_proj.shape[1]
    chunks = slots // ROWS
    part = width // (2 * RING)
    share = width // readers
    levels = readers // RING
    some = levels // 4
    vmem = pl.BlockSpec(memory_space=pltpu.VMEM)
    anywhere = pl.BlockSpec(memory_space=pl.ANY)
    half = ROWS // RING // 2
    dma = pltpu.SemaphoreType.DMA
    return pl.pallas_call(
        functools.partial(block_kernel, chunks, heads, levels),
        name="blocks",
        out_shape=(
            pltpu.VMEM((slots, width), BF16),
            pltpu.VMEM((share, inner), BF16),
        ),
        in_specs=[vmem] * 8 + [anywhere] * 6,
        out_specs=(vmem, vmem),
        scratch_shapes=[
            pltpu.VMEM((width, inner), BF16),
            pltpu.VMEM((width, inner), BF16),
            pltpu.VMEM((width, 2 * NSTATE), BF16),
            pltpu.VMEM((128, width), BF16),
            pltpu.VMEM((inner, width), BF16),
            pltpu.VMEM((3, 8, 128), F32),
            pltpu.VMEM((tok_rows, part), BF16),
            pltpu.VMEM((slots, part), BF16),
            pltpu.VMEM((slots, part), BF16),
            pltpu.VMEM((chunks, ROWS, part), BF16),
            pltpu.VMEM((slots, width), BF16),
            pltpu.VMEM((slots, width), BF16),
            pltpu.VMEM((chunks, ROWS, width), BF16),
            pltpu.VMEM((chunks, half, width), BF16),
            pltpu.VMEM((chunks, half, width), BF16),
            pltpu.VMEM((chunks, 2, half, width), BF16),
            pltpu.VMEM((chunks, 2, half, width), BF16),
            pltpu.VMEM((ROWS, width), BF16),
            pltpu.VMEM((ROWS, inner), BF16),
            pltpu.VMEM((ROWS, inner), F32),
            pltpu.VMEM((ROWS, 2 * NSTATE), BF16),
            pltpu.VMEM((ROWS, 128), F32),
            pltpu.VMEM((slots, inner), BF16),
            pltpu.VMEM((slots, inner), BF16),
            pltpu.VMEM((slots, 128), F32),
            pltpu.VMEM((NSTATE, inner), F32),
            pltpu.VMEM((8, 128), F32),
            pltpu.VMEM((slots, 128), F32),
            pltpu.VMEM((slots // SUB, 8, 128), F32),
            pltpu.VMEM((RING, chunks, ROWS // SUB, 8, 128), F32),
            pltpu.VMEM((8, inner), F32),
            pltpu.VMEM((slots, width), BF16),
            pltpu.VMEM((levels, RING * share, slots), BF16),
            pltpu.VMEM((levels, RING * share, inner), F32),
            pltpu.VMEM((levels, RING, share, inner), BF16),
            pltpu.VMEM((2, some, share, inner), BF16),
            pltpu.VMEM((2, some, share, inner), BF16),
            pltpu.VMEM((levels, share, inner), BF16),
            pltpu.VMEM((levels, share, inner), BF16),
            pltpu.VMEM((levels, share, inner), BF16),
            pltpu.VMEM((levels, share, inner), BF16),
            dma((6,)),
            dma((readers,)),
            dma((readers,)),
            dma((RING, chunks)),
            dma((chunks,)),
            dma((5, chunks)),
            dma((chunks,)),
            dma((6, chunks)),
            dma((6, chunks)),
            dma((6, chunks)),
            dma((6, chunks)),
            dma((3, chunks)),
            dma((3, chunks)),
            dma((6, 2)),
            dma((6, 2)),
            dma((levels,)),
            dma((levels,)),
        ],
        compiler_params=pltpu.CompilerParams(
            collective_id=1, has_side_effects=True, vmem_limit_bytes=60 * 1024 * 1024
        ),
    )(
        *tables,
        pre_gain[None],
        step_bias[None],
        decay_log[None],
        skip_gain[None],
        norm_gain[None],
        step_proj.T,
        tokens,
        input_proj,
        gate_proj,
        state_proj,
        out_proj,
        cot,
    )


def per_device(
    tokens,
    base_rows,
    baseline_owner,
    cotangent,
    *params,
):
    tables = (base_rows[None, :], baseline_owner[None, :])
    result, grad = run_blocks(
        tables, tokens, cotangent[0], tuple(item[0] for item in params)
    )
    return (result[None], grad.T[None])


def solution(mesh):
    return jax.shard_map(
        per_device,
        mesh=mesh,
        in_specs=(
            P("dp", None),
            P(),
            P(),
            P("section", "dp", None),
            P("section", None),
            P("section", None, "tensor"),
            P("section", None, "tensor"),
            P("section", None, None),
            P("section", None, "tensor"),
            P("section", "tensor"),
            P("section", "tensor"),
            P("section", "tensor"),
            P("section", "tensor"),
            P("section", "tensor", None),
        ),
        out_specs=(P("section", "dp", None), P("section", "tensor", "dp")),
        check_vma=False,
    )
```

```python
import functools

import jax
import jax.numpy as jnp
from jax import lax
from jax.experimental import pallas as pl
from jax.experimental.pallas import tpu as pltpu
from jax.sharding import PartitionSpec as P

MESH = pl.DeviceIdType.MESH
HEADDIM = 64
NSTATE = 128
ROWS = 128
SUB = 128
RING = 4
EPS = 1e-05
F32 = jnp.float32
BF16 = jnp.bfloat16


def iota(shape, axis):
    return lax.broadcasted_iota(jnp.int32, shape, axis)


def silu(value):
    return value / (1.0 + jnp.exp(-value))


def softplus(value):
    return jnp.maximum(value, 0.0) + jnp.log1p(jnp.exp(-jnp.abs(value)))


def owner_starts(rows_c, rows_r, own_c, own_r):
    count = rows_r.shape[1]
    down, across = iota((count, count), 0), iota((count, count), 1)
    same = own_c == own_r
    row = jnp.sum(jnp.where(same & (down < across), rows_c, 0), axis=0, keepdims=True)
    col = jnp.sum(jnp.where(same & (across < down), rows_r, 0), axis=1, keepdims=True)
    return row, col


def block_kernel(
    chunks,
    heads,
    levels,
    rows_r,
    own_r,
    pre_gain,
    step_bias,
    decay_log,
    skip_gain,
    norm_gain,
    step_t,
    tokens,
    in_hbm,
    gate_hbm,
    state_hbm,
    out_hbm,
    cot_hbm,
    out_ref,
    grad_ref,
    w_in,
    w_gate,
    w_state,
    w_step,
    w_out,
    small,
    tok_buf,
    away,
    arrived,
    s_buf,
    u_buf,
    o_buf,
    p_buf,
    a1,
    b1,
    a2,
    b2,
    normed,
    xs_buf,
    gate_buf,
    bc_buf,
    dt_buf,
    y_ref,
    yn_buf,
    rs_ref,
    state,
    prev,
    seg_col,
    seg_row,
    sq_buf,
    skip_row,
    cot,
    cot_t,
    g_acc,
    g_buf,
    ga1,
    gb1,
    ga2,
    gb2,
    h_buf,
    z_buf,
    load_sem,
    turn_send,
    turn_recv,
    feed_send,
    hand_sem,
    hand_send,
    out_sem,
    rs_send,
    rs_recv,
    ag_send,
    ag_recv,
    sq_send,
    sq_recv,
    g_send,
    g_recv,
    z_send,
    z_recv,
):
    me = lax.axis_index("tensor")
    sec = lax.axis_index("section")
    owner = lax.axis_index("dp")
    right, left, opposite = ((me + 1) % RING, (me + 3) % RING, (me + 2) % RING)
    readers = lax.axis_size("dp")
    inner = w_in.shape[1]
    pairs = heads // 2
    piece = ROWS // RING
    half = piece // 2
    count = rows_r.shape[1]
    slots = chunks * ROWS
    subs = ROWS // SUB
    cap = slots // readers
    tok_rows, part = tok_buf.shape
    my_cols = pl.ds(pl.multiple_of((2 * me + sec) * part, part), part)
    my_z, my_y = owner // RING, owner % RING
    right_y, left_y, opposite_y = ((my_y + 1) % RING, (my_y + 3) % RING, (my_y + 2) % RING)
    share = g_buf.shape[2]
    block = RING * share
    group = levels // 2
    some = group // 2

    loads = [
        pltpu.make_async_copy(src, dst, load_sem.at[k])
        for k, (src, dst) in enumerate(
            (
                (tokens.at[:, my_cols], tok_buf),
                (in_hbm, w_in),
                (state_hbm, w_state),
                (gate_hbm, w_gate),
                (out_hbm, w_out),
                (cot_hbm, cot),
            )
        )
    ]
    loads[0].start()

    barrier = pltpu.get_barrier_semaphore()

    def greet(k, carry):
        pl.semaphore_signal(
            barrier, inc=1, device_id={"dp": (owner + k) % readers}, device_id_type=MESH
        )
        return carry

    lax.fori_loop(1, readers, greet, 0)
    for k in range(RING):
        other = (me + k) % RING
        if k:
            pl.semaphore_signal(barrier, inc=1, device_id={"tensor": other}, device_id_type=MESH)
        pl.semaphore_signal(
            barrier,
            inc=1,
            device_id={"section": 1 - sec, "tensor": other},
            device_id_type=MESH,
        )

    def rows_of(t):
        return pl.ds(pl.multiple_of(t * ROWS, ROWS), ROWS)

    def piece_of(who, which=None):
        if which is None:
            return pl.ds(pl.multiple_of(who * piece, piece), piece)
        return pl.ds(pl.multiple_of(who * piece + which * half, half), half)

    def out_piece(t, who, which=None):
        if which is None:
            return pl.ds(pl.multiple_of(t * ROWS + who * piece, piece), piece)
        return pl.ds(pl.multiple_of(t * ROWS + who * piece + which * half, half), half)

    def cap_of(who):
        return pl.ds(pl.multiple_of(who * cap, cap), cap)

    def push(src, dst, send_sem, recv_sem, **where):
        return pltpu.make_async_remote_copy(
            src_ref=src,
            dst_ref=dst,
            send_sem=send_sem,
            recv_sem=recv_sem,
            device_id=where,
            device_id_type=MESH,
        )

    def turn(k):
        other = (owner + k) % readers
        return push(
            away.at[cap_of(other)],
            arrived.at[cap_of(owner)],
            turn_send.at[k],
            turn_recv.at[k],
            dp=other,
        )

    def feed_own(t):
        return pltpu.make_async_copy(s_buf.at[t], u_buf.at[rows_of(t), my_cols], hand_sem.at[t])

    def feed(t, k):
        return push(
            s_buf.at[t],
            u_buf.at[rows_of(t), my_cols],
            feed_send.at[k, t],
            hand_sem.at[t],
            section=0,
            tensor=(me + k) % RING,
        )

    def hand_over(t, k):
        where = (
            lambda: out_piece(t, me),
            lambda: out_piece(t, left),
            lambda: out_piece(t, right),
            lambda: out_piece(t, opposite, 0),
            lambda: out_piece(t, opposite, 1),
        )[k]()
        return push(
            o_buf.at[where], u_buf.at[where], hand_send.at[k, t], hand_sem.at[t], section=1 - sec
        )

    def pass_on(t, *which):
        @pl.when(sec == 0)
        def _():
            for k in which:
                hand_over(t, k).start()

    def store_out(t):
        return pltpu.make_async_copy(o_buf.at[rows_of(t)], out_ref.at[rows_of(t)], out_sem.at[t])

    def column(row):
        return jnp.broadcast_to(row.astype(F32), (count, count)).T[:, 0:1].astype(jnp.int32)

    rows_c, own_c = column(rows_r[...]), column(own_r[...])
    start_row, start_col = owner_starts(rows_c, rows_r[...], own_c, own_r[...])
    down, across = iota((count, count), 0), iota((count, count), 1)
    first_c = jnp.sum(jnp.where(across < down, rows_r[...], 0), axis=1, keepdims=True)
    token = iota((count, tok_rows), 1)
    inside = (token >= first_c) & (token < first_c + rows_c)
    target = jnp.sum(
        jnp.where(inside, own_c * cap + start_col - first_c + token, 0), axis=0, keepdims=True
    )
    chosen = (iota((slots, tok_rows), 0) == target).astype(F32).astype(BF16)
    loads[0].wait()
    for load in loads[1:]:
        load.start()
    away[...] = jnp.dot(chosen, tok_buf[...], preferred_element_type=F32).astype(BF16)
    arrived[cap_of(owner), :] = away[cap_of(owner), :]
    pl.semaphore_wait(barrier, readers - 1 + RING - 1 + RING)

    def send_turn(k, carry):
        far = (k + readers // 2) % readers

        @pl.when(far != 0)
        def _():
            turn(far).start()

        return carry

    lax.fori_loop(0, readers, send_turn, 0)

    ids_c = (iota((count, 1), 0) + 1).astype(F32)
    ids_r = (iota((1, count), 1) + 1).astype(F32)
    slot_r = iota((count, slots), 1)
    held_c = (
        (own_c == owner)
        & (slot_r >= readers * start_col)
        & (slot_r < readers * (start_col + rows_c))
    )
    ids_row = jnp.sum(jnp.where(held_c, ids_c, 0.0), axis=0, keepdims=True)
    for k in range(slots // SUB):
        seg_row[k] = jnp.broadcast_to(ids_row[:, k * SUB : (k + 1) * SUB], (8, SUB))
    slot_c = iota((slots, count), 0)
    held_r = (
        (own_r[...] == owner)
        & (slot_c >= readers * start_row)
        & (slot_c < readers * (start_row + rows_r[...]))
    )
    ids_col = jnp.sum(jnp.where(held_r, ids_r, 0.0), axis=1, keepdims=True)
    seg_col[...] = jnp.broadcast_to(ids_col, (slots, SUB))
    place, reader = slot_r % cap, slot_r // cap
    held = (own_c == owner) & (place >= start_col) & (place < start_col + rows_c)
    goal = jnp.sum(
        jnp.where(held, (readers - 1) * start_col + reader * rows_c + place + 1, 0),
        axis=0,
        keepdims=True,
    ) - 1
    state[...] = jnp.zeros_like(state)
    prev[...] = jnp.full(prev.shape, -1.0, F32)
    lane = iota((SUB, 128), 1)
    low = lane < HEADDIM

    def spread(value, pair):
        shape = (value.shape[0], 128)
        first = jnp.broadcast_to(value[:, 2 * pair : 2 * pair + 1], shape)
        second = jnp.broadcast_to(value[:, 2 * pair + 1 : 2 * pair + 2], shape)
        return jnp.where(iota(shape, 1) < HEADDIM, first, second)

    small[...] = jnp.zeros_like(small)
    for k, ref in enumerate((step_bias, decay_log, skip_gain)):
        small[k, 0:1, 0:heads] = ref[...]
    w_step[...] = jnp.concatenate(
        [step_t[...].astype(F32), jnp.zeros((128 - heads, step_t.shape[1]), F32)], axis=0
    ).astype(BF16)
    for pair in range(pairs):
        skip_row[:, pair * 128 : (pair + 1) * 128] = spread(
            jnp.broadcast_to(small[2, 0:1, :], (8, 128)), pair
        )
    rate = -jnp.exp(small[1, 0:1, :])

    loads[5].wait()

    def level_of(m):
        return (my_z + m + 2) % levels

    def turn_cot(m, carry):
        cols = pl.ds(pl.multiple_of(level_of(m) * block, block), block)
        cot_t[m] = cot[:, cols].T
        return carry

    lax.fori_loop(0, levels, turn_cot, 0)

    def take_turn(k, carry):
        turn(k).wait_recv()
        return carry

    lax.fori_loop(1, readers, take_turn, 0)
    for t in range(chunks):
        placed = (iota((ROWS, slots), 0) + t * ROWS == goal).astype(F32).astype(BF16)
        s_buf[t] = jnp.dot(placed, arrived[...], preferred_element_type=F32).astype(BF16)
        for k in (2, 1, 3):
            feed(t, k).start()

        @pl.when(sec == 0)
        def _():
            feed_own(t).start()

        @pl.when(sec == 1)
        def _():
            feed(t, 0).start()

    for load in loads[1:5]:
        load.wait()

    def stage_in(t):
        pltpu.make_async_copy(u_buf.at[rows_of(t)], u_buf.at[rows_of(t)], hand_sem.at[t]).wait()
        rows_f = u_buf[rows_of(t), :].astype(F32)
        scale = lax.rsqrt(jnp.mean(rows_f * rows_f, axis=-1, keepdims=True) + EPS)
        normed[...] = (rows_f * scale * pre_gain[...]).astype(BF16)
        xs_buf[...] = silu(jnp.dot(normed[...], w_in[...], preferred_element_type=F32)).astype(BF16)
        bc_buf[...] = silu(jnp.dot(normed[...], w_state[...], preferred_element_type=F32)).astype(
            BF16
        )
        dt_buf[...] = softplus(
            lax.dot_general(
                normed[...], w_step[...], (((1,), (1,)), ((), ())), preferred_element_type=F32
            )
            + small[0, 0:1, :]
        )
        gate_buf[...] = silu(jnp.dot(normed[...], w_gate[...], preferred_element_type=F32))

    def stage_scan(t, sub):
        here = slice(sub * SUB, (sub + 1) * SUB)
        rows = pl.ds(pl.multiple_of(t * ROWS + sub * SUB, SUB), SUB)
        segment_c = seg_col[rows, :]
        segment_r = jnp.broadcast_to(seg_row[t * subs + sub][0:1, :], (SUB, SUB))
        before = jnp.broadcast_to(prev[0:1, :], (SUB, SUB))
        last = segment_c[SUB - 1 : SUB, :]
        down, across = iota((SUB, SUB), 0), iota((SUB, SUB), 1)
        causal = down >= across
        hidden = jnp.where(causal & (segment_c == segment_r), 0.0, -1e30)
        dt = dt_buf[here, :]
        cum = jnp.dot(
            causal.astype(F32),
            dt * rate,
            preferred_element_type=F32,
            precision=lax.Precision.HIGHEST,
        )
        cum_t, dt_t = cum.T, dt.T
        grown = jnp.exp(cum)
        from_before = jnp.where(segment_c == before, grown, 0.0)
        last_cum = cum[SUB - 1 : SUB, :]
        tail = jnp.where(segment_c == last, jnp.exp(last_cum - cum), 0.0) * dt
        kept = jnp.where(last == prev[0:1, :], jnp.exp(last_cum), 0.0)
        b_rows, c_rows = bc_buf[here, :NSTATE], bc_buf[here, NSTATE:]
        scores = lax.dot_general(
            c_rows, b_rows, (((1,), (1,)), ((), ())), preferred_element_type=F32
        )
        readout = jnp.dot(c_rows, state[...].astype(BF16), preferred_element_type=F32)
        squares = jnp.zeros((SUB, 128), F32)
        for pair in range(pairs):
            cols = slice(pair * 128, (pair + 1) * 128)
            x_pair = xs_buf[here, cols]
            x_f = x_pair.astype(F32)
            parts = []
            for head in (2 * pair, 2 * pair + 1):
                falling = jnp.minimum(cum[:, head : head + 1] - cum_t[head : head + 1, :], 0.0)
                weights = jnp.exp(falling + hidden) * scores * dt_t[head : head + 1, :]
                parts.append(jnp.dot(weights.astype(BF16), x_pair, preferred_element_type=F32))
            total = (
                jnp.where(low, parts[0], parts[1])
                + spread(from_before, pair) * readout[:, cols]
                + skip_row[0:1, cols] * x_f
            )
            gated = total * gate_buf[here, cols]
            squares = squares + gated * gated
            y_ref[rows, cols] = (gated * norm_gain[:, cols]).astype(BF16)
            scaled = (spread(tail, pair) * x_f).astype(BF16)
            fresh = lax.dot_general(
                b_rows, scaled, (((0,), (0,)), ((), ())), preferred_element_type=F32
            )
            state[:, cols] = spread(kept, pair) * state[:, cols] + fresh
        prev[...] = jnp.broadcast_to(last, prev.shape)
        sq_buf[0, t, sub] = jnp.broadcast_to(jnp.sum(squares.T, axis=0, keepdims=True), (8, SUB))

    def square_copy(t, k):
        return push(
            sq_buf.at[0, t],
            sq_buf.at[k, t],
            sq_send.at[k - 1, t],
            sq_recv.at[k - 1, t],
            tensor=(me + k) % RING,
        )

    def reduce_copy(t, k):
        who, which, dst, to = (
            (opposite, 0, lambda: a1.at[t], right),
            (opposite, 1, lambda: b1.at[t], left),
            (right, 1, lambda: a2.at[t, 1], right),
            (left, 0, lambda: b2.at[t, 0], left),
            (right, 0, lambda: a2.at[t, 0], right),
            (left, 1, lambda: b2.at[t, 1], left),
        )[k]
        return push(
            p_buf.at[t, piece_of(who, which)], dst(), rs_send.at[k, t], rs_recv.at[k, t], tensor=to
        )

    def gather_copy(t, k):
        who, which, to = (
            (me, 0, right),
            (me, 1, left),
            (me, 1, right),
            (me, 0, left),
            (left, 0, right),
            (right, 1, left),
        )[k]
        rows = o_buf.at[out_piece(t, who, which)]
        return push(rows, rows, ag_send.at[k, t], ag_recv.at[k, t], tensor=to)

    def stage_out(t):
        p_buf[t] = jnp.dot(y_ref[rows_of(t), :], w_out[...], preferred_element_type=F32).astype(
            BF16
        )
        for k in range(4):
            reduce_copy(t, k).start()

    def reduce_second(t):
        for k, who, which, got in ((0, right, 0, a1), (1, left, 1, b1)):
            reduce_copy(t, k).wait_recv()
            where = piece_of(who, which)
            p_buf[t, where, :] = (p_buf[t, where, :].astype(F32) + got[t].astype(F32)).astype(BF16)
            reduce_copy(t, k + 4).start()

    def reduce_last(t):
        for k in range(1, RING):
            square_copy(t, k).wait_recv()
        total = sq_buf[0, t] + sq_buf[1, t] + sq_buf[2, t] + sq_buf[3, t]
        scale = lax.rsqrt(total / (RING * inner) + EPS)
        for sub in range(subs):
            rows = pl.ds(pl.multiple_of(t * ROWS + sub * SUB, SUB), SUB)
            rs_ref[rows, :] = jnp.broadcast_to(scale[sub, 0:1, :], (SUB, SUB)).T
        yn_buf[rows_of(t), :] = (
            y_ref[rows_of(t), :].astype(F32) * rs_ref[rows_of(t), 0:1]
        ).astype(BF16)
        for k in range(2, 6):
            reduce_copy(t, k).wait_recv()
        for which in (0, 1):
            where = out_piece(t, me, which)
            summed = (
                p_buf[t, piece_of(me, which), :].astype(F32)
                + a2[t, which].astype(F32)
                + b2[t, which].astype(F32)
            )
            o_buf[where, :] = (
                u_buf[where, :].astype(F32) + rs_ref[where, 0:1] * summed
            ).astype(BF16)
        for k in range(4):
            gather_copy(t, k).start()
        pass_on(t, 0)

    def gather_second(t):
        for k in (0, 1):
            gather_copy(t, k).wait_recv()
            gather_copy(t, k + 4).start()
        for k in (2, 3):
            gather_copy(t, k).wait_recv()
        pass_on(t, 1, 2)

    def gather_last(t):
        gather_copy(t, 4).wait_recv()
        gather_copy(t, 5).wait_recv()
        pass_on(t, 3, 4)
        store_out(t).start()

    early = (chunks - 1) * ROWS

    def grad_early(m, carry):
        g_acc[m] = jnp.dot(cot_t[m, :, :early], yn_buf[:early, :], preferred_element_type=F32)
        return carry

    def grad_late(m, carry):
        term = g_acc[m] + jnp.dot(
            cot_t[m, :, early:], yn_buf[early:, :], preferred_element_type=F32
        )
        g_buf[m] = term.astype(BF16).reshape(RING, share, inner)
        return carry

    def grad_copy(g, k):
        base = g * group
        first, second = pl.ds(base, some), pl.ds(base + some, some)
        src, dst, to = (
            (lambda: g_buf.at[first, opposite_y], lambda: ga1.at[g], right_y),
            (lambda: g_buf.at[second, opposite_y], lambda: gb1.at[g], left_y),
            (lambda: g_buf.at[second, right_y], lambda: ga2.at[second], right_y),
            (lambda: g_buf.at[first, left_y], lambda: gb2.at[first], left_y),
            (lambda: g_buf.at[first, right_y], lambda: ga2.at[first], right_y),
            (lambda: g_buf.at[second, left_y], lambda: gb2.at[second], left_y),
        )[k]
        return push(src(), dst(), g_send.at[k, g], g_recv.at[k, g], dp=my_z * RING + to)

    def exchange(m):
        return push(
            h_buf.at[m],
            z_buf.at[m],
            z_send.at[m],
            z_recv.at[m],
            dp=level_of(m) * RING + my_y,
        )

    def grad_send(g):
        lax.fori_loop(g * group, (g + 1) * group, grad_late, 0)
        for k in range(4):
            grad_copy(g, k).start()

    def grad_second(g):
        for k, offset, who, got in ((0, 0, right_y, ga1), (1, some, left_y, gb1)):
            grad_copy(g, k).wait_recv()
            for j in range(some):
                m = g * group + offset + j
                g_buf[m, who] = (g_buf[m, who].astype(F32) + got[g, j].astype(F32)).astype(BF16)
            grad_copy(g, k + 4).start()

    def level_sum(m):
        return g_buf[m, my_y].astype(F32) + ga2[m].astype(F32) + gb2[m].astype(F32)

    def grad_finish(g):
        for k in range(2, 6):
            grad_copy(g, k).wait_recv()
        for m in ((2, 1, 3, 0), (4, 7, 5))[g]:
            if m != levels - 2:
                h_buf[m] = level_sum(m).astype(BF16)
                exchange(m).start()

    def step(t, carry):
        @pl.when(t < chunks)
        def _():
            stage_in(t)
            for sub in range(subs):
                stage_scan(t, sub)
            for k in range(1, RING):
                square_copy(t, k).start()
            stage_out(t)

        @pl.when((t >= 1) & (t < chunks + 1))
        def _():
            reduce_second(t - 1)

        @pl.when((t >= 2) & (t < chunks + 2))
        def _():
            reduce_last(t - 2)

        @pl.when(t == chunks + 4 * (1 - sec))
        def _():
            lax.fori_loop(0, levels, grad_early, 0)

        @pl.when(t == chunks + 1 + 3 * (1 - sec))
        def _():
            grad_send(0)
            grad_send(1)

        @pl.when((t >= 3) & (t < chunks + 3))
        def _():
            gather_second(t - 3)

        @pl.when(t == chunks + 2 + 3 * (1 - sec))
        def _():
            grad_second(0)

        @pl.when((t >= 4) & (t < chunks + 4))
        def _():
            gather_last(t - 4)

        return carry

    lax.fori_loop(0, chunks + 4 + 2 * (1 - sec), step, 0)
    grad_second(1)
    grad_finish(0)
    grad_finish(1)
    total = level_sum(levels - 2)
    for m in range(levels):
        if m != levels - 2:
            exchange(m).wait_recv()
            total = total + z_buf[m].astype(F32)
    grad_ref[...] = total.astype(BF16)
    for g in (0, 1):
        for k in range(6):
            grad_copy(g, k).wait_send()
    for m in range(levels):
        if m != levels - 2:
            exchange(m).wait_send()

    def sent_turn(k, carry):
        turn(k).wait_send()
        return carry

    lax.fori_loop(1, readers, sent_turn, 0)

    def drain(t, carry):
        for k in range(6):
            reduce_copy(t, k).wait_send()
        for k in range(6):
            gather_copy(t, k).wait_send()
        for k in range(1, RING):
            square_copy(t, k).wait_send()
            feed(t, k).wait_send()

        @pl.when(sec == 0)
        def _():
            for k in range(5):
                hand_over(t, k).wait_send()

        @pl.when(sec == 1)
        def _():
            feed(t, 0).wait_send()

        store_out(t).wait()
        return carry

    lax.fori_loop(0, chunks, drain, 0)


def run_blocks(tables, tokens, cot, params):
    (
        pre_gain,
        input_proj,
        gate_proj,
        state_proj,
        step_proj,
        step_bias,
        decay_log,
        skip_gain,
        norm_gain,
        out_proj,
    ) = params
    readers = lax.axis_size("dp")
    tok_rows, width = tokens.shape
    slots = 2 * tok_rows
    inner = input_proj.shape[1]
    heads = step_proj.shape[1]
    chunks = slots // ROWS
    part = width // (2 * RING)
    share = width // readers
    levels = readers // RING
    some = levels // 4
    vmem = pl.BlockSpec(memory_space=pltpu.VMEM)
    anywhere = pl.BlockSpec(memory_space=pl.ANY)
    half = ROWS // RING // 2
    dma = pltpu.SemaphoreType.DMA
    return pl.pallas_call(
        functools.partial(block_kernel, chunks, heads, levels),
        name="blocks",
        out_shape=(
            pltpu.VMEM((slots, width), BF16),
            pltpu.VMEM((share, inner), BF16),
        ),
        in_specs=[vmem] * 8 + [anywhere] * 6,
        out_specs=(vmem, vmem),
        scratch_shapes=[
            pltpu.VMEM((width, inner), BF16),
            pltpu.VMEM((width, inner), BF16),
            pltpu.VMEM((width, 2 * NSTATE), BF16),
            pltpu.VMEM((128, width), BF16),
            pltpu.VMEM((inner, width), BF16),
            pltpu.VMEM((3, 8, 128), F32),
            pltpu.VMEM((tok_rows, part), BF16),
            pltpu.VMEM((slots, part), BF16),
            pltpu.VMEM((slots, part), BF16),
            pltpu.VMEM((chunks, ROWS, part), BF16),
            pltpu.VMEM((slots, width), BF16),
            pltpu.VMEM((slots, width), BF16),
            pltpu.VMEM((chunks, ROWS, width), BF16),
            pltpu.VMEM((chunks, half, width), BF16),
            pltpu.VMEM((chunks, half, width), BF16),
            pltpu.VMEM((chunks, 2, half, width), BF16),
            pltpu.VMEM((chunks, 2, half, width), BF16),
            pltpu.VMEM((ROWS, width), BF16),
            pltpu.VMEM((ROWS, inner), BF16),
            pltpu.VMEM((ROWS, inner), F32),
            pltpu.VMEM((ROWS, 2 * NSTATE), BF16),
            pltpu.VMEM((ROWS, 128), F32),
            pltpu.VMEM((slots, inner), BF16),
            pltpu.VMEM((slots, inner), BF16),
            pltpu.VMEM((slots, 128), F32),
            pltpu.VMEM((NSTATE, inner), F32),
            pltpu.VMEM((8, 128), F32),
            pltpu.VMEM((slots, 128), F32),
            pltpu.VMEM((slots // SUB, 8, 128), F32),
            pltpu.VMEM((RING, chunks, ROWS // SUB, 8, 128), F32),
            pltpu.VMEM((8, inner), F32),
            pltpu.VMEM((slots, width), BF16),
            pltpu.VMEM((levels, RING * share, slots), BF16),
            pltpu.VMEM((levels, RING * share, inner), F32),
            pltpu.VMEM((levels, RING, share, inner), BF16),
            pltpu.VMEM((2, some, share, inner), BF16),
            pltpu.VMEM((2, some, share, inner), BF16),
            pltpu.VMEM((levels, share, inner), BF16),
            pltpu.VMEM((levels, share, inner), BF16),
            pltpu.VMEM((levels, share, inner), BF16),
            pltpu.VMEM((levels, share, inner), BF16),
            dma((6,)),
            dma((readers,)),
            dma((readers,)),
            dma((RING, chunks)),
            dma((chunks,)),
            dma((5, chunks)),
            dma((chunks,)),
            dma((6, chunks)),
            dma((6, chunks)),
            dma((6, chunks)),
            dma((6, chunks)),
            dma((3, chunks)),
            dma((3, chunks)),
            dma((6, 2)),
            dma((6, 2)),
            dma((levels,)),
            dma((levels,)),
        ],
        compiler_params=pltpu.CompilerParams(
            collective_id=1, has_side_effects=True, vmem_limit_bytes=60 * 1024 * 1024
        ),
    )(
        *tables,
        pre_gain[None],
        step_bias[None],
        decay_log[None],
        skip_gain[None],
        norm_gain[None],
        step_proj.T,
        tokens,
        input_proj,
        gate_proj,
        state_proj,
        out_proj,
        cot,
    )


def per_device(
    tokens,
    base_rows,
    baseline_owner,
    cotangent,
    *params,
):
    tables = (base_rows[None, :], baseline_owner[None, :])
    result, grad = run_blocks(
        tables, tokens, cotangent[0], tuple(item[0] for item in params)
    )
    return (result[None], grad.T[None])


def solution(mesh):
    return jax.shard_map(
        per_device,
        mesh=mesh,
        in_specs=(
            P("dp", None),
            P(),
            P(),
            P("section", "dp", None),
            P("section", None),
            P("section", None, "tensor"),
            P("section", None, "tensor"),
            P("section", None, None),
            P("section", None, "tensor"),
            P("section", "tensor"),
            P("section", "tensor"),
            P("section", "tensor"),
            P("section", "tensor"),
            P("section", "tensor", None),
        ),
        out_specs=(P("section", "dp", None), P("section", "tensor", "dp")),
        check_vma=False,
    )
```

```python
import functools

import jax
import jax.numpy as jnp
from jax import lax
from jax.experimental import pallas as pl
from jax.experimental.pallas import tpu as pltpu
from jax.sharding import PartitionSpec as P

MESH = pl.DeviceIdType.MESH
HEADDIM = 64
NSTATE = 128
ROWS = 128
SUB = 128
RING = 4
EPS = 1e-05
F32 = jnp.float32
BF16 = jnp.bfloat16


def iota(shape, axis):
    return lax.broadcasted_iota(jnp.int32, shape, axis)


def silu(value):
    return value / (1.0 + jnp.exp(-value))


def softplus(value):
    return jnp.maximum(value, 0.0) + jnp.log1p(jnp.exp(-jnp.abs(value)))


def owner_starts(rows_c, rows_r, own_c, own_r):
    count = rows_r.shape[1]
    down, across = iota((count, count), 0), iota((count, count), 1)
    same = own_c == own_r
    row = jnp.sum(jnp.where(same & (down < across), rows_c, 0), axis=0, keepdims=True)
    col = jnp.sum(jnp.where(same & (across < down), rows_r, 0), axis=1, keepdims=True)
    return row, col


def block_kernel(
    chunks,
    heads,
    levels,
    rows_r,
    own_r,
    pre_gain,
    step_bias,
    decay_log,
    skip_gain,
    norm_gain,
    step_t,
    tokens,
    in_hbm,
    gate_hbm,
    state_hbm,
    out_hbm,
    cot_hbm,
    out_ref,
    grad_ref,
    w_in,
    w_gate,
    w_state,
    w_step,
    w_out,
    small,
    tok_buf,
    away,
    arrived,
    s_buf,
    u_buf,
    o_buf,
    p_buf,
    a1,
    b1,
    a2,
    b2,
    normed,
    xs_buf,
    gate_buf,
    bc_buf,
    dt_buf,
    y_ref,
    yn_buf,
    rs_ref,
    state,
    prev,
    seg_col,
    seg_row,
    sq_buf,
    skip_row,
    cot,
    cot_t,
    g_acc,
    g_buf,
    ga1,
    gb1,
    ga2,
    gb2,
    h_buf,
    z_buf,
    load_sem,
    turn_send,
    turn_recv,
    feed_send,
    hand_sem,
    hand_send,
    out_sem,
    rs_send,
    rs_recv,
    ag_send,
    ag_recv,
    sq_send,
    sq_recv,
    g_send,
    g_recv,
    z_send,
    z_recv,
):
    me = lax.axis_index("tensor")
    sec = lax.axis_index("section")
    owner = lax.axis_index("dp")
    right, left, opposite = ((me + 1) % RING, (me + 3) % RING, (me + 2) % RING)
    readers = lax.axis_size("dp")
    inner = w_in.shape[1]
    pairs = heads // 2
    piece = ROWS // RING
    half = piece // 2
    count = rows_r.shape[1]
    slots = chunks * ROWS
    subs = ROWS // SUB
    cap = slots // readers
    tok_rows, part = tok_buf.shape
    my_cols = pl.ds(pl.multiple_of((2 * me + sec) * part, part), part)
    my_z, my_y = owner // RING, owner % RING
    right_y, left_y, opposite_y = ((my_y + 1) % RING, (my_y + 3) % RING, (my_y + 2) % RING)
    share = g_buf.shape[2]
    block = RING * share
    group = levels // 2
    some = group // 2

    loads = [
        pltpu.make_async_copy(src, dst, load_sem.at[k])
        for k, (src, dst) in enumerate(
            (
                (tokens.at[:, my_cols], tok_buf),
                (in_hbm, w_in),
                (state_hbm, w_state),
                (gate_hbm, w_gate),
                (out_hbm, w_out),
                (cot_hbm, cot),
            )
        )
    ]
    loads[0].start()

    barrier = pltpu.get_barrier_semaphore()

    def greet(k, carry):
        pl.semaphore_signal(
            barrier, inc=1, device_id={"dp": (owner + k) % readers}, device_id_type=MESH
        )
        return carry

    lax.fori_loop(1, readers, greet, 0)
    for k in range(RING):
        other = (me + k) % RING
        if k:
            pl.semaphore_signal(barrier, inc=1, device_id={"tensor": other}, device_id_type=MESH)
        pl.semaphore_signal(
            barrier,
            inc=1,
            device_id={"section": 1 - sec, "tensor": other},
            device_id_type=MESH,
        )

    def rows_of(t):
        return pl.ds(pl.multiple_of(t * ROWS, ROWS), ROWS)

    def piece_of(who, which=None):
        if which is None:
            return pl.ds(pl.multiple_of(who * piece, piece), piece)
        return pl.ds(pl.multiple_of(who * piece + which * half, half), half)

    def out_piece(t, who, which=None):
        if which is None:
            return pl.ds(pl.multiple_of(t * ROWS + who * piece, piece), piece)
        return pl.ds(pl.multiple_of(t * ROWS + who * piece + which * half, half), half)

    def cap_of(who):
        return pl.ds(pl.multiple_of(who * cap, cap), cap)

    def push(src, dst, send_sem, recv_sem, **where):
        return pltpu.make_async_remote_copy(
            src_ref=src,
            dst_ref=dst,
            send_sem=send_sem,
            recv_sem=recv_sem,
            device_id=where,
            device_id_type=MESH,
        )

    def turn(k):
        other = (owner + k) % readers
        return push(
            away.at[cap_of(other)],
            arrived.at[cap_of(owner)],
            turn_send.at[k],
            turn_recv.at[k],
            dp=other,
        )

    def feed_own(t):
        return pltpu.make_async_copy(s_buf.at[t], u_buf.at[rows_of(t), my_cols], hand_sem.at[t])

    def feed(t, k):
        return push(
            s_buf.at[t],
            u_buf.at[rows_of(t), my_cols],
            feed_send.at[k, t],
            hand_sem.at[t],
            section=0,
            tensor=(me + k) % RING,
        )

    def hand_over(t, k):
        where = (
            lambda: out_piece(t, me),
            lambda: out_piece(t, left),
            lambda: out_piece(t, right),
            lambda: out_piece(t, opposite, 0),
            lambda: out_piece(t, opposite, 1),
        )[k]()
        return push(
            o_buf.at[where], u_buf.at[where], hand_send.at[k, t], hand_sem.at[t], section=1 - sec
        )

    def pass_on(t, *which):
        @pl.when(sec == 0)
        def _():
            for k in which:
                hand_over(t, k).start()

    def store_out(t):
        return pltpu.make_async_copy(o_buf.at[rows_of(t)], out_ref.at[rows_of(t)], out_sem.at[t])

    def column(row):
        return jnp.broadcast_to(row.astype(F32), (count, count)).T[:, 0:1].astype(jnp.int32)

    rows_c, own_c = column(rows_r[...]), column(own_r[...])
    start_row, start_col = owner_starts(rows_c, rows_r[...], own_c, own_r[...])
    down, across = iota((count, count), 0), iota((count, count), 1)
    first_c = jnp.sum(jnp.where(across < down, rows_r[...], 0), axis=1, keepdims=True)
    token = iota((count, tok_rows), 1)
    inside = (token >= first_c) & (token < first_c + rows_c)
    target = jnp.sum(
        jnp.where(inside, own_c * cap + start_col - first_c + token, 0), axis=0, keepdims=True
    )
    chosen = (iota((slots, tok_rows), 0) == target).astype(F32).astype(BF16)
    loads[0].wait()
    for load in loads[1:]:
        load.start()
    away[...] = jnp.dot(chosen, tok_buf[...], preferred_element_type=F32).astype(BF16)
    arrived[cap_of(owner), :] = away[cap_of(owner), :]
    pl.semaphore_wait(barrier, readers - 1 + RING - 1 + RING)

    def send_turn(k, carry):
        far = (k + readers // 2) % readers

        @pl.when(far != 0)
        def _():
            turn(far).start()

        return carry

    lax.fori_loop(0, readers, send_turn, 0)

    ids_c = (iota((count, 1), 0) + 1).astype(F32)
    ids_r = (iota((1, count), 1) + 1).astype(F32)
    slot_r = iota((count, slots), 1)
    held_c = (
        (own_c == owner)
        & (slot_r >= readers * start_col)
        & (slot_r < readers * (start_col + rows_c))
    )
    ids_row = jnp.sum(jnp.where(held_c, ids_c, 0.0), axis=0, keepdims=True)
    for k in range(slots // SUB):
        seg_row[k] = jnp.broadcast_to(ids_row[:, k * SUB : (k + 1) * SUB], (8, SUB))
    slot_c = iota((slots, count), 0)
    held_r = (
        (own_r[...] == owner)
        & (slot_c >= readers * start_row)
        & (slot_c < readers * (start_row + rows_r[...]))
    )
    ids_col = jnp.sum(jnp.where(held_r, ids_r, 0.0), axis=1, keepdims=True)
    seg_col[...] = jnp.broadcast_to(ids_col, (slots, SUB))
    place, reader = slot_r % cap, slot_r // cap
    held = (own_c == owner) & (place >= start_col) & (place < start_col + rows_c)
    goal = jnp.sum(
        jnp.where(held, (readers - 1) * start_col + reader * rows_c + place + 1, 0),
        axis=0,
        keepdims=True,
    ) - 1
    state[...] = jnp.zeros_like(state)
    prev[...] = jnp.full(prev.shape, -1.0, F32)
    lane = iota((SUB, 128), 1)
    low = lane < HEADDIM

    def spread(value, pair):
        shape = (value.shape[0], 128)
        first = jnp.broadcast_to(value[:, 2 * pair : 2 * pair + 1], shape)
        second = jnp.broadcast_to(value[:, 2 * pair + 1 : 2 * pair + 2], shape)
        return jnp.where(iota(shape, 1) < HEADDIM, first, second)

    small[...] = jnp.zeros_like(small)
    for k, ref in enumerate((step_bias, decay_log, skip_gain)):
        small[k, 0:1, 0:heads] = ref[...]
    w_step[...] = jnp.concatenate(
        [step_t[...].astype(F32), jnp.zeros((128 - heads, step_t.shape[1]), F32)], axis=0
    ).astype(BF16)
    for pair in range(pairs):
        skip_row[:, pair * 128 : (pair + 1) * 128] = spread(
            jnp.broadcast_to(small[2, 0:1, :], (8, 128)), pair
        )
    rate = -jnp.exp(small[1, 0:1, :])

    loads[5].wait()

    def level_of(m):
        return (my_z + m + 2) % levels

    def turn_cot(m, carry):
        cols = pl.ds(pl.multiple_of(level_of(m) * block, block), block)
        cot_t[m] = cot[:, cols].T
        return carry

    lax.fori_loop(0, levels, turn_cot, 0)

    def take_turn(k, carry):
        turn(k).wait_recv()
        return carry

    lax.fori_loop(1, readers, take_turn, 0)
    for t in range(chunks):
        placed = (iota((ROWS, slots), 0) + t * ROWS == goal).astype(F32).astype(BF16)
        s_buf[t] = jnp.dot(placed, arrived[...], preferred_element_type=F32).astype(BF16)
        for k in (2, 1, 3):
            feed(t, k).start()

        @pl.when(sec == 0)
        def _():
            feed_own(t).start()

        @pl.when(sec == 1)
        def _():
            feed(t, 0).start()

    for load in loads[1:5]:
        load.wait()

    def stage_in(t):
        pltpu.make_async_copy(u_buf.at[rows_of(t)], u_buf.at[rows_of(t)], hand_sem.at[t]).wait()
        rows_f = u_buf[rows_of(t), :].astype(F32)
        scale = lax.rsqrt(jnp.mean(rows_f * rows_f, axis=-1, keepdims=True) + EPS)
        normed[...] = (rows_f * scale * pre_gain[...]).astype(BF16)
        xs_buf[...] = silu(jnp.dot(normed[...], w_in[...], preferred_element_type=F32)).astype(BF16)
        bc_buf[...] = silu(jnp.dot(normed[...], w_state[...], preferred_element_type=F32)).astype(
            BF16
        )
        dt_buf[...] = softplus(
            lax.dot_general(
                normed[...], w_step[...], (((1,), (1,)), ((), ())), preferred_element_type=F32
            )
            + small[0, 0:1, :]
        )
        gate_buf[...] = silu(jnp.dot(normed[...], w_gate[...], preferred_element_type=F32))

    def stage_scan(t, sub):
        here = slice(sub * SUB, (sub + 1) * SUB)
        rows = pl.ds(pl.multiple_of(t * ROWS + sub * SUB, SUB), SUB)
        segment_c = seg_col[rows, :]
        segment_r = jnp.broadcast_to(seg_row[t * subs + sub][0:1, :], (SUB, SUB))
        before = jnp.broadcast_to(prev[0:1, :], (SUB, SUB))
        last = segment_c[SUB - 1 : SUB, :]
        down, across = iota((SUB, SUB), 0), iota((SUB, SUB), 1)
        causal = down >= across
        hidden = jnp.where(causal & (segment_c == segment_r), 0.0, -1e30)
        dt = dt_buf[here, :]
        cum = jnp.dot(
            causal.astype(F32),
            dt * rate,
            preferred_element_type=F32,
            precision=lax.Precision.HIGHEST,
        )
        cum_t, dt_t = cum.T, dt.T
        grown = jnp.exp(cum)
        from_before = jnp.where(segment_c == before, grown, 0.0)
        last_cum = cum[SUB - 1 : SUB, :]
        tail = jnp.where(segment_c == last, jnp.exp(last_cum - cum), 0.0) * dt
        kept = jnp.where(last == prev[0:1, :], jnp.exp(last_cum), 0.0)
        b_rows, c_rows = bc_buf[here, :NSTATE], bc_buf[here, NSTATE:]
        scores = lax.dot_general(
            c_rows, b_rows, (((1,), (1,)), ((), ())), preferred_element_type=F32
        )
        readout = jnp.dot(c_rows, state[...].astype(BF16), preferred_element_type=F32)
        squares = jnp.zeros((SUB, 128), F32)
        for pair in range(pairs):
            cols = slice(pair * 128, (pair + 1) * 128)
            x_pair = xs_buf[here, cols]
            x_f = x_pair.astype(F32)
            parts = []
            for head in (2 * pair, 2 * pair + 1):
                falling = jnp.minimum(cum[:, head : head + 1] - cum_t[head : head + 1, :], 0.0)
                weights = jnp.exp(falling + hidden) * scores * dt_t[head : head + 1, :]
                parts.append(jnp.dot(weights.astype(BF16), x_pair, preferred_element_type=F32))
            total = (
                jnp.where(low, parts[0], parts[1])
                + spread(from_before, pair) * readout[:, cols]
                + skip_row[0:1, cols] * x_f
            )
            gated = total * gate_buf[here, cols]
            squares = squares + gated * gated
            y_ref[rows, cols] = (gated * norm_gain[:, cols]).astype(BF16)
            scaled = (spread(tail, pair) * x_f).astype(BF16)
            fresh = lax.dot_general(
                b_rows, scaled, (((0,), (0,)), ((), ())), preferred_element_type=F32
            )
            state[:, cols] = spread(kept, pair) * state[:, cols] + fresh
        prev[...] = jnp.broadcast_to(last, prev.shape)
        sq_buf[0, t, sub] = jnp.broadcast_to(jnp.sum(squares.T, axis=0, keepdims=True), (8, SUB))

    def square_copy(t, k):
        return push(
            sq_buf.at[0, t],
            sq_buf.at[k, t],
            sq_send.at[k - 1, t],
            sq_recv.at[k - 1, t],
            tensor=(me + k) % RING,
        )

    def reduce_copy(t, k):
        who, which, dst, to = (
            (opposite, 0, lambda: a1.at[t], right),
            (opposite, 1, lambda: b1.at[t], left),
            (right, 1, lambda: a2.at[t, 1], right),
            (left, 0, lambda: b2.at[t, 0], left),
            (right, 0, lambda: a2.at[t, 0], right),
            (left, 1, lambda: b2.at[t, 1], left),
        )[k]
        return push(
            p_buf.at[t, piece_of(who, which)], dst(), rs_send.at[k, t], rs_recv.at[k, t], tensor=to
        )

    def gather_copy(t, k):
        who, which, to = (
            (me, 0, right),
            (me, 1, left),
            (me, 1, right),
            (me, 0, left),
            (left, 0, right),
            (right, 1, left),
        )[k]
        rows = o_buf.at[out_piece(t, who, which)]
        return push(rows, rows, ag_send.at[k, t], ag_recv.at[k, t], tensor=to)

    def stage_out(t):
        p_buf[t] = jnp.dot(y_ref[rows_of(t), :], w_out[...], preferred_element_type=F32).astype(
            BF16
        )
        for k in range(4):
            reduce_copy(t, k).start()

    def reduce_second(t):
        for k, who, which, got in ((0, right, 0, a1), (1, left, 1, b1)):
            reduce_copy(t, k).wait_recv()
            where = piece_of(who, which)
            p_buf[t, where, :] = (p_buf[t, where, :].astype(F32) + got[t].astype(F32)).astype(BF16)
            reduce_copy(t, k + 4).start()

    def reduce_last(t):
        for k in range(1, RING):
            square_copy(t, k).wait_recv()
        total = sq_buf[0, t] + sq_buf[1, t] + sq_buf[2, t] + sq_buf[3, t]
        scale = lax.rsqrt(total / (RING * inner) + EPS)
        for sub in range(subs):
            rows = pl.ds(pl.multiple_of(t * ROWS + sub * SUB, SUB), SUB)
            rs_ref[rows, :] = jnp.broadcast_to(scale[sub, 0:1, :], (SUB, SUB)).T
        yn_buf[rows_of(t), :] = (
            y_ref[rows_of(t), :].astype(F32) * rs_ref[rows_of(t), 0:1]
        ).astype(BF16)
        for k in range(2, 6):
            reduce_copy(t, k).wait_recv()
        for which in (0, 1):
            where = out_piece(t, me, which)
            summed = (
                p_buf[t, piece_of(me, which), :].astype(F32)
                + a2[t, which].astype(F32)
                + b2[t, which].astype(F32)
            )
            o_buf[where, :] = (
                u_buf[where, :].astype(F32) + rs_ref[where, 0:1] * summed
            ).astype(BF16)
        for k in range(4):
            gather_copy(t, k).start()
        pass_on(t, 0)

    def gather_second(t):
        for k in (0, 1):
            gather_copy(t, k).wait_recv()
            gather_copy(t, k + 4).start()
        for k in (2, 3):
            gather_copy(t, k).wait_recv()
        pass_on(t, 1, 2)

    def gather_last(t):
        gather_copy(t, 4).wait_recv()
        pass_on(t, 3)
        gather_copy(t, 5).wait_recv()
        pass_on(t, 4)
        store_out(t).start()

    early = (chunks - 1) * ROWS

    def grad_early(m, carry):
        g_acc[m] = jnp.dot(cot_t[m, :, :early], yn_buf[:early, :], preferred_element_type=F32)
        return carry

    def grad_late(m, carry):
        term = g_acc[m] + jnp.dot(
            cot_t[m, :, early:], yn_buf[early:, :], preferred_element_type=F32
        )
        g_buf[m] = term.astype(BF16).reshape(RING, share, inner)
        return carry

    def grad_copy(g, k):
        base = g * group
        first, second = pl.ds(base, some), pl.ds(base + some, some)
        src, dst, to = (
            (lambda: g_buf.at[first, opposite_y], lambda: ga1.at[g], right_y),
            (lambda: g_buf.at[second, opposite_y], lambda: gb1.at[g], left_y),
            (lambda: g_buf.at[second, right_y], lambda: ga2.at[second], right_y),
            (lambda: g_buf.at[first, left_y], lambda: gb2.at[first], left_y),
            (lambda: g_buf.at[first, right_y], lambda: ga2.at[first], right_y),
            (lambda: g_buf.at[second, left_y], lambda: gb2.at[second], left_y),
        )[k]
        return push(src(), dst(), g_send.at[k, g], g_recv.at[k, g], dp=my_z * RING + to)

    def exchange(m):
        return push(
            h_buf.at[m],
            z_buf.at[m],
            z_send.at[m],
            z_recv.at[m],
            dp=level_of(m) * RING + my_y,
        )

    def grad_send(g):
        lax.fori_loop(g * group, (g + 1) * group, grad_late, 0)
        for k in range(4):
            grad_copy(g, k).start()

    def grad_second(g):
        for k, offset, who, got in ((0, 0, right_y, ga1), (1, some, left_y, gb1)):
            grad_copy(g, k).wait_recv()
            for j in range(some):
                m = g * group + offset + j
                g_buf[m, who] = (g_buf[m, who].astype(F32) + got[g, j].astype(F32)).astype(BF16)
            grad_copy(g, k + 4).start()

    def level_sum(m):
        return g_buf[m, my_y].astype(F32) + ga2[m].astype(F32) + gb2[m].astype(F32)

    def grad_finish(g):
        for k in range(2, 6):
            grad_copy(g, k).wait_recv()
        for m in range(g * group, (g + 1) * group):
            if m != levels - 2:
                h_buf[m] = level_sum(m).astype(BF16)
                exchange(m).start()

    def step(t, carry):
        @pl.when(t < chunks)
        def _():
            stage_in(t)
            for sub in range(subs):
                stage_scan(t, sub)
            for k in range(1, RING):
                square_copy(t, k).start()
            stage_out(t)

        @pl.when((t >= 1) & (t < chunks + 1))
        def _():
            reduce_second(t - 1)

        @pl.when((t >= 2) & (t < chunks + 2))
        def _():
            reduce_last(t - 2)

        @pl.when(t == chunks + 4 * (1 - sec))
        def _():
            lax.fori_loop(0, levels, grad_early, 0)

        @pl.when(t == chunks + 1 + 3 * (1 - sec))
        def _():
            grad_send(0)
            grad_send(1)

        @pl.when((t >= 3) & (t < chunks + 3))
        def _():
            gather_second(t - 3)

        @pl.when((t >= 4) & (t < chunks + 4))
        def _():
            gather_last(t - 4)

        return carry

    lax.fori_loop(0, chunks + 4 + (1 - sec), step, 0)
    grad_second(0)
    grad_second(1)
    grad_finish(0)
    grad_finish(1)
    total = level_sum(levels - 2)
    for m in range(levels):
        if m != levels - 2:
            exchange(m).wait_recv()
            total = total + z_buf[m].astype(F32)
    grad_ref[...] = total.astype(BF16)
    for g in (0, 1):
        for k in range(6):
            grad_copy(g, k).wait_send()
    for m in range(levels):
        if m != levels - 2:
            exchange(m).wait_send()

    def sent_turn(k, carry):
        turn(k).wait_send()
        return carry

    lax.fori_loop(1, readers, sent_turn, 0)

    def drain(t, carry):
        for k in range(6):
            reduce_copy(t, k).wait_send()
        for k in range(6):
            gather_copy(t, k).wait_send()
        for k in range(1, RING):
            square_copy(t, k).wait_send()
            feed(t, k).wait_send()

        @pl.when(sec == 0)
        def _():
            for k in range(5):
                hand_over(t, k).wait_send()

        @pl.when(sec == 1)
        def _():
            feed(t, 0).wait_send()

        store_out(t).wait()
        return carry

    lax.fori_loop(0, chunks, drain, 0)


def run_blocks(tables, tokens, cot, params):
    (
        pre_gain,
        input_proj,
        gate_proj,
        state_proj,
        step_proj,
        step_bias,
        decay_log,
        skip_gain,
        norm_gain,
        out_proj,
    ) = params
    readers = lax.axis_size("dp")
    tok_rows, width = tokens.shape
    slots = 2 * tok_rows
    inner = input_proj.shape[1]
    heads = step_proj.shape[1]
    chunks = slots // ROWS
    part = width // (2 * RING)
    share = width // readers
    levels = readers // RING
    some = levels // 4
    vmem = pl.BlockSpec(memory_space=pltpu.VMEM)
    anywhere = pl.BlockSpec(memory_space=pl.ANY)
    half = ROWS // RING // 2
    dma = pltpu.SemaphoreType.DMA
    return pl.pallas_call(
        functools.partial(block_kernel, chunks, heads, levels),
        name="blocks",
        out_shape=(
            pltpu.VMEM((slots, width), BF16),
            pltpu.VMEM((share, inner), BF16),
        ),
        in_specs=[vmem] * 8 + [anywhere] * 6,
        out_specs=(vmem, vmem),
        scratch_shapes=[
            pltpu.VMEM((width, inner), BF16),
            pltpu.VMEM((width, inner), BF16),
            pltpu.VMEM((width, 2 * NSTATE), BF16),
            pltpu.VMEM((128, width), BF16),
            pltpu.VMEM((inner, width), BF16),
            pltpu.VMEM((3, 8, 128), F32),
            pltpu.VMEM((tok_rows, part), BF16),
            pltpu.VMEM((slots, part), BF16),
            pltpu.VMEM((slots, part), BF16),
            pltpu.VMEM((chunks, ROWS, part), BF16),
            pltpu.VMEM((slots, width), BF16),
            pltpu.VMEM((slots, width), BF16),
            pltpu.VMEM((chunks, ROWS, width), BF16),
            pltpu.VMEM((chunks, half, width), BF16),
            pltpu.VMEM((chunks, half, width), BF16),
            pltpu.VMEM((chunks, 2, half, width), BF16),
            pltpu.VMEM((chunks, 2, half, width), BF16),
            pltpu.VMEM((ROWS, width), BF16),
            pltpu.VMEM((ROWS, inner), BF16),
            pltpu.VMEM((ROWS, inner), F32),
            pltpu.VMEM((ROWS, 2 * NSTATE), BF16),
            pltpu.VMEM((ROWS, 128), F32),
            pltpu.VMEM((slots, inner), BF16),
            pltpu.VMEM((slots, inner), BF16),
            pltpu.VMEM((slots, 128), F32),
            pltpu.VMEM((NSTATE, inner), F32),
            pltpu.VMEM((8, 128), F32),
            pltpu.VMEM((slots, 128), F32),
            pltpu.VMEM((slots // SUB, 8, 128), F32),
            pltpu.VMEM((RING, chunks, ROWS // SUB, 8, 128), F32),
            pltpu.VMEM((8, inner), F32),
            pltpu.VMEM((slots, width), BF16),
            pltpu.VMEM((levels, RING * share, slots), BF16),
            pltpu.VMEM((levels, RING * share, inner), F32),
            pltpu.VMEM((levels, RING, share, inner), BF16),
            pltpu.VMEM((2, some, share, inner), BF16),
            pltpu.VMEM((2, some, share, inner), BF16),
            pltpu.VMEM((levels, share, inner), BF16),
            pltpu.VMEM((levels, share, inner), BF16),
            pltpu.VMEM((levels, share, inner), BF16),
            pltpu.VMEM((levels, share, inner), BF16),
            dma((6,)),
            dma((readers,)),
            dma((readers,)),
            dma((RING, chunks)),
            dma((chunks,)),
            dma((5, chunks)),
            dma((chunks,)),
            dma((6, chunks)),
            dma((6, chunks)),
            dma((6, chunks)),
            dma((6, chunks)),
            dma((3, chunks)),
            dma((3, chunks)),
            dma((6, 2)),
            dma((6, 2)),
            dma((levels,)),
            dma((levels,)),
        ],
        compiler_params=pltpu.CompilerParams(
            collective_id=1, has_side_effects=True, vmem_limit_bytes=60 * 1024 * 1024
        ),
    )(
        *tables,
        pre_gain[None],
        step_bias[None],
        decay_log[None],
        skip_gain[None],
        norm_gain[None],
        step_proj.T,
        tokens,
        input_proj,
        gate_proj,
        state_proj,
        out_proj,
        cot,
    )


def per_device(
    tokens,
    base_rows,
    baseline_owner,
    cotangent,
    *params,
):
    tables = (base_rows[None, :], baseline_owner[None, :])
    result, grad = run_blocks(
        tables, tokens, cotangent[0], tuple(item[0] for item in params)
    )
    return (result[None], grad.T[None])


def solution(mesh):
    return jax.shard_map(
        per_device,
        mesh=mesh,
        in_specs=(
            P("dp", None),
            P(),
            P(),
            P("section", "dp", None),
            P("section", None),
            P("section", None, "tensor"),
            P("section", None, "tensor"),
            P("section", None, None),
            P("section", None, "tensor"),
            P("section", "tensor"),
            P("section", "tensor"),
            P("section", "tensor"),
            P("section", "tensor"),
            P("section", "tensor", None),
        ),
        out_specs=(P("section", "dp", None), P("section", "tensor", "dp")),
        check_vma=False,
    )
```
